128 devices in a mesh: ctx: 8 (over y, core), tp: 16 (over z, x).
Axes of the slice: x: 4, y: 4, z: 4, core: 2. Of those that a mesh axis runs over, the one named last changes fastest.
Arguments:
- queries: bfloat16 [16384, 8192], P(('ctx', 'tp')), may hold values from -16 to 16
- key_tensor: bfloat16 [16384, 1024], P(('ctx', 'tp')), may hold values from -6 to 6
- value_tensor: bfloat16 [16384, 1024], P(('ctx', 'tp')), may hold values from -6 to 6
- output_gradient: bfloat16 [16384, 8192], P(('ctx', 'tp')), may hold values from -6 to 6
- key_blocks: int32 [128, 8], replicated, may hold values from 0 to 127, as said below
- slot_valid: int32 [128, 8], replicated, may hold values from 0 to 1, as said below
Outputs:
- d_q: bfloat16 [16384, 8192], P(('ctx', 'tp'))
- key_gradient: bfloat16 [16384, 1024], P(('ctx', 'tp'))
- value_gradient: bfloat16 [16384, 1024], P(('ctx', 'tp'))
The draws below stay inside these ranges and needn't reach their ends.
Inputs may be any that keep to these rules, and one draw needn't show every extreme that they name: `key_blocks`: row b names blocks b - 1, b, b + 1 (clamped to the sequence), block 0, then 8 - 4 blocks that differ from one another and from b - 1, b and b + 1. Row 0 is not read. `slot_valid`: the slot of block b itself is 1 in every row; a window slot naming a block below 1 or above 127 is 0, the block 0 slot is 1, and among the random slots a ragged leading part is 1 except where it names block 0.
All inputs are finite; a program needn't handle non-finite values.
Results may differ from the reference program's by a relative error of at most 0.006.
Values may be sent and summed in bfloat16 or wider, within the bound.
No kernel may reach another device: no remote copies, remote signals or barrier semaphores. Data moves between devices by JAX's collectives and lax.ppermute only.
A program may use at most 256 MiB of HBM per device.

```python
import math
import jax
import jax.numpy as jnp
from jax import lax

QUERY_HEADS = 64
KEY_HEADS = 8
HEAD_SIZE = 128
BLOCK_TOKENS = 128
NB = 8
GROUP_SIZE = 8
SEQUENCE_LENGTH = 16384
BLOCK_COUNT = 128


def pair_draw(key):
    group_index = QUERY_HEADS // KEY_HEADS
    random_seed_keys = jax.random.fold_in(key, 101)
    random_seed_query = jax.random.fold_in(key, 102)
    key_row_block = jnp.clip(jax.random.normal(random_seed_keys, (SEQUENCE_LENGTH, KEY_HEADS, HEAD_SIZE), jnp.float32), -5.0, 5.0)
    query_row_block = jnp.clip(jax.random.normal(random_seed_query, (SEQUENCE_LENGTH, KEY_HEADS, group_index, HEAD_SIZE), jnp.float32), -5.0, 5.0)
    return (query_row_block.reshape(SEQUENCE_LENGTH, QUERY_HEADS * HEAD_SIZE), key_row_block.reshape(SEQUENCE_LENGTH, KEY_HEADS * HEAD_SIZE))


def one_offsets(seed_row):
    return jax.random.permutation(seed_row, BLOCK_COUNT - 3)[:NB - 4]


def list_draw(key):
    extra = NB - 4
    blocks_seq = jnp.arange(BLOCK_COUNT, dtype=jnp.int32)
    seeds_rows = jax.random.split(jax.random.fold_in(key, 201), BLOCK_COUNT)
    offsets = jax.vmap(one_offsets)(seeds_rows) + 2
    random_ids = (blocks_seq[:, None] + offsets) % BLOCK_COUNT
    counts_rows = jax.random.randint(jax.random.fold_in(key, 202), (BLOCK_COUNT, 1), 1, extra + 1)
    random_live = (jnp.arange(extra)[None, :] < counts_rows) & (random_ids != 0)
    window_ids = jnp.stack([blocks_seq - 1, blocks_seq, blocks_seq + 1], axis=1)
    window_live = jnp.stack([blocks_seq - 1 >= 1, blocks_seq >= 0, blocks_seq + 1 <= BLOCK_COUNT - 1], axis=1)
    listed = jnp.concatenate([jnp.clip(window_ids, 0, BLOCK_COUNT - 1), jnp.zeros((BLOCK_COUNT, 1), jnp.int32), random_ids.astype(jnp.int32)], axis=1)
    live_all = jnp.concatenate([window_live, (blocks_seq >= 0)[:, None], random_live], axis=1)
    return (listed.astype(jnp.int32), live_all.astype(jnp.int32))


def draw_queries(key, part):
    return pair_draw(key)[0].astype(jnp.bfloat16)


def draw_key_tensor(key, part):
    return pair_draw(key)[1].astype(jnp.bfloat16)


def draw_key_blocks(key, part):
    return list_draw(key)[0]


def draw_slot_valid(key, part):
    return list_draw(key)[1]


def levels(own_key, dims, shards, least, largest):
    def one(position, blocks):
        heights = jax.random.uniform(jax.random.fold_in(jax.random.fold_in(own_key, 6), position), (blocks,), jnp.float32, least / len(shards), largest / len(shards))
        return jnp.repeat(jnp.exp(heights), dims[position] // blocks).reshape((-1,) + (1,) * (len(dims) - position - 1))

    factor_of = one(*shards[0])
    for cut in shards[1:]:
        factor_of = factor_of * one(*cut)
    return factor_of


def normal_values(rng, extent, scale, reach, pieces=(), held_as=jnp.bfloat16):
    result = jax.random.normal(rng, extent, jnp.float32) * scale
    if len(pieces) > 0:
        result = levels(rng, extent, pieces, -0.22, 0.18) * result
    return jnp.clip(result, min=-reach, max=reach).astype(held_as)


def setup_inputs(seed: int = 0) -> dict:
    key_list = jax.random.split(jax.random.key(seed), 7)
    queries = draw_queries(jax.random.fold_in(key_list[6], 71), 0)
    key_tensor = draw_key_tensor(jax.random.fold_in(key_list[6], 71), 0)
    value_tensor = normal_values(key_list[2], (SEQUENCE_LENGTH, KEY_HEADS * HEAD_SIZE), 1.0, 6.0, ((0, 128),))
    output_gradient = normal_values(key_list[3], (SEQUENCE_LENGTH, QUERY_HEADS * HEAD_SIZE), 1.0, 6.0, ((0, 128),))
    key_blocks = draw_key_blocks(jax.random.fold_in(key_list[6], 71), 0)
    slot_valid = draw_slot_valid(jax.random.fold_in(key_list[6], 71), 0)
    return {"queries": queries, "key_tensor": key_tensor, "value_tensor": value_tensor, "output_gradient": output_gradient, "key_blocks": key_blocks, "slot_valid": slot_valid}


def block_grads(q_block, o_block, key_row_block, value_rows, live_mask):
    scaling = 1.0 / math.sqrt(HEAD_SIZE)
    scores = jnp.einsum('qgd,kd->gqk', q_block, key_row_block) * scaling
    scores = jnp.where(live_mask[None, None, :], scores, -jnp.inf)
    row_max = lax.optimization_barrier(jnp.max(scores, axis=-1, keepdims=True))
    raised = jnp.exp(scores - row_max)
    weights = raised / lax.optimization_barrier(jnp.sum(raised, axis=-1, keepdims=True))
    prob_grad = jnp.einsum('qgd,kd->gqk', o_block, value_rows)
    row_dot = lax.optimization_barrier(jnp.sum(weights * prob_grad, axis=-1, keepdims=True))
    score_grad = lax.optimization_barrier((weights * (prob_grad - row_dot)).astype(jnp.bfloat16)).astype(jnp.float32)
    rounded_weights = lax.optimization_barrier(weights.astype(jnp.bfloat16)).astype(jnp.float32)
    value_grad = jnp.einsum('gqk,qgd->kd', rounded_weights, o_block)
    key_grad = jnp.einsum('gqk,qgd->kd', score_grad, q_block) * scaling
    query_grad = jnp.einsum('gqk,kd->qgd', score_grad, key_row_block) * scaling
    return (query_grad, key_grad, value_grad)

def reference(queries, key_tensor, value_tensor, output_gradient, key_blocks, slot_valid):
    query_everything = queries.astype(jnp.float32).reshape(BLOCK_COUNT, BLOCK_TOKENS, KEY_HEADS, GROUP_SIZE, HEAD_SIZE)
    output_gradients = output_gradient.astype(jnp.float32).reshape(BLOCK_COUNT, BLOCK_TOKENS, KEY_HEADS, GROUP_SIZE, HEAD_SIZE)
    keep_rows = (jnp.arange(BLOCK_COUNT) != 0).astype(jnp.float32)
    masked_grads = output_gradients * keep_rows[:, None, None, None, None]
    key_everything = key_tensor.astype(jnp.float32).reshape(BLOCK_COUNT, BLOCK_TOKENS, KEY_HEADS, HEAD_SIZE)
    value_everything = value_tensor.astype(jnp.float32).reshape(BLOCK_COUNT, BLOCK_TOKENS, KEY_HEADS, HEAD_SIZE)
    live_rows = jnp.broadcast_to((slot_valid > 0)[:, :, None], (BLOCK_COUNT, NB, BLOCK_TOKENS)).reshape(BLOCK_COUNT, NB * BLOCK_TOKENS)
    every_key = jnp.ones((SEQUENCE_LENGTH,), jnp.int32) > 0
    query_list = []
    key_sequence = []
    value_sequence = []
    for head_index in range(KEY_HEADS):
        key_head = key_everything[:, :, head_index]
        value_head = value_everything[:, :, head_index]

        def sparse_row(packed):
            q_block, o_block, blocks, live_mask = packed
            key_row_block = key_head[blocks].reshape(NB * BLOCK_TOKENS, HEAD_SIZE)
            value_rows = value_head[blocks].reshape(NB * BLOCK_TOKENS, HEAD_SIZE)
            return block_grads(q_block, o_block, key_row_block, value_rows, live_mask)
        dq_sparse, dk_slots, dv_slots = lax.map(sparse_row, (query_everything[:, :, head_index], masked_grads[:, :, head_index], key_blocks, live_rows))
        dk_head = jnp.zeros((BLOCK_COUNT, BLOCK_TOKENS, HEAD_SIZE), jnp.float32).at[key_blocks].add(dk_slots.reshape(BLOCK_COUNT, NB, BLOCK_TOKENS, HEAD_SIZE))
        dv_head = jnp.zeros((BLOCK_COUNT, BLOCK_TOKENS, HEAD_SIZE), jnp.float32).at[key_blocks].add(dv_slots.reshape(BLOCK_COUNT, NB, BLOCK_TOKENS, HEAD_SIZE))
        dq_first, dk_first, dv_first = block_grads(query_everything[0, :, head_index], output_gradients[0, :, head_index], key_head.reshape(SEQUENCE_LENGTH, HEAD_SIZE), value_head.reshape(SEQUENCE_LENGTH, HEAD_SIZE), every_key)
        query_list.append(dq_sparse.at[0].add(dq_first))
        key_sequence.append(dk_head + dk_first.reshape(BLOCK_COUNT, BLOCK_TOKENS, HEAD_SIZE))
        value_sequence.append(dv_head + dv_first.reshape(BLOCK_COUNT, BLOCK_TOKENS, HEAD_SIZE))
    d_q = jnp.stack(query_list, axis=2).reshape(SEQUENCE_LENGTH, QUERY_HEADS * HEAD_SIZE).astype(jnp.bfloat16)
    key_gradient = jnp.stack(key_sequence, axis=2).reshape(SEQUENCE_LENGTH, KEY_HEADS * HEAD_SIZE).astype(jnp.bfloat16)
    value_gradient = jnp.stack(value_sequence, axis=2).reshape(SEQUENCE_LENGTH, KEY_HEADS * HEAD_SIZE).astype(jnp.bfloat16)
    return (d_q, key_gradient, value_gradient)
```

```python
import functools
import math

import jax
import jax.numpy as jnp
from jax import lax
from jax.experimental import pallas as pl
from jax.experimental.pallas import tpu as pltpu
from jax.sharding import PartitionSpec as P

KEY_HEADS = 8
GROUP_SIZE = 8
HEAD_SIZE = 128
BLOCK = 128
NB = 8
GROUPS = 16
PIECE = 8
SENT = 5
FIRST_SENT = NB - SENT
BOTH = ("ctx", "tp")
SCALING = 1.0 / math.sqrt(HEAD_SIZE)
EXP_SCALE = SCALING * math.log2(math.e)
FAR = 1e30
F32 = jnp.float32
BF16 = jnp.bfloat16
VM = pltpu.VMEM


def dot(a, b, ca, cb):
    return lax.dot_general(a, b, (((ca,), (cb,)), ((), ())), preferred_element_type=F32)


def pack_body(k_ref, v_ref, out_ref):
    for h in range(KEY_HEADS):
        cols = pl.ds(h * HEAD_SIZE, HEAD_SIZE)
        out_ref[h, :, 0] = k_ref[:, cols].reshape(GROUPS, PIECE, HEAD_SIZE)
        out_ref[h, :, 1] = v_ref[:, cols].reshape(GROUPS, PIECE, HEAD_SIZE)


def pack_pieces(k, v):
    return pl.pallas_call(
        pack_body,
        out_shape=jax.ShapeDtypeStruct((KEY_HEADS, GROUPS, 2, PIECE, HEAD_SIZE), BF16),
        in_specs=[pl.BlockSpec(memory_space=VM)] * 2,
        out_specs=pl.BlockSpec(memory_space=VM),
        name="pack_pieces",
    )(k, v)


def gather_body(table_ref, held_ref, out_ref, *, rows):
    base = pl.program_id(0) * rows

    def one(d, carry):
        for s in range(SENT):
            block = table_ref[(base + d) * NB + FIRST_SENT + s]
            out_ref[d, s] = held_ref[block]
        return carry

    lax.fori_loop(0, rows, one, 0, unroll=4)


def gather_pieces(table, held, blocks):
    steps = 4
    rows = blocks // steps
    return pl.pallas_call(
        functools.partial(gather_body, rows=rows),
        out_shape=jax.ShapeDtypeStruct((blocks, SENT, 2, PIECE, HEAD_SIZE), BF16),
        grid_spec=pltpu.PrefetchScalarGridSpec(
            num_scalar_prefetch=1,
            grid=(steps,),
            in_specs=[pl.BlockSpec((blocks, 2, PIECE, HEAD_SIZE), lambda i, t: (0, 0, 0, 0))],
            out_specs=pl.BlockSpec(
                (rows, SENT, 2, PIECE, HEAD_SIZE), lambda i, t: (i, 0, 0, 0, 0)
            ),
        ),
        name="gather_pieces",
    )(table, held)


def scatter_body(table_ref, got_ref, dense_ref, out_ref, acc_ref, *, rows, blocks):
    step = pl.program_id(0)
    base = step * rows

    @pl.when(step == 0)
    def _():
        for kv in range(2):
            acc_ref[:, kv] = dense_ref[kv].reshape(blocks, PIECE, HEAD_SIZE)

    def one(d, carry):
        for s in range(SENT):
            block = table_ref[(base + d) * NB + FIRST_SENT + s]
            acc_ref[block] += got_ref[d, s].astype(F32)
        return carry

    lax.fori_loop(0, rows, one, 0, unroll=4)

    @pl.when(step == pl.num_programs(0) - 1)
    def _():
        out_ref[...] = acc_ref[...].astype(BF16)


def scatter_pieces(table, got, dense, blocks):
    steps = 4
    rows = blocks // steps
    return pl.pallas_call(
        functools.partial(scatter_body, rows=rows, blocks=blocks),
        out_shape=jax.ShapeDtypeStruct((blocks, 2, PIECE, HEAD_SIZE), BF16),
        grid_spec=pltpu.PrefetchScalarGridSpec(
            num_scalar_prefetch=1,
            grid=(steps,),
            in_specs=[
                pl.BlockSpec((rows, SENT, 2, PIECE, HEAD_SIZE), lambda i, t: (i, 0, 0, 0, 0)),
                pl.BlockSpec((2, blocks * PIECE, HEAD_SIZE), lambda i, t: (0, 0, 0)),
            ],
            out_specs=pl.BlockSpec((blocks, 2, PIECE, HEAD_SIZE), lambda i, t: (0, 0, 0, 0)),
            scratch_shapes=[VM((blocks, 2, PIECE, HEAD_SIZE), F32)],
        ),
        name="scatter_pieces",
    )(table, got, dense)


def two_heads(ref, p):
    first = ref[:, pl.ds(2 * p * HEAD_SIZE, HEAD_SIZE)]
    second = ref[:, pl.ds((2 * p + 1) * HEAD_SIZE, HEAD_SIZE)]
    return jnp.concatenate([first, second], axis=0)


def col_sum(x):
    return jnp.sum(x, axis=0, keepdims=True)


def sparse_body(
    meta_ref, valid_ref, q_ref, o_ref, k_ref, v_ref, kp_ref, vp_ref, kn_ref, vn_ref, g_ref,
    dq_ref, own_ref, prev_ref, next_ref, sent_ref,
    kc, vc, kt, st, dp, pb, ds, dk, dv,
):
    b = meta_ref[0]

    @pl.when(b == 0)
    def _():
        dq_ref[...] = jnp.zeros_like(dq_ref)
        own_ref[...] = jnp.zeros_like(own_ref)
        prev_ref[...] = jnp.zeros_like(prev_ref)
        next_ref[...] = jnp.zeros_like(next_ref)
        sent_ref[...] = jnp.zeros_like(sent_ref)

    @pl.when(b != 0)
    def _():
        for dst, parts, kv in ((kc, (kp_ref, k_ref, kn_ref), 0), (vc, (vp_ref, v_ref, vn_ref), 1)):
            for s, part in enumerate(parts):
                dst[s * BLOCK : (s + 1) * BLOCK] = part[...]
            for s in range(SENT):
                at = (FIRST_SENT + s) * BLOCK
                dst[at : at + BLOCK] = g_ref[0, :, s, kv].reshape(BLOCK, HEAD_SIZE)
        kt[...] = kc[...].T
        live = [valid_ref[b * NB + s] > 0 for s in range(NB)]
        for p in range(GROUP_SIZE // 2):
            w = p % 2
            qp = two_heads(q_ref, p)
            op = two_heads(o_ref, p)
            st[w] = dot(kc[...], qp, 1, 1)
            dp[w] = dot(vc[...], op, 1, 1)
            top = jnp.full((1, 2 * BLOCK), -FAR, F32)
            for s in range(NB):
                here = jnp.max(st[w, s * BLOCK : (s + 1) * BLOCK], axis=0, keepdims=True)
                top = jnp.maximum(top, jnp.where(live[s], here, -FAR))
            top = top * EXP_SCALE
            total = jnp.zeros((1, 2 * BLOCK), F32)
            cross = jnp.zeros((1, 2 * BLOCK), F32)
            for s in range(NB):
                rows = slice(s * BLOCK, (s + 1) * BLOCK)
                shift = jnp.where(live[s], top, FAR)
                raised = jnp.exp2(st[w, rows] * EXP_SCALE - shift)
                st[w, rows] = raised
                total = total + col_sum(raised)
                cross = cross + col_sum(raised * dp[w, rows])
            inverse = 1.0 / total
            delta = cross * inverse
            for s in range(NB):
                rows = slice(s * BLOCK, (s + 1) * BLOCK)
                weights = st[w, rows] * inverse
                pb[w, rows] = weights.astype(BF16)
                ds[w, rows] = (weights * (dp[w, rows] - delta)).astype(BF16)
            new_dv = dot(pb[w], op, 1, 0)
            new_dk = dot(ds[w], qp, 1, 0)
            dv[...] = new_dv if p == 0 else dv[...] + new_dv
            dk[...] = new_dk if p == 0 else dk[...] + new_dk
            dqt = dot(kt[...], ds[w], 1, 0) * SCALING
            for j in range(2):
                dq_ref[:, pl.ds((2 * p + j) * HEAD_SIZE, HEAD_SIZE)] = (
                    dqt[:, j * BLOCK : (j + 1) * BLOCK].T.astype(BF16)
                )
        for kv, acc, factor in ((0, dk, SCALING), (1, dv, 1.0)):
            prev_ref[kv] = (acc[0:BLOCK] * factor).astype(BF16)
            own_ref[kv] = acc[BLOCK : 2 * BLOCK] * factor
            next_ref[kv] = (acc[2 * BLOCK : 3 * BLOCK] * factor).astype(BF16)
            for s in range(SENT):
                at = (FIRST_SENT + s) * BLOCK
                sent_ref[0, :, s, kv] = (
                    (acc[at : at + BLOCK] * factor).astype(BF16).reshape(GROUPS, PIECE, HEAD_SIZE)
                )


def sparse_grads(meta, valid, q, o, k, v, kp, vp, kn, vn, got):
    wide = pl.BlockSpec((BLOCK, GROUP_SIZE * HEAD_SIZE), lambda h, m, t: (0, h))
    narrow = pl.BlockSpec((BLOCK, HEAD_SIZE), lambda h, m, t: (0, h))
    pair = pl.BlockSpec((2, BLOCK, HEAD_SIZE), lambda h, m, t: (0, 0, h))
    pieces = pl.BlockSpec(
        (1, GROUPS, SENT, 2, PIECE, HEAD_SIZE), lambda h, m, t: (h, 0, 0, 0, 0, 0)
    )
    keys = NB * BLOCK
    width = KEY_HEADS * HEAD_SIZE
    return pl.pallas_call(
        sparse_body,
        out_shape=(
            jax.ShapeDtypeStruct(q.shape, BF16),
            jax.ShapeDtypeStruct((2, BLOCK, width), F32),
            jax.ShapeDtypeStruct((2, BLOCK, width), BF16),
            jax.ShapeDtypeStruct((2, BLOCK, width), BF16),
            jax.ShapeDtypeStruct((KEY_HEADS, GROUPS, SENT, 2, PIECE, HEAD_SIZE), BF16),
        ),
        grid_spec=pltpu.PrefetchScalarGridSpec(
            num_scalar_prefetch=2,
            grid=(KEY_HEADS,),
            in_specs=[wide, wide] + [narrow] * 6 + [pieces],
            out_specs=[wide, pair, pair, pair, pieces],
            scratch_shapes=[
                VM((keys, HEAD_SIZE), BF16),
                VM((keys, HEAD_SIZE), BF16),
                VM((HEAD_SIZE, keys), BF16),
                VM((2, keys, 2 * BLOCK), F32),
                VM((2, keys, 2 * BLOCK), F32),
                VM((2, keys, 2 * BLOCK), BF16),
                VM((2, keys, 2 * BLOCK), BF16),
                VM((keys, HEAD_SIZE), F32),
                VM((keys, HEAD_SIZE), F32),
            ],
        ),
        name="sparse_grads",
    )(meta, valid, q, o, k, v, kp, vp, kn, vn, got)


def stats_body(q_ref, held_ref, out_ref, kc, vc):
    keys = kc.shape[0]
    kc[...] = held_ref[:, 0].reshape(keys, HEAD_SIZE)
    vc[...] = held_ref[:, 1].reshape(keys, HEAD_SIZE)
    for p in range(GROUP_SIZE // 2):
        cols = pl.ds(2 * p * BLOCK, 2 * BLOCK)
        scores = dot(kc[...], two_heads(q_ref.at[0], p), 1, 1)
        grads = dot(vc[...], two_heads(q_ref.at[1], p), 1, 1)
        top = jnp.max(scores, axis=0, keepdims=True) * EXP_SCALE
        raised = jnp.exp2(scores * EXP_SCALE - top)
        out_ref[0:1, cols] = top
        out_ref[1:2, cols] = col_sum(raised)
        out_ref[2:3, cols] = col_sum(raised * grads)
        out_ref[3:8, cols] = jnp.zeros((5, 2 * BLOCK), F32)


def dense_stats(qo, held):
    keys = held.shape[0] * PIECE
    return pl.pallas_call(
        stats_body,
        out_shape=jax.ShapeDtypeStruct((8, GROUP_SIZE * BLOCK), F32),
        in_specs=[pl.BlockSpec(memory_space=VM)] * 2,
        out_specs=pl.BlockSpec(memory_space=VM),
        scratch_shapes=[VM((keys, HEAD_SIZE), BF16), VM((keys, HEAD_SIZE), BF16)],
        name="dense_stats",
    )(qo, held)


def dense_body(q_ref, held_ref, stats_ref, dkv_ref, dq_ref, kc, vc, kt):
    keys = kc.shape[0]
    kc[...] = held_ref[:, 0].reshape(keys, HEAD_SIZE)
    vc[...] = held_ref[:, 1].reshape(keys, HEAD_SIZE)
    kt[...] = kc[...].T
    for p in range(GROUP_SIZE // 2):
        cols = pl.ds(2 * p * BLOCK, 2 * BLOCK)
        tops = stats_ref[:, 0, cols]
        top = jnp.max(tops, axis=0, keepdims=True)
        factors = jnp.exp2(tops - top)
        inverse = 1.0 / col_sum(stats_ref[:, 1, cols] * factors)
        delta = col_sum(stats_ref[:, 2, cols] * factors) * inverse
        qp = two_heads(q_ref.at[0], p)
        op = two_heads(q_ref.at[1], p)
        scores = dot(kc[...], qp, 1, 1)
        grads = dot(vc[...], op, 1, 1)
        weights = jnp.exp2(scores * EXP_SCALE - top) * inverse
        rounded = weights.astype(BF16)
        score_grad = (weights * (grads - delta)).astype(BF16)
        new_dk = dot(score_grad, qp, 1, 0) * SCALING
        new_dv = dot(rounded, op, 1, 0)
        dkv_ref[0] = new_dk if p == 0 else dkv_ref[0] + new_dk
        dkv_ref[1] = new_dv if p == 0 else dkv_ref[1] + new_dv
        dqt = dot(kt[...], score_grad, 1, 0) * SCALING
        for j in range(2):
            dq_ref[:, pl.ds((2 * p + j) * HEAD_SIZE, HEAD_SIZE)] = dqt[
                :, j * BLOCK : (j + 1) * BLOCK
            ].T


def dense_grads(qo, held, stats):
    keys = held.shape[0] * PIECE
    return pl.pallas_call(
        dense_body,
        out_shape=(
            jax.ShapeDtypeStruct((2, keys, HEAD_SIZE), F32),
            jax.ShapeDtypeStruct((BLOCK, GROUP_SIZE * HEAD_SIZE), F32),
        ),
        in_specs=[pl.BlockSpec(memory_space=VM)] * 3,
        out_specs=[pl.BlockSpec(memory_space=VM)] * 2,
        scratch_shapes=[
            VM((keys, HEAD_SIZE), BF16),
            VM((keys, HEAD_SIZE), BF16),
            VM((HEAD_SIZE, keys), BF16),
        ],
        name="dense_grads",
    )(qo, held, stats)


def combine_body(own_ref, prev_ref, next_ref, got_ref, dk_ref, dv_ref):
    for kv, out in ((0, dk_ref), (1, dv_ref)):
        for h in range(KEY_HEADS):
            cols = pl.ds(h * HEAD_SIZE, HEAD_SIZE)
            total = own_ref[kv, :, cols] + prev_ref[kv, :, cols].astype(F32)
            total = total + next_ref[kv, :, cols].astype(F32)
            total = total + got_ref[h, :, kv].reshape(BLOCK, HEAD_SIZE).astype(F32)
            out[:, cols] = total.astype(BF16)


def combine(own, from_prev, from_next, got):
    width = KEY_HEADS * HEAD_SIZE
    return pl.pallas_call(
        combine_body,
        out_shape=(jax.ShapeDtypeStruct((BLOCK, width), BF16),) * 2,
        in_specs=[pl.BlockSpec(memory_space=VM)] * 4,
        out_specs=[pl.BlockSpec(memory_space=VM)] * 2,
        name="combine",
    )(own, from_prev, from_next, got)


def spread_body(meta_ref, q_ref, o_ref, *rest):
    outs, sems = rest[:-1], rest[-1]

    @pl.when(meta_ref[0] == 0)
    def _():
        copies = []
        for h, out in enumerate(outs):
            cols = pl.ds(h * GROUP_SIZE * HEAD_SIZE, GROUP_SIZE * HEAD_SIZE)
            for j, ref in enumerate((q_ref, o_ref)):
                copies.append(pltpu.make_async_copy(ref.at[:, cols], out.at[j], sems.at[h, j]))
        for copy in copies:
            copy.start()
        for copy in copies:
            copy.wait()


def spread_heads(meta, q, o):
    hbm = pl.BlockSpec(memory_space=pl.ANY)
    return pl.pallas_call(
        spread_body,
        out_shape=(jax.ShapeDtypeStruct((2, BLOCK, GROUP_SIZE * HEAD_SIZE), BF16),) * KEY_HEADS,
        in_specs=[pl.BlockSpec(memory_space=pltpu.SMEM), hbm, hbm],
        out_specs=[hbm] * KEY_HEADS,
        scratch_shapes=[pltpu.SemaphoreType.DMA((KEY_HEADS, 2))],
        name="spread_heads",
    )(meta, q, o)


def first_body(meta_ref, dq_ref, *rest):
    parts, out, sems = rest[:KEY_HEADS], rest[KEY_HEADS], rest[KEY_HEADS + 1]

    @pl.when(meta_ref[0] == 0)
    def _():
        copies = []
        for h, part in enumerate(parts):
            cols = pl.ds(h * GROUP_SIZE * HEAD_SIZE, GROUP_SIZE * HEAD_SIZE)
            copies.append(pltpu.make_async_copy(part, out.at[:, cols], sems.at[h]))
        for copy in copies:
            copy.start()
        for copy in copies:
            copy.wait()


def put_first(meta, dq, parts):
    hbm = pl.BlockSpec(memory_space=pl.ANY)
    return pl.pallas_call(
        first_body,
        out_shape=jax.ShapeDtypeStruct(dq.shape, dq.dtype),
        in_specs=[pl.BlockSpec(memory_space=pltpu.SMEM)] + [hbm] * (KEY_HEADS + 1),
        out_specs=hbm,
        input_output_aliases={1: 0},
        scratch_shapes=[pltpu.SemaphoreType.DMA((KEY_HEADS,))],
        name="put_first",
    )(meta, dq, *parts)


def per_device(queries, key_tensor, value_tensor, output_gradient, key_blocks, slot_valid):
    tp_size = lax.axis_size("tp")
    blocks = lax.axis_size("ctx") * tp_size
    c_index = lax.axis_index("ctx")
    t_index = lax.axis_index("tp")
    b_index = c_index * tp_size + t_index
    meta = b_index.astype(jnp.int32).reshape(1)
    table = key_blocks.reshape(-1)
    valid = slot_valid.reshape(-1)
    up = [(i, (i + 1) % blocks) for i in range(blocks)]
    down = [(i, (i - 1) % blocks) for i in range(blocks)]

    def swap(x):
        return lax.all_to_all(x, BOTH, split_axis=0, concat_axis=0, tiled=True)

    pieces = pack_pieces(key_tensor, value_tensor)
    held = swap(pieces.reshape(blocks, 2, PIECE, HEAD_SIZE))
    kp, vp = lax.ppermute(key_tensor, BOTH, up), lax.ppermute(value_tensor, BOTH, up)
    kn, vn = lax.ppermute(key_tensor, BOTH, down), lax.ppermute(value_tensor, BOTH, down)
    listed = gather_pieces(table, held, blocks)
    got = swap(listed).reshape(KEY_HEADS, GROUPS, SENT, 2, PIECE, HEAD_SIZE)

    slices = spread_heads(meta, queries, output_gradient)
    qo = jnp.where(b_index == 0, slices[0], jnp.zeros_like(slices[0]))
    for h in range(1, KEY_HEADS):
        qo = qo + lax.ppermute(slices[h], BOTH, [(0, h * tp_size)])
    qo = lax.psum(qo, "tp")

    dq, own, to_prev, to_next, sent = sparse_grads(
        meta, valid, queries, output_gradient, key_tensor, value_tensor, kp, vp, kn, vn, got
    )
    back = swap(sent.reshape(blocks, SENT, 2, PIECE, HEAD_SIZE))
    from_next = lax.ppermute(to_prev, BOTH, down)
    from_prev = lax.ppermute(to_next, BOTH, up)

    stats = dense_stats(qo, held)
    stats = lax.all_gather(stats, "tp", axis=0)
    dense, dq_part = dense_grads(qo, held, stats)
    dq_first = lax.psum(dq_part, "tp").astype(BF16)
    parts = [dq_first] + [
        lax.ppermute(dq_first, BOTH, [(h * tp_size, 0)]) for h in range(1, KEY_HEADS)
    ]
    d_q = put_first(meta, dq, parts)

    summed = scatter_pieces(table, back, dense, blocks)
    home = swap(summed).reshape(KEY_HEADS, GROUPS, 2, PIECE, HEAD_SIZE)
    d_k, d_v = combine(own, from_prev, from_next, home)
    return d_q, d_k, d_v


def solution(mesh):
    spec = P(BOTH, None)
    return jax.shard_map(
        per_device,
        mesh=mesh,
        in_specs=(spec, spec, spec, spec, P(), P()),
        out_specs=(spec, spec, spec),
        check_vma=False,
    )
```

```python
import functools
import math

import jax
import jax.numpy as jnp
from jax import lax
from jax.experimental import pallas as pl
from jax.experimental.pallas import tpu as pltpu
from jax.sharding import PartitionSpec as P

KEY_HEADS = 8
GROUP_SIZE = 8
HEAD_SIZE = 128
BLOCK = 128
NB = 8
GROUPS = 16
PIECE = 8
SENT = 5
FIRST_SENT = NB - SENT
CHUNKS = 2
HALF = KEY_HEADS // CHUNKS
BOTH = ("ctx", "tp")
SCALING = 1.0 / math.sqrt(HEAD_SIZE)
EXP_SCALE = SCALING * math.log2(math.e)
FAR = 1e30
F32 = jnp.float32
BF16 = jnp.bfloat16
VM = pltpu.VMEM


def dot(a, b, ca, cb):
    return lax.dot_general(a, b, (((ca,), (cb,)), ((), ())), preferred_element_type=F32)


def pack_body(k_ref, v_ref, out_ref, both_ref):
    for kv, ref in enumerate((k_ref, v_ref)):
        both_ref[kv] = ref[...]
        for j in range(CHUNKS):
            for y in range(HALF):
                cols = pl.ds((j * HALF + y) * HEAD_SIZE, HEAD_SIZE)
                out_ref[y, kv, :, j] = ref[:, cols].reshape(GROUPS, PIECE, HEAD_SIZE)


def pack_pieces(k, v):
    return pl.pallas_call(
        pack_body,
        out_shape=(
            jax.ShapeDtypeStruct((HALF, 2, GROUPS, CHUNKS, PIECE, HEAD_SIZE), BF16),
            jax.ShapeDtypeStruct((2,) + k.shape, BF16),
        ),
        in_specs=[pl.BlockSpec(memory_space=VM)] * 2,
        out_specs=[pl.BlockSpec(memory_space=VM)] * 2,
        name="pack_pieces",
    )(k, v)


def gather_body(table_ref, held_ref, out_ref, *, rows, chunk):
    base = pl.program_id(0) * rows

    def one(d, carry):
        for s in range(SENT):
            block = table_ref[(base + d) * NB + FIRST_SENT + s]
            out_ref[d, s] = held_ref[block, chunk]
        return carry

    lax.fori_loop(0, rows, one, 0, unroll=4)


def gather_pieces(table, held, blocks, chunk):
    steps = 4
    rows = blocks // steps
    return pl.pallas_call(
        functools.partial(gather_body, rows=rows, chunk=chunk),
        out_shape=jax.ShapeDtypeStruct((blocks, SENT, PIECE, HEAD_SIZE), BF16),
        grid_spec=pltpu.PrefetchScalarGridSpec(
            num_scalar_prefetch=1,
            grid=(steps,),
            in_specs=[
                pl.BlockSpec((blocks, CHUNKS, PIECE, HEAD_SIZE), lambda i, t: (0, 0, 0, 0))
            ],
            out_specs=pl.BlockSpec((rows, SENT, PIECE, HEAD_SIZE), lambda i, t: (i, 0, 0, 0)),
        ),
        name="gather_pieces",
    )(table, held)


def give_body(meta_ref, held_ref, out_ref):
    out_ref[...] = held_ref[:, 1 - meta_ref[1]]


def give_pieces(meta, held):
    return pl.pallas_call(
        give_body,
        out_shape=jax.ShapeDtypeStruct(held.shape[:1] + held.shape[2:], BF16),
        in_specs=[pl.BlockSpec(memory_space=pltpu.SMEM), pl.BlockSpec(memory_space=VM)],
        out_specs=pl.BlockSpec(memory_space=VM),
        name="give_pieces",
    )(meta, held)


def add_listed(table_ref, got_ref, acc_ref, rows):
    base = pl.program_id(0) * rows

    def one(d, carry):
        for s in range(SENT):
            block = table_ref[(base + d) * NB + FIRST_SENT + s]
            acc_ref[block] += got_ref[d, s].astype(F32)
        return carry

    lax.fori_loop(0, rows, one, 0, unroll=4)


def scatter_body(table_ref, got_ref, out_ref, *, rows):
    @pl.when(pl.program_id(0) == 0)
    def _():
        out_ref[...] = jnp.zeros_like(out_ref)

    add_listed(table_ref, got_ref, out_ref, rows)


def scatter_last_body(
    table_ref, meta_ref, got_ref, first_ref, dense_ref, other_ref, out_ref, acc_ref, *, rows
):
    @pl.when(pl.program_id(0) == 0)
    def _():
        acc_ref[...] = jnp.zeros_like(acc_ref)

    add_listed(table_ref, got_ref, acc_ref, rows)

    @pl.when(pl.program_id(0) == pl.num_programs(0) - 1)
    def _():
        core = meta_ref[1]
        mine = dense_ref[0].reshape(acc_ref.shape)
        other = other_ref[...].reshape(acc_ref.shape)
        out_ref[:, core] = (jnp.where(core == 0, first_ref[...], acc_ref[...]) + mine).astype(BF16)
        out_ref[:, 1 - core] = (
            jnp.where(core == 0, acc_ref[...], first_ref[...]) + other
        ).astype(BF16)


def scatter_pieces(table, got, blocks):
    steps = 4
    rows = blocks // steps
    return pl.pallas_call(
        functools.partial(scatter_body, rows=rows),
        out_shape=jax.ShapeDtypeStruct((blocks, PIECE, HEAD_SIZE), F32),
        grid_spec=pltpu.PrefetchScalarGridSpec(
            num_scalar_prefetch=1,
            grid=(steps,),
            in_specs=[pl.BlockSpec((rows, SENT, PIECE, HEAD_SIZE), lambda i, t: (i, 0, 0, 0))],
            out_specs=pl.BlockSpec((blocks, PIECE, HEAD_SIZE), lambda i, t: (0, 0, 0)),
        ),
        name="scatter_pieces",
    )(table, got)


def scatter_last(table, meta, got, first, dense, other, blocks):
    steps = 4
    rows = blocks // steps
    whole = pl.BlockSpec((blocks, PIECE, HEAD_SIZE), lambda i, t, m: (0, 0, 0))
    return pl.pallas_call(
        functools.partial(scatter_last_body, rows=rows),
        out_shape=jax.ShapeDtypeStruct((blocks, CHUNKS, PIECE, HEAD_SIZE), BF16),
        grid_spec=pltpu.PrefetchScalarGridSpec(
            num_scalar_prefetch=2,
            grid=(steps,),
            in_specs=[
                pl.BlockSpec((rows, SENT, PIECE, HEAD_SIZE), lambda i, t, m: (i, 0, 0, 0)),
                whole,
                pl.BlockSpec((1, blocks * PIECE, HEAD_SIZE), lambda i, t, m: (0, 0, 0)),
                pl.BlockSpec((blocks * PIECE, HEAD_SIZE), lambda i, t, m: (0, 0)),
            ],
            out_specs=pl.BlockSpec(
                (blocks, CHUNKS, PIECE, HEAD_SIZE), lambda i, t, m: (0, 0, 0, 0)
            ),
            scratch_shapes=[VM((blocks, PIECE, HEAD_SIZE), F32)],
        ),
        name="scatter_last",
    )(table, meta, got, first, dense, other)


def two_heads(ref, p):
    first = ref[:, pl.ds(2 * p * HEAD_SIZE, HEAD_SIZE)]
    second = ref[:, pl.ds((2 * p + 1) * HEAD_SIZE, HEAD_SIZE)]
    return jnp.concatenate([first, second], axis=0)


def col_sum(x):
    return jnp.sum(x, axis=0, keepdims=True)


def sparse_body(
    meta_ref, valid_ref, q_ref, o_ref, self_ref, before_ref, after_ref, g_ref, *rest
):
    dq_ref, own_ref, prev_ref, next_ref, sent_ref = rest[-14:-9]
    kc, vc, kt, st, dp, pb, ds, dk, dv = rest[-9:]
    b = meta_ref[0]

    @pl.when(b == 0)
    def _():
        dq_ref[...] = jnp.zeros_like(dq_ref)
        own_ref[...] = jnp.zeros_like(own_ref)
        prev_ref[...] = jnp.zeros_like(prev_ref)
        next_ref[...] = jnp.zeros_like(next_ref)
        sent_ref[...] = jnp.zeros_like(sent_ref)

    @pl.when(b != 0)
    def _():
        for kv, dst in ((0, kc), (1, vc)):
            for s, part in enumerate((before_ref, self_ref, after_ref)):
                dst[s * BLOCK : (s + 1) * BLOCK] = part[kv]
            for s in range(SENT):
                at = (FIRST_SENT + s) * BLOCK
                dst[at : at + BLOCK] = g_ref[0, kv, :, s].reshape(BLOCK, HEAD_SIZE)
        kt[...] = kc[...].T
        live = [valid_ref[b * NB + s] > 0 for s in range(NB)]
        for p in range(GROUP_SIZE // 2):
            w = p % 2
            qp = two_heads(q_ref, p)
            op = two_heads(o_ref, p)
            st[w] = dot(kc[...], qp, 1, 1)
            dp[w] = dot(vc[...], op, 1, 1)
            top = jnp.full((1, 2 * BLOCK), -FAR, F32)
            for s in range(NB):
                here = jnp.max(st[w, s * BLOCK : (s + 1) * BLOCK], axis=0, keepdims=True)
                top = jnp.maximum(top, jnp.where(live[s], here, -FAR))
            top = top * EXP_SCALE
            total = jnp.zeros((1, 2 * BLOCK), F32)
            cross = jnp.zeros((1, 2 * BLOCK), F32)
            for s in range(NB):
                rows = slice(s * BLOCK, (s + 1) * BLOCK)
                shift = jnp.where(live[s], top, FAR)
                raised = jnp.exp2(st[w, rows] * EXP_SCALE - shift)
                st[w, rows] = raised
                total = total + col_sum(raised)
                cross = cross + col_sum(raised * dp[w, rows])
            inverse = 1.0 / total
            delta = cross * inverse
            for s in range(NB):
                rows = slice(s * BLOCK, (s + 1) * BLOCK)
                weights = st[w, rows] * inverse
                pb[w, rows] = weights.astype(BF16)
                ds[w, rows] = (weights * (dp[w, rows] - delta)).astype(BF16)
            new_dv = dot(pb[w], op, 1, 0)
            new_dk = dot(ds[w], qp, 1, 0)
            dv[...] = new_dv if p == 0 else dv[...] + new_dv
            dk[...] = new_dk if p == 0 else dk[...] + new_dk
            dqt = dot(kt[...], ds[w], 1, 0) * SCALING
            for j in range(2):
                dq_ref[:, pl.ds((2 * p + j) * HEAD_SIZE, HEAD_SIZE)] = (
                    dqt[:, j * BLOCK : (j + 1) * BLOCK].T.astype(BF16)
                )
        for kv, acc, factor in ((0, dk, SCALING), (1, dv, 1.0)):
            prev_ref[kv] = (acc[0:BLOCK] * factor).astype(BF16)
            own_ref[kv] = acc[BLOCK : 2 * BLOCK] * factor
            next_ref[kv] = (acc[2 * BLOCK : 3 * BLOCK] * factor).astype(BF16)
            for s in range(SENT):
                at = (FIRST_SENT + s) * BLOCK
                sent_ref[0, kv, :, s] = (
                    (acc[at : at + BLOCK] * factor).astype(BF16).reshape(GROUPS, PIECE, HEAD_SIZE)
                )


def sparse_grads(chunk, meta, valid, q, o, own, before, after, got, earlier=()):
    def at(h):
        return chunk * HALF + h

    wide = pl.BlockSpec((BLOCK, GROUP_SIZE * HEAD_SIZE), lambda h, m, t: (0, at(h)))
    pair = pl.BlockSpec((2, BLOCK, HEAD_SIZE), lambda h, m, t: (0, 0, at(h)))
    pieces = pl.BlockSpec(
        (1, 2, GROUPS, SENT, PIECE, HEAD_SIZE), lambda h, m, t: (h, 0, 0, 0, 0, 0)
    )
    keys = NB * BLOCK
    width = KEY_HEADS * HEAD_SIZE
    return pl.pallas_call(
        sparse_body,
        out_shape=(
            jax.ShapeDtypeStruct(q.shape, BF16),
            jax.ShapeDtypeStruct((2, BLOCK, width), F32),
            jax.ShapeDtypeStruct((2, BLOCK, width), BF16),
            jax.ShapeDtypeStruct((2, BLOCK, width), BF16),
            jax.ShapeDtypeStruct((HALF, 2, GROUPS, SENT, PIECE, HEAD_SIZE), BF16),
        ),
        grid_spec=pltpu.PrefetchScalarGridSpec(
            num_scalar_prefetch=2,
            grid=(HALF,),
            in_specs=[wide, wide, pair, pair, pair, pieces]
            + [pl.BlockSpec(memory_space=pl.ANY)] * len(earlier),
            out_specs=[wide, pair, pair, pair, pieces],
            scratch_shapes=[
                VM((keys, HEAD_SIZE), BF16),
                VM((keys, HEAD_SIZE), BF16),
                VM((HEAD_SIZE, keys), BF16),
                VM((2, keys, 2 * BLOCK), F32),
                VM((2, keys, 2 * BLOCK), F32),
                VM((2, keys, 2 * BLOCK), BF16),
                VM((2, keys, 2 * BLOCK), BF16),
                VM((keys, HEAD_SIZE), F32),
                VM((keys, HEAD_SIZE), F32),
            ],
        ),
        input_output_aliases={8 + n: n for n in range(len(earlier))},
        name="sparse_grads",
    )(meta, valid, q, o, own, before, after, got, *earlier)


def load_held(meta_ref, held_ref, other_ref, kc, vc):
    core = meta_ref[1]
    mine = held_ref[:, core].reshape(kc.shape)
    other = other_ref[...].reshape(kc.shape)

    @pl.when(core == 0)
    def _():
        kc[...] = mine
        vc[...] = other

    @pl.when(core != 0)
    def _():
        kc[...] = other
        vc[...] = mine


def stats_body(meta_ref, q_ref, held_ref, other_ref, out_ref, kc, vc):
    load_held(meta_ref, held_ref, other_ref, kc, vc)
    for p in range(GROUP_SIZE // 2):
        scores = dot(kc[...], two_heads(q_ref.at[0], p), 1, 1)
        grads = dot(vc[...], two_heads(q_ref.at[1], p), 1, 1)
        top = jnp.max(scores, axis=0, keepdims=True) * EXP_SCALE
        raised = jnp.exp2(scores * EXP_SCALE - top)
        for n, row in enumerate((top, col_sum(raised), col_sum(raised * grads))):
            for j in range(2):
                at = n * GROUP_SIZE + 2 * p + j
                out_ref[at : at + 1] = row[:, j * BLOCK : (j + 1) * BLOCK]


def dense_stats(meta, qo, held, other):
    keys = held.shape[0] * PIECE
    return pl.pallas_call(
        stats_body,
        out_shape=jax.ShapeDtypeStruct((3 * GROUP_SIZE, BLOCK), F32),
        in_specs=[pl.BlockSpec(memory_space=pltpu.SMEM)] + [pl.BlockSpec(memory_space=VM)] * 3,
        out_specs=pl.BlockSpec(memory_space=VM),
        scratch_shapes=[VM((keys, HEAD_SIZE), BF16), VM((keys, HEAD_SIZE), BF16)],
        name="dense_stats",
    )(meta, qo, held, other)


def merge_stats(parts):
    n = GROUP_SIZE
    top = functools.reduce(jnp.maximum, [x[:n] for x in parts])
    factors = [jnp.exp2(x[:n] - top) for x in parts]
    total = sum(x[n : 2 * n] * f for x, f in zip(parts, factors))
    cross = sum(x[2 * n :] * f for x, f in zip(parts, factors))
    return jnp.concatenate([top, total, cross], axis=0)


def dense_body(
    meta_ref, q_ref, held_ref, other_ref, s0, s1, s2, s3, dkv_ref, dq_ref, kc, vc, kt, stats
):
    load_held(meta_ref, held_ref, other_ref, kc, vc)
    kt[...] = kc[...].T
    stats[...] = merge_stats([s0[...], s1[...], s2[...], s3[...]])
    core = meta_ref[1]

    def row(n, p):
        at = n * GROUP_SIZE + 2 * p
        return jnp.concatenate([stats[at : at + 1], stats[at + 1 : at + 2]], axis=1)

    for p in range(GROUP_SIZE // 2):
        top = row(0, p)
        inverse = 1.0 / row(1, p)
        delta = row(2, p) * inverse
        qp = two_heads(q_ref.at[0], p)
        op = two_heads(q_ref.at[1], p)
        scores = dot(kc[...], qp, 1, 1)
        grads = dot(vc[...], op, 1, 1)
        weights = jnp.exp2(scores * EXP_SCALE - top) * inverse
        rounded = weights.astype(BF16)
        score_grad = (weights * (grads - delta)).astype(BF16)
        new_dk = dot(score_grad, qp, 1, 0) * SCALING
        new_dv = dot(rounded, op, 1, 0)
        dkv_ref[core] = new_dk if p == 0 else dkv_ref[core] + new_dk
        dkv_ref[1 - core] = new_dv if p == 0 else dkv_ref[1 - core] + new_dv
        dqt = dot(kt[...], score_grad, 1, 0) * SCALING
        for j in range(2):
            dq_ref[:, pl.ds((2 * p + j) * HEAD_SIZE, HEAD_SIZE)] = (
                dqt[:, j * BLOCK : (j + 1) * BLOCK].T.astype(BF16)
            )


def dense_grads(meta, qo, held, other, stats):
    keys = held.shape[0] * PIECE
    return pl.pallas_call(
        dense_body,
        out_shape=(
            jax.ShapeDtypeStruct((2, keys, HEAD_SIZE), F32),
            jax.ShapeDtypeStruct((BLOCK, GROUP_SIZE * HEAD_SIZE), BF16),
        ),
        in_specs=[pl.BlockSpec(memory_space=pltpu.SMEM)] + [pl.BlockSpec(memory_space=VM)] * 7,
        out_specs=[pl.BlockSpec(memory_space=VM)] * 2,
        scratch_shapes=[
            VM((keys, HEAD_SIZE), BF16),
            VM((keys, HEAD_SIZE), BF16),
            VM((HEAD_SIZE, keys), BF16),
            VM((3 * GROUP_SIZE, BLOCK), F32),
        ],
        name="dense_grads",
    )(meta, qo, held, other, *stats)


def combine_body(own_ref, prev_ref, next_ref, got_ref, dk_ref, dv_ref):
    for kv, out in ((0, dk_ref), (1, dv_ref)):
        for h in range(KEY_HEADS):
            cols = pl.ds(h * HEAD_SIZE, HEAD_SIZE)
            total = own_ref[kv, :, cols] + prev_ref[kv, :, cols].astype(F32)
            total = total + next_ref[kv, :, cols].astype(F32)
            pieces = got_ref[h % HALF, kv, :, h // HALF].reshape(BLOCK, HEAD_SIZE)
            out[:, cols] = (total + pieces.astype(F32)).astype(BF16)


def combine(own, from_prev, from_next, got):
    width = KEY_HEADS * HEAD_SIZE
    return pl.pallas_call(
        combine_body,
        out_shape=(jax.ShapeDtypeStruct((BLOCK, width), BF16),) * 2,
        in_specs=[pl.BlockSpec(memory_space=VM)] * 4,
        out_specs=[pl.BlockSpec(memory_space=VM)] * 2,
        name="combine",
    )(own, from_prev, from_next, got)


def spread_body(meta_ref, q_ref, o_ref, *rest):
    outs, stage, sems = rest[:-2], rest[-2], rest[-1]

    @pl.when(meta_ref[0] == 0)
    def _():
        loads, stores = [], []
        for h, out in enumerate(outs):
            cols = pl.ds(h * GROUP_SIZE * HEAD_SIZE, GROUP_SIZE * HEAD_SIZE)
            for j, ref in enumerate((q_ref, o_ref)):
                loads.append(
                    pltpu.make_async_copy(ref.at[:, cols], stage.at[h, j], sems.at[0, h, j])
                )
                stores.append(pltpu.make_async_copy(stage.at[h, j], out.at[j], sems.at[1, h, j]))
        for copy in loads:
            copy.start()
        for load, store in zip(loads, stores):
            load.wait()
            store.start()
        for copy in stores:
            copy.wait()


def spread_heads(meta, q, o):
    hbm = pl.BlockSpec(memory_space=pl.ANY)
    shape = (2, BLOCK, GROUP_SIZE * HEAD_SIZE)
    return pl.pallas_call(
        spread_body,
        out_shape=(jax.ShapeDtypeStruct(shape, BF16),) * KEY_HEADS,
        in_specs=[pl.BlockSpec(memory_space=pltpu.SMEM), hbm, hbm],
        out_specs=[hbm] * KEY_HEADS,
        scratch_shapes=[
            VM((KEY_HEADS,) + shape, BF16),
            pltpu.SemaphoreType.DMA((2, KEY_HEADS, 2)),
        ],
        name="spread_heads",
    )(meta, q, o)


def first_body(meta_ref, dq_ref, *rest):
    parts, out, stage, sems = rest[:KEY_HEADS], rest[KEY_HEADS], rest[-2], rest[-1]

    @pl.when(meta_ref[0] == 0)
    def _():
        loads, stores = [], []
        for h, part in enumerate(parts):
            cols = pl.ds(h * GROUP_SIZE * HEAD_SIZE, GROUP_SIZE * HEAD_SIZE)
            loads.append(pltpu.make_async_copy(part, stage.at[h], sems.at[0, h]))
            stores.append(pltpu.make_async_copy(stage.at[h], out.at[:, cols], sems.at[1, h]))
        for copy in loads:
            copy.start()
        for load, store in zip(loads, stores):
            load.wait()
            store.start()
        for copy in stores:
            copy.wait()


def put_first(meta, dq, parts):
    hbm = pl.BlockSpec(memory_space=pl.ANY)
    return pl.pallas_call(
        first_body,
        out_shape=jax.ShapeDtypeStruct(dq.shape, dq.dtype),
        in_specs=[pl.BlockSpec(memory_space=pltpu.SMEM)] + [hbm] * (KEY_HEADS + 1),
        out_specs=hbm,
        input_output_aliases={1: 0},
        scratch_shapes=[
            VM((KEY_HEADS, BLOCK, GROUP_SIZE * HEAD_SIZE), BF16),
            pltpu.SemaphoreType.DMA((2, KEY_HEADS)),
        ],
        name="put_first",
    )(meta, dq, *parts)


def tp_pairs(pairs, ctx_size, tp_size):
    return [(c * tp_size + a, c * tp_size + b) for c in range(ctx_size) for a, b in pairs]


def per_device(queries, key_tensor, value_tensor, output_gradient, key_blocks, slot_valid):
    tp_size, ctx_size = lax.axis_size("tp"), lax.axis_size("ctx")
    blocks = ctx_size * tp_size
    b_index = lax.axis_index("ctx") * tp_size + lax.axis_index("tp")
    core = lax.axis_index("ctx") % 2
    meta = jnp.stack([b_index, core]).astype(jnp.int32)
    table = key_blocks.reshape(-1)
    valid = slot_valid.reshape(-1)
    up = [(i, (i + 1) % blocks) for i in range(blocks)]
    down = [(i, (i - 1) % blocks) for i in range(blocks)]
    partner = [(i, (i // tp_size ^ 1) * tp_size + i % tp_size) for i in range(blocks)]
    rows = range(4)

    def swap(x):
        return lax.all_to_all(x, BOTH, split_axis=0, concat_axis=0, tiled=True)

    def send(x, pairs):
        return lax.ppermute(x, BOTH, pairs)

    def send_tp(x, pairs):
        return send(x, tp_pairs(pairs, ctx_size, tp_size))

    pieces, both = pack_pieces(key_tensor, value_tensor)
    held = swap(pieces.reshape(blocks, CHUNKS, PIECE, HEAD_SIZE))
    before, after = send(both, up), send(both, down)
    slices = spread_heads(meta, queries, output_gradient)
    qo = jnp.where(b_index == 0, slices[0], jnp.zeros_like(slices[0]))
    for c in range(1, ctx_size):
        qo = qo + send(slices[c // 2 + HALF * (c % 2)], [(0, c * tp_size)])

    listed = [gather_pieces(table, held, blocks, j) for j in range(CHUNKS)]
    given = send(give_pieces(meta, held), partner)

    one = send_tp(qo, [(0, 1)])
    qo = qo + one + send_tp(qo, [(0, 3)]) + send_tp(one, [(1, 2)])
    one = send_tp(qo, [(x, 4 + x) for x in rows])
    three = send_tp(qo, [(x, 12 + x) for x in rows])
    qo = qo + one + three + send_tp(one, [(4 + x, 8 + x) for x in rows])

    shape = (HALF, 2, GROUPS, SENT, PIECE, HEAD_SIZE)
    got = [swap(x).reshape(shape) for x in listed]
    *earlier, sent0 = sparse_grads(
        0, meta, valid, queries, output_gradient, both, before, after, got[0]
    )
    back0 = swap(sent0.reshape(blocks, SENT, PIECE, HEAD_SIZE))

    stats = dense_stats(meta, qo, held, given)
    others = [
        send_tp(stats, [(4 * z + x, 4 * z + (x + n) % 4) for z in rows for x in rows])
        for n in range(1, 4)
    ]
    stats = merge_stats([stats] + others)
    others = [
        send_tp(stats, [(4 * z + x, 4 * ((z + n) % 4) + x) for z in rows for x in rows])
        for n in range(1, 4)
    ]

    *grads, sent1 = sparse_grads(
        1, meta, valid, queries, output_gradient, both, before, after, got[1], earlier
    )
    dq, own, to_prev, to_next = grads
    back1 = swap(sent1.reshape(blocks, SENT, PIECE, HEAD_SIZE))
    from_next, from_prev = send(to_prev, down), send(to_next, up)

    dense, part = dense_grads(meta, qo, held, given, [stats] + others)
    dense_other = send(dense[1], partner)

    def add(*xs):
        return sum(x.astype(F32) for x in xs).astype(BF16)

    near = add(part, send_tp(part, [(4 * z + 2, 4 * z + 1) for z in rows]))
    part = add(
        part,
        send_tp(part, [(4 * z + 3, 4 * z) for z in rows]),
        send_tp(near, [(4 * z + 1, 4 * z) for z in rows]),
    )
    near = add(part, send_tp(part, [(8, 4)]))
    part = add(part, send_tp(part, [(12, 0)]), send_tp(near, [(4, 0)]))
    parts = [part] * KEY_HEADS
    for c in range(1, ctx_size):
        parts[c // 2 + HALF * (c % 2)] = send(part, [(c * tp_size, 0)])
    d_q = put_first(meta, dq, parts)

    first = scatter_pieces(table, back0, blocks)
    summed = scatter_last(table, meta, back1, first, dense, dense_other, blocks)
    home = swap(summed).reshape(HALF, 2, GROUPS, CHUNKS, PIECE, HEAD_SIZE)
    d_k, d_v = combine(own, from_prev, from_next, home)
    return d_q, d_k, d_v


def solution(mesh):
    spec = P(BOTH, None)
    return jax.shard_map(
        per_device,
        mesh=mesh,
        in_specs=(spec, spec, spec, spec, P(), P()),
        out_specs=(spec, spec, spec),
        check_vma=False,
    )
```

```python
import functools
import math

import jax
import jax.numpy as jnp
from jax import lax
from jax.experimental import pallas as pl
from jax.experimental.pallas import tpu as pltpu
from jax.sharding import PartitionSpec as P


KEY_HEADS = 8
GROUP_SIZE = 8
HEAD_SIZE = 128
BLOCK = 128
NB = 8
GROUPS = 16
PIECE = 8
SENT = 5
FIRST_SENT = NB - SENT
CHUNKS = 2
HALF = KEY_HEADS // CHUNKS
CALL_HEADS = 2
BOTH = ("ctx", "tp")
SCALING = 1.0 / math.sqrt(HEAD_SIZE)
EXP_SCALE = SCALING * math.log2(math.e)
FAR = 1e30
F32 = jnp.float32
BF16 = jnp.bfloat16
VM = pltpu.VMEM


def dot(a, b, ca, cb):
    return lax.dot_general(a, b, (((ca,), (cb,)), ((), ())), preferred_element_type=F32)


def pack_body(k_ref, v_ref, out_ref, both_ref):
    for kv, ref in enumerate((k_ref, v_ref)):
        both_ref[kv] = ref[...]
        for j in range(CHUNKS):
            for y in range(HALF):
                cols = pl.ds((j * HALF + y) * HEAD_SIZE, HEAD_SIZE)
                out_ref[y, kv, :, j] = ref[:, cols].reshape(GROUPS, PIECE, HEAD_SIZE)


def pack_pieces(k, v):
    return pl.pallas_call(
        pack_body,
        out_shape=(
            jax.ShapeDtypeStruct((HALF, 2, GROUPS, CHUNKS, PIECE, HEAD_SIZE), BF16),
            jax.ShapeDtypeStruct((2,) + k.shape, BF16),
        ),
        in_specs=[pl.BlockSpec(memory_space=VM)] * 2,
        out_specs=[pl.BlockSpec(memory_space=VM)] * 2,
        name="pack_pieces",
    )(k, v)


def gather_body(table_ref, held_ref, out_ref, *, rows, chunk):
    base = pl.program_id(0) * rows

    def one(d, carry):
        for s in range(SENT):
            block = table_ref[(base + d) * NB + FIRST_SENT + s]
            out_ref[d, s] = held_ref[block, chunk]
        return carry

    lax.fori_loop(0, rows, one, 0, unroll=4)


def gather_pieces(table, held, blocks, chunk):
    steps = 4
    rows = blocks // steps
    return pl.pallas_call(
        functools.partial(gather_body, rows=rows, chunk=chunk),
        out_shape=jax.ShapeDtypeStruct((blocks, SENT, PIECE, HEAD_SIZE), BF16),
        grid_spec=pltpu.PrefetchScalarGridSpec(
            num_scalar_prefetch=1,
            grid=(steps,),
            in_specs=[
                pl.BlockSpec((blocks, CHUNKS, PIECE, HEAD_SIZE), lambda i, t: (0, 0, 0, 0))
            ],
            out_specs=pl.BlockSpec((rows, SENT, PIECE, HEAD_SIZE), lambda i, t: (i, 0, 0, 0)),
        ),
        name="gather_pieces",
    )(table, held)


def give_body(meta_ref, held_ref, out_ref):
    out_ref[...] = held_ref[:, 1 - meta_ref[1]]


def give_pieces(meta, held):
    return pl.pallas_call(
        give_body,
        out_shape=jax.ShapeDtypeStruct(held.shape[:1] + held.shape[2:], BF16),
        in_specs=[pl.BlockSpec(memory_space=pltpu.SMEM), pl.BlockSpec(memory_space=VM)],
        out_specs=pl.BlockSpec(memory_space=VM),
        name="give_pieces",
    )(meta, held)


def add_listed(table_ref, got_ref, acc_ref, rows):
    base = pl.program_id(0) * rows

    def one(d, carry):
        for s in range(SENT):
            block = table_ref[(base + d) * NB + FIRST_SENT + s]
            acc_ref[block] += got_ref[d, s].astype(F32)
        return carry

    lax.fori_loop(0, rows, one, 0, unroll=4)


def scatter_body(table_ref, got_ref, out_ref, *, rows):
    @pl.when(pl.program_id(0) == 0)
    def _():
        out_ref[...] = jnp.zeros_like(out_ref)

    add_listed(table_ref, got_ref, out_ref, rows)


def scatter_last_body(
    table_ref, meta_ref, got_ref, first_ref, dense_ref, other_ref, out_ref, acc_ref, *, rows
):
    @pl.when(pl.program_id(0) == 0)
    def _():
        acc_ref[...] = jnp.zeros_like(acc_ref)

    add_listed(table_ref, got_ref, acc_ref, rows)

    @pl.when(pl.program_id(0) == pl.num_programs(0) - 1)
    def _():
        core = meta_ref[1]
        mine = dense_ref[0].reshape(acc_ref.shape)
        other = other_ref[...].reshape(acc_ref.shape)
        out_ref[:, core] = (jnp.where(core == 0, first_ref[...], acc_ref[...]) + mine).astype(BF16)
        out_ref[:, 1 - core] = (
            jnp.where(core == 0, acc_ref[...], first_ref[...]) + other
        ).astype(BF16)


def scatter_pieces(table, got, blocks):
    steps = 4
    rows = blocks // steps
    return pl.pallas_call(
        functools.partial(scatter_body, rows=rows),
        out_shape=jax.ShapeDtypeStruct((blocks, PIECE, HEAD_SIZE), F32),
        grid_spec=pltpu.PrefetchScalarGridSpec(
            num_scalar_prefetch=1,
            grid=(steps,),
            in_specs=[pl.BlockSpec((rows, SENT, PIECE, HEAD_SIZE), lambda i, t: (i, 0, 0, 0))],
            out_specs=pl.BlockSpec((blocks, PIECE, HEAD_SIZE), lambda i, t: (0, 0, 0)),
        ),
        name="scatter_pieces",
    )(table, got)


def scatter_last(table, meta, got, first, dense, other, blocks):
    steps = 4
    rows = blocks // steps
    whole = pl.BlockSpec((blocks, PIECE, HEAD_SIZE), lambda i, t, m: (0, 0, 0))
    return pl.pallas_call(
        functools.partial(scatter_last_body, rows=rows),
        out_shape=jax.ShapeDtypeStruct((blocks, CHUNKS, PIECE, HEAD_SIZE), BF16),
        grid_spec=pltpu.PrefetchScalarGridSpec(
            num_scalar_prefetch=2,
            grid=(steps,),
            in_specs=[
                pl.BlockSpec((rows, SENT, PIECE, HEAD_SIZE), lambda i, t, m: (i, 0, 0, 0)),
                whole,
                pl.BlockSpec((1, blocks * PIECE, HEAD_SIZE), lambda i, t, m: (0, 0, 0)),
                pl.BlockSpec((blocks * PIECE, HEAD_SIZE), lambda i, t, m: (0, 0)),
            ],
            out_specs=pl.BlockSpec(
                (blocks, CHUNKS, PIECE, HEAD_SIZE), lambda i, t, m: (0, 0, 0, 0)
            ),
            scratch_shapes=[VM((blocks, PIECE, HEAD_SIZE), F32)],
        ),
        name="scatter_last",
    )(table, meta, got, first, dense, other)


def two_heads(ref, p):
    first = ref[:, pl.ds(2 * p * HEAD_SIZE, HEAD_SIZE)]
    second = ref[:, pl.ds((2 * p + 1) * HEAD_SIZE, HEAD_SIZE)]
    return jnp.concatenate([first, second], axis=0)


def col_sum(x):
    return jnp.sum(x, axis=0, keepdims=True)


def sparse_body(
    meta_ref, valid_ref, q_ref, o_ref, self_ref, before_ref, after_ref, g_ref, *rest
):
    dq_ref, own_ref, prev_ref, next_ref, sent_ref = rest[-14:-9]
    kc, vc, kt, st, dp, pb, ds, dk, dv = rest[-9:]
    b = meta_ref[0]

    @pl.when(b == 0)
    def _():
        dq_ref[...] = jnp.zeros_like(dq_ref)
        own_ref[...] = jnp.zeros_like(own_ref)
        prev_ref[...] = jnp.zeros_like(prev_ref)
        next_ref[...] = jnp.zeros_like(next_ref)
        sent_ref[...] = jnp.zeros_like(sent_ref)

    @pl.when(b != 0)
    def _():
        for kv, dst in ((0, kc), (1, vc)):
            for s, part in enumerate((before_ref, self_ref, after_ref)):
                dst[s * BLOCK : (s + 1) * BLOCK] = part[kv]
            for s in range(SENT):
                at = (FIRST_SENT + s) * BLOCK
                dst[at : at + BLOCK] = g_ref[0, kv, :, s].reshape(BLOCK, HEAD_SIZE)
        kt[...] = kc[...].T
        live = [valid_ref[b * NB + s] > 0 for s in range(NB)]
        dk[...] = jnp.zeros_like(dk)
        dv[...] = jnp.zeros_like(dv)

        def heads(ref, p):
            at = pl.multiple_of(2 * p * HEAD_SIZE, 2 * HEAD_SIZE)
            both = ref[:, pl.ds(at, 2 * HEAD_SIZE)]
            return jnp.concatenate([both[:, :HEAD_SIZE], both[:, HEAD_SIZE:]], axis=0)

        def pair(p, w):
            qp = heads(q_ref, p)
            op = heads(o_ref, p)
            st[w] = dot(kc[...], qp, 1, 1)
            dp[w] = dot(vc[...], op, 1, 1)
            top = jnp.full((1, 2 * BLOCK), -FAR, F32)
            for s in range(NB):
                here = jnp.max(st[w, s * BLOCK : (s + 1) * BLOCK], axis=0, keepdims=True)
                top = jnp.maximum(top, jnp.where(live[s], here, -FAR))
            top = top * EXP_SCALE
            total = jnp.zeros((1, 2 * BLOCK), F32)
            cross = jnp.zeros((1, 2 * BLOCK), F32)
            for s in range(NB):
                rows = slice(s * BLOCK, (s + 1) * BLOCK)
                shift = jnp.where(live[s], top, FAR)
                raised = jnp.exp2(st[w, rows] * EXP_SCALE - shift)
                st[w, rows] = raised
                total = total + col_sum(raised)
                cross = cross + col_sum(raised * dp[w, rows])
            inverse = 1.0 / total
            delta = cross * inverse
            for s in range(NB):
                rows = slice(s * BLOCK, (s + 1) * BLOCK)
                weights = st[w, rows] * inverse
                pb[w, rows] = weights.astype(BF16)
                ds[w, rows] = (weights * (dp[w, rows] - delta)).astype(BF16)
            new_dv = dot(pb[w], op, 1, 0)
            new_dk = dot(ds[w], qp, 1, 0)
            dv[...] += new_dv
            dk[...] += new_dk
            dqt = dot(kt[...], ds[w], 1, 0) * SCALING
            out = jnp.concatenate([dqt[:, :BLOCK].T, dqt[:, BLOCK:].T], axis=1).astype(BF16)
            dq_ref[:, pl.ds(pl.multiple_of(2 * p * HEAD_SIZE, 2 * HEAD_SIZE), 2 * HEAD_SIZE)] = out

        def two_pairs(i, carry):
            for w in range(2):
                pair(2 * i + w, w)
            return carry

        lax.fori_loop(0, GROUP_SIZE // 4, two_pairs, 0)
        for kv, acc, factor in ((0, dk, SCALING), (1, dv, 1.0)):
            prev_ref[kv] = (acc[0:BLOCK] * factor).astype(BF16)
            own_ref[kv] = acc[BLOCK : 2 * BLOCK] * factor
            next_ref[kv] = (acc[2 * BLOCK : 3 * BLOCK] * factor).astype(BF16)
            for s in range(SENT):
                at = (FIRST_SENT + s) * BLOCK
                sent_ref[0, kv, :, s] = (
                    (acc[at : at + BLOCK] * factor).astype(BF16).reshape(GROUPS, PIECE, HEAD_SIZE)
                )


def sparse_grads(call, meta, valid, q, o, own, before, after, got, earlier=()):
    first = call * CALL_HEADS
    inside = first % HALF

    wide = pl.BlockSpec((BLOCK, GROUP_SIZE * HEAD_SIZE), lambda h, m, t: (0, first + h))
    pair = pl.BlockSpec((2, BLOCK, HEAD_SIZE), lambda h, m, t: (0, 0, first + h))
    pieces = pl.BlockSpec(
        (1, 2, GROUPS, SENT, PIECE, HEAD_SIZE), lambda h, m, t: (inside + h, 0, 0, 0, 0, 0)
    )
    keys = NB * BLOCK
    width = KEY_HEADS * HEAD_SIZE
    return pl.pallas_call(
        sparse_body,
        out_shape=(
            jax.ShapeDtypeStruct(q.shape, BF16),
            jax.ShapeDtypeStruct((2, BLOCK, width), F32),
            jax.ShapeDtypeStruct((2, BLOCK, width), BF16),
            jax.ShapeDtypeStruct((2, BLOCK, width), BF16),
            jax.ShapeDtypeStruct((HALF, 2, GROUPS, SENT, PIECE, HEAD_SIZE), BF16),
        ),
        grid_spec=pltpu.PrefetchScalarGridSpec(
            num_scalar_prefetch=2,
            grid=(CALL_HEADS,),
            in_specs=[wide, wide, pair, pair, pair, pieces]
            + [pl.BlockSpec(memory_space=pl.ANY)] * len(earlier),
            out_specs=[wide, pair, pair, pair, pieces],
            scratch_shapes=[
                VM((keys, HEAD_SIZE), BF16),
                VM((keys, HEAD_SIZE), BF16),
                VM((HEAD_SIZE, keys), BF16),
                VM((2, keys, 2 * BLOCK), F32),
                VM((2, keys, 2 * BLOCK), F32),
                VM((2, keys, 2 * BLOCK), BF16),
                VM((2, keys, 2 * BLOCK), BF16),
                VM((keys, HEAD_SIZE), F32),
                VM((keys, HEAD_SIZE), F32),
            ],
        ),
        input_output_aliases={8 + n: n for n in range(len(earlier))},
        name="sparse_grads",
    )(meta, valid, q, o, own, before, after, got, *earlier)


def load_held(meta_ref, held_ref, other_ref, kc, vc):
    core = meta_ref[1]
    mine = held_ref[:, core].reshape(kc.shape)
    other = other_ref[...].reshape(kc.shape)

    @pl.when(core == 0)
    def _():
        kc[...] = mine
        vc[...] = other

    @pl.when(core != 0)
    def _():
        kc[...] = other
        vc[...] = mine


def stats_body(meta_ref, q_ref, held_ref, other_ref, out_ref, kc, vc):
    load_held(meta_ref, held_ref, other_ref, kc, vc)
    for p in range(GROUP_SIZE // 2):
        scores = dot(kc[...], two_heads(q_ref.at[0], p), 1, 1)
        grads = dot(vc[...], two_heads(q_ref.at[1], p), 1, 1)
        top = jnp.max(scores, axis=0, keepdims=True) * EXP_SCALE
        raised = jnp.exp2(scores * EXP_SCALE - top)
        for n, row in enumerate((top, col_sum(raised), col_sum(raised * grads))):
            for j in range(2):
                at = n * GROUP_SIZE + 2 * p + j
                out_ref[at : at + 1] = row[:, j * BLOCK : (j + 1) * BLOCK]


def dense_stats(meta, qo, held, other):
    keys = held.shape[0] * PIECE
    return pl.pallas_call(
        stats_body,
        out_shape=jax.ShapeDtypeStruct((3 * GROUP_SIZE, BLOCK), F32),
        in_specs=[pl.BlockSpec(memory_space=pltpu.SMEM)] + [pl.BlockSpec(memory_space=VM)] * 3,
        out_specs=pl.BlockSpec(memory_space=VM),
        scratch_shapes=[VM((keys, HEAD_SIZE), BF16), VM((keys, HEAD_SIZE), BF16)],
        name="dense_stats",
    )(meta, qo, held, other)


def merge_stats(parts):
    n = GROUP_SIZE
    top = functools.reduce(jnp.maximum, [x[:n] for x in parts])
    factors = [jnp.exp2(x[:n] - top) for x in parts]
    total = sum(x[n : 2 * n] * f for x, f in zip(parts, factors))
    cross = sum(x[2 * n :] * f for x, f in zip(parts, factors))
    return jnp.concatenate([top, total, cross], axis=0)


def dense_body(
    meta_ref, q_ref, held_ref, other_ref, s0, s1, s2, s3, dkv_ref, d0, d1, d2, d3,
    kc, vc, kt, stats,
):
    load_held(meta_ref, held_ref, other_ref, kc, vc)
    kt[...] = kc[...].T
    stats[...] = merge_stats([s0[...], s1[...], s2[...], s3[...]])
    core = meta_ref[1]

    for m, dq_ref in enumerate((d0, d1, d2, d3)):
        p = lax.rem(meta_ref[2] + m, 4)

        def row(n):
            at = n * GROUP_SIZE + 2 * p
            return jnp.concatenate([stats[pl.ds(at, 1)], stats[pl.ds(at + 1, 1)]], axis=1)

        def heads(ref):
            at = pl.multiple_of(2 * p * HEAD_SIZE, 2 * HEAD_SIZE)
            both = ref[:, pl.ds(at, 2 * HEAD_SIZE)]
            return jnp.concatenate([both[:, :HEAD_SIZE], both[:, HEAD_SIZE:]], axis=0)

        top = row(0)
        inverse = 1.0 / row(1)
        delta = row(2) * inverse
        qp = heads(q_ref.at[0])
        op = heads(q_ref.at[1])
        scores = dot(kc[...], qp, 1, 1)
        grads = dot(vc[...], op, 1, 1)
        weights = jnp.exp2(scores * EXP_SCALE - top) * inverse
        rounded = weights.astype(BF16)
        score_grad = (weights * (grads - delta)).astype(BF16)
        new_dk = dot(score_grad, qp, 1, 0) * SCALING
        new_dv = dot(rounded, op, 1, 0)
        dkv_ref[core] = new_dk if m == 0 else dkv_ref[core] + new_dk
        dkv_ref[1 - core] = new_dv if m == 0 else dkv_ref[1 - core] + new_dv
        dqt = dot(kt[...], score_grad, 1, 0) * SCALING
        for j in range(2):
            dq_ref[:, j * HEAD_SIZE : (j + 1) * HEAD_SIZE] = (
                dqt[:, j * BLOCK : (j + 1) * BLOCK].T.astype(BF16)
            )


def dense_grads(meta, qo, held, other, stats):
    keys = held.shape[0] * PIECE
    quarter = jax.ShapeDtypeStruct((BLOCK, 2 * HEAD_SIZE), BF16)
    return pl.pallas_call(
        dense_body,
        out_shape=(jax.ShapeDtypeStruct((2, keys, HEAD_SIZE), F32),) + (quarter,) * 4,
        in_specs=[pl.BlockSpec(memory_space=pltpu.SMEM)] + [pl.BlockSpec(memory_space=VM)] * 7,
        out_specs=[pl.BlockSpec(memory_space=VM)] * 5,
        scratch_shapes=[
            VM((keys, HEAD_SIZE), BF16),
            VM((keys, HEAD_SIZE), BF16),
            VM((HEAD_SIZE, keys), BF16),
            VM((3 * GROUP_SIZE, BLOCK), F32),
        ],
        name="dense_grads",
    )(meta, qo, held, other, *stats)


def combine_body(own_ref, prev_ref, next_ref, got_ref, dk_ref, dv_ref):
    for kv, out in ((0, dk_ref), (1, dv_ref)):
        for h in range(KEY_HEADS):
            cols = pl.ds(h * HEAD_SIZE, HEAD_SIZE)
            total = own_ref[kv, :, cols] + prev_ref[kv, :, cols].astype(F32)
            total = total + next_ref[kv, :, cols].astype(F32)
            pieces = got_ref[h % HALF, kv, :, h // HALF].reshape(BLOCK, HEAD_SIZE)
            out[:, cols] = (total + pieces.astype(F32)).astype(BF16)


def combine(own, from_prev, from_next, got):
    width = KEY_HEADS * HEAD_SIZE
    return pl.pallas_call(
        combine_body,
        out_shape=(jax.ShapeDtypeStruct((BLOCK, width), BF16),) * 2,
        in_specs=[pl.BlockSpec(memory_space=VM)] * 4,
        out_specs=[pl.BlockSpec(memory_space=VM)] * 2,
        name="combine",
    )(own, from_prev, from_next, got)


def spread_body(meta_ref, q_ref, o_ref, *rest):
    outs, stage, sems = rest[:-2], rest[-2], rest[-1]

    @pl.when(meta_ref[0] == 0)
    def _():
        loads, stores = [], []
        for h, out in enumerate(outs):
            cols = pl.ds(h * GROUP_SIZE * HEAD_SIZE, GROUP_SIZE * HEAD_SIZE)
            for j, ref in enumerate((q_ref, o_ref)):
                loads.append(
                    pltpu.make_async_copy(ref.at[:, cols], stage.at[h, j], sems.at[0, h, j])
                )
                stores.append(pltpu.make_async_copy(stage.at[h, j], out.at[j], sems.at[1, h, j]))
        for copy in loads:
            copy.start()
        for load, store in zip(loads, stores):
            load.wait()
            store.start()
        for copy in stores:
            copy.wait()


def spread_heads(meta, q, o):
    hbm = pl.BlockSpec(memory_space=pl.ANY)
    shape = (2, BLOCK, GROUP_SIZE * HEAD_SIZE)
    return pl.pallas_call(
        spread_body,
        out_shape=(jax.ShapeDtypeStruct(shape, BF16),) * KEY_HEADS,
        in_specs=[pl.BlockSpec(memory_space=pltpu.SMEM), hbm, hbm],
        out_specs=[hbm] * KEY_HEADS,
        scratch_shapes=[
            VM((KEY_HEADS,) + shape, BF16),
            pltpu.SemaphoreType.DMA((2, KEY_HEADS, 2)),
        ],
        name="spread_heads",
    )(meta, q, o)


def first_body(meta_ref, dq_ref, *rest):
    parts, out, stage, sems = rest[:KEY_HEADS], rest[KEY_HEADS], rest[-2], rest[-1]

    @pl.when(meta_ref[0] == 0)
    def _():
        loads, stores = [], []
        for h, part in enumerate(parts):
            cols = pl.ds(h * GROUP_SIZE * HEAD_SIZE, GROUP_SIZE * HEAD_SIZE)
            loads.append(pltpu.make_async_copy(part, stage.at[h], sems.at[0, h]))
            stores.append(pltpu.make_async_copy(stage.at[h], out.at[:, cols], sems.at[1, h]))
        for copy in loads:
            copy.start()
        for load, store in zip(loads, stores):
            load.wait()
            store.start()
        for copy in stores:
            copy.wait()


def put_first(meta, dq, parts):
    hbm = pl.BlockSpec(memory_space=pl.ANY)
    return pl.pallas_call(
        first_body,
        out_shape=jax.ShapeDtypeStruct(dq.shape, dq.dtype),
        in_specs=[pl.BlockSpec(memory_space=pltpu.SMEM)] + [hbm] * (KEY_HEADS + 1),
        out_specs=hbm,
        input_output_aliases={1: 0},
        scratch_shapes=[
            VM((KEY_HEADS, BLOCK, GROUP_SIZE * HEAD_SIZE), BF16),
            pltpu.SemaphoreType.DMA((2, KEY_HEADS)),
        ],
        name="put_first",
    )(meta, dq, *parts)


def tp_pairs(pairs, ctx_size, tp_size):
    return [(c * tp_size + a, c * tp_size + b) for c in range(ctx_size) for a, b in pairs]


def add(*xs):
    return sum(x.astype(F32) for x in xs).astype(BF16)


def per_device(queries, key_tensor, value_tensor, output_gradient, key_blocks, slot_valid):
    tp_size, ctx_size = lax.axis_size("tp"), lax.axis_size("ctx")
    blocks = ctx_size * tp_size
    b_index = lax.axis_index("ctx") * tp_size + lax.axis_index("tp")
    core = lax.axis_index("ctx") % 2
    meta = jnp.stack([b_index, core, lax.axis_index("tp") % 4]).astype(jnp.int32)
    table = key_blocks.reshape(-1)
    valid = slot_valid.reshape(-1)
    up = [(i, (i + 1) % blocks) for i in range(blocks)]
    down = [(i, (i - 1) % blocks) for i in range(blocks)]
    partner = [(i, (i // tp_size ^ 1) * tp_size + i % tp_size) for i in range(blocks)]
    four = range(4)

    def swap(x):
        return lax.all_to_all(x, BOTH, split_axis=0, concat_axis=0, tiled=True)

    def send(x, pairs):
        return lax.ppermute(x, BOTH, pairs)

    def send_tp(x, pairs):
        return send(x, tp_pairs(pairs, ctx_size, tp_size))

    def along_x(n):
        return [(4 * z + x, 4 * z + (x + n) % 4) for z in four for x in four]

    def along_z(n):
        return [(4 * z + x, 4 * ((z + n) % 4) + x) for z in four for x in four]

    pieces, both = pack_pieces(key_tensor, value_tensor)
    held = swap(pieces.reshape(blocks, CHUNKS, PIECE, HEAD_SIZE))
    before, after = send(both, up), send(both, down)
    slices = spread_heads(meta, queries, output_gradient)
    qo = jnp.where(b_index == 0, slices[0], jnp.zeros_like(slices[0]))
    for c in range(1, ctx_size):
        qo = qo + send(slices[c // 2 + HALF * (c % 2)], [(0, c * tp_size)])

    listed = []
    for j in range(CHUNKS):
        listed.append(gather_pieces(table, held, blocks, j))
    given = give_pieces(meta, held)
    given = send(given, partner)
    shape = (HALF, 2, GROUPS, SENT, PIECE, HEAD_SIZE)
    got = []
    for j in range(CHUNKS):
        got.append(swap(listed[j]).reshape(shape))

    qo = qo + send_tp(qo, [(0, 1)])
    qo = qo + send_tp(qo, [(0, 3), (1, 2)])
    qo = qo + send_tp(qo, [(x, 4 + x) for x in four])
    qo = qo + send_tp(qo, [(x, 12 + x) for x in four] + [(4 + x, 8 + x) for x in four])

    grads, back = (), []
    calls = HALF // CALL_HEADS
    for j in range(CHUNKS):
        for n in range(calls):
            call = calls * j + n
            grads = sparse_grads(
                call, meta, valid, queries, output_gradient, both, before, after, got[j],
                grads if n > 0 else grads[:4],
            )
        back.append(swap(grads[4].reshape(blocks, SENT, PIECE, HEAD_SIZE)))
    dq, own, to_prev, to_next = grads[:4]
    from_next, from_prev = send(to_prev, down), send(to_next, up)

    stats = dense_stats(meta, qo, held, given)
    others = [send_tp(stats, along_x(n)) for n in range(1, 4)]
    stats = merge_stats([stats] + others)
    others = [send_tp(stats, along_z(n)) for n in range(1, 4)]
    dense, *part = dense_grads(meta, qo, held, given, [stats] + others)
    dense_other = send(dense[1], partner)
    others = [send_tp(part[n], along_x(n)) for n in range(1, 4)]
    total = add(part[0], *others)
    others = [send_tp(total, [(4 * n + x, x) for x in four]) for n in range(1, 4)]
    total = add(total, *others)
    others = [send_tp(total, [(n, 0)]) for n in range(1, 4)]
    total = jnp.concatenate([total] + others, axis=1)
    parts = [total] * KEY_HEADS
    for c in range(1, ctx_size):
        parts[c // 2 + HALF * (c % 2)] = send(total, [(c * tp_size, 0)])
    d_q = put_first(meta, dq, parts)

    first = scatter_pieces(table, back[0], blocks)
    summed = scatter_last(table, meta, back[1], first, dense, dense_other, blocks)
    home = swap(summed).reshape(HALF, 2, GROUPS, CHUNKS, PIECE, HEAD_SIZE)
    d_k, d_v = combine(own, from_prev, from_next, home)
    return d_q, d_k, d_v


def solution(mesh):
    spec = P(BOTH, None)

    return jax.shard_map(
        per_device,
        mesh=mesh,
        in_specs=(spec, spec, spec, spec, P(), P()),
        out_specs=(spec, spec, spec),
        check_vma=False,
    )
```

```python
import functools
import math

import jax
import jax.numpy as jnp
from jax import lax
from jax.experimental import pallas as pl
from jax.experimental.pallas import tpu as pltpu
from jax.sharding import PartitionSpec as P


KEY_HEADS = 8
GROUP_SIZE = 8
HEAD_SIZE = 128
BLOCK = 128
NB = 8
GROUPS = 16
PIECE = 8
SENT = 5
FIRST_SENT = NB - SENT
CHUNKS = 2
HALF = KEY_HEADS // CHUNKS
CALL_HEADS = 2
BOTH = ("ctx", "tp")
SCALING = 1.0 / math.sqrt(HEAD_SIZE)
EXP_SCALE = SCALING * math.log2(math.e)
FAR = 1e30
F32 = jnp.float32
BF16 = jnp.bfloat16
VM = pltpu.VMEM


def dot(a, b, ca, cb):
    return lax.dot_general(a, b, (((ca,), (cb,)), ((), ())), preferred_element_type=F32)


def pack_body(k_ref, v_ref, out_ref, both_ref):
    for kv, ref in enumerate((k_ref, v_ref)):
        both_ref[kv] = ref[...]
        for j in range(CHUNKS):
            for y in range(HALF):
                cols = pl.ds((j * HALF + y) * HEAD_SIZE, HEAD_SIZE)
                out_ref[y, kv, :, j] = ref[:, cols].reshape(GROUPS, PIECE, HEAD_SIZE)


def pack_pieces(k, v):
    return pl.pallas_call(
        pack_body,
        out_shape=(
            jax.ShapeDtypeStruct((HALF, 2, GROUPS, CHUNKS, PIECE, HEAD_SIZE), BF16),
            jax.ShapeDtypeStruct((2,) + k.shape, BF16),
        ),
        in_specs=[pl.BlockSpec(memory_space=VM)] * 2,
        out_specs=[pl.BlockSpec(memory_space=VM)] * 2,
        name="pack_pieces",
    )(k, v)


def gather_body(table_ref, held_ref, out_ref, *, rows, chunk):
    base = pl.program_id(0) * rows

    def one(d, carry):
        for s in range(SENT):
            block = table_ref[(base + d) * NB + FIRST_SENT + s]
            out_ref[d, s] = held_ref[block, chunk]
        return carry

    lax.fori_loop(0, rows, one, 0, unroll=4)


def gather_pieces(table, held, blocks, chunk):
    steps = 4
    rows = blocks // steps
    return pl.pallas_call(
        functools.partial(gather_body, rows=rows, chunk=chunk),
        out_shape=jax.ShapeDtypeStruct((blocks, SENT, PIECE, HEAD_SIZE), BF16),
        grid_spec=pltpu.PrefetchScalarGridSpec(
            num_scalar_prefetch=1,
            grid=(steps,),
            in_specs=[
                pl.BlockSpec((blocks, CHUNKS, PIECE, HEAD_SIZE), lambda i, t: (0, 0, 0, 0))
            ],
            out_specs=pl.BlockSpec((rows, SENT, PIECE, HEAD_SIZE), lambda i, t: (i, 0, 0, 0)),
        ),
        name="gather_pieces",
    )(table, held)


def give_body(meta_ref, held_ref, out_ref):
    out_ref[...] = held_ref[:, 1 - meta_ref[1]]


def give_pieces(meta, held):
    return pl.pallas_call(
        give_body,
        out_shape=jax.ShapeDtypeStruct(held.shape[:1] + held.shape[2:], BF16),
        in_specs=[pl.BlockSpec(memory_space=pltpu.SMEM), pl.BlockSpec(memory_space=VM)],
        out_specs=pl.BlockSpec(memory_space=VM),
        name="give_pieces",
    )(meta, held)


def add_listed(table_ref, got_ref, acc_ref, rows):
    base = pl.program_id(0) * rows

    def one(d, carry):
        for s in range(SENT):
            block = table_ref[(base + d) * NB + FIRST_SENT + s]
            acc_ref[block] += got_ref[d, s].astype(F32)
        return carry

    lax.fori_loop(0, rows, one, 0, unroll=4)


def scatter_body(table_ref, got_ref, out_ref, *, rows):
    @pl.when(pl.program_id(0) == 0)
    def _():
        out_ref[...] = jnp.zeros_like(out_ref)

    add_listed(table_ref, got_ref, out_ref, rows)


def scatter_last_body(
    table_ref, meta_ref, got_ref, first_ref, dense_ref, other_ref, out_ref, acc_ref, *, rows
):
    @pl.when(pl.program_id(0) == 0)
    def _():
        acc_ref[...] = jnp.zeros_like(acc_ref)

    add_listed(table_ref, got_ref, acc_ref, rows)

    @pl.when(pl.program_id(0) == pl.num_programs(0) - 1)
    def _():
        core = meta_ref[1]
        mine = dense_ref[0].reshape(acc_ref.shape)
        other = other_ref[...].reshape(acc_ref.shape)
        out_ref[:, core] = (jnp.where(core == 0, first_ref[...], acc_ref[...]) + mine).astype(BF16)
        out_ref[:, 1 - core] = (
            jnp.where(core == 0, acc_ref[...], first_ref[...]) + other
        ).astype(BF16)


def scatter_pieces(table, got, blocks):
    steps = 4
    rows = blocks // steps
    return pl.pallas_call(
        functools.partial(scatter_body, rows=rows),
        out_shape=jax.ShapeDtypeStruct((blocks, PIECE, HEAD_SIZE), F32),
        grid_spec=pltpu.PrefetchScalarGridSpec(
            num_scalar_prefetch=1,
            grid=(steps,),
            in_specs=[pl.BlockSpec((rows, SENT, PIECE, HEAD_SIZE), lambda i, t: (i, 0, 0, 0))],
            out_specs=pl.BlockSpec((blocks, PIECE, HEAD_SIZE), lambda i, t: (0, 0, 0)),
        ),
        name="scatter_pieces",
    )(table, got)


def scatter_last(table, meta, got, first, dense, other, blocks):
    steps = 4
    rows = blocks // steps
    whole = pl.BlockSpec((blocks, PIECE, HEAD_SIZE), lambda i, t, m: (0, 0, 0))
    return pl.pallas_call(
        functools.partial(scatter_last_body, rows=rows),
        out_shape=jax.ShapeDtypeStruct((blocks, CHUNKS, PIECE, HEAD_SIZE), BF16),
        grid_spec=pltpu.PrefetchScalarGridSpec(
            num_scalar_prefetch=2,
            grid=(steps,),
            in_specs=[
                pl.BlockSpec((rows, SENT, PIECE, HEAD_SIZE), lambda i, t, m: (i, 0, 0, 0)),
                whole,
                pl.BlockSpec((1, blocks * PIECE, HEAD_SIZE), lambda i, t, m: (0, 0, 0)),
                pl.BlockSpec((blocks * PIECE, HEAD_SIZE), lambda i, t, m: (0, 0)),
            ],
            out_specs=pl.BlockSpec(
                (blocks, CHUNKS, PIECE, HEAD_SIZE), lambda i, t, m: (0, 0, 0, 0)
            ),
            scratch_shapes=[VM((blocks, PIECE, HEAD_SIZE), F32)],
        ),
        name="scatter_last",
    )(table, meta, got, first, dense, other)


def two_heads(ref, p):
    first = ref[:, pl.ds(2 * p * HEAD_SIZE, HEAD_SIZE)]
    second = ref[:, pl.ds((2 * p + 1) * HEAD_SIZE, HEAD_SIZE)]
    return jnp.concatenate([first, second], axis=0)


def dynamic_heads(ref, p):
    at = pl.multiple_of(2 * p * HEAD_SIZE, 2 * HEAD_SIZE)
    both = ref[:, pl.ds(at, 2 * HEAD_SIZE)]
    return jnp.concatenate([both[:, :HEAD_SIZE], both[:, HEAD_SIZE:]], axis=0)


def col_sum(x):
    return jnp.sum(x, axis=0, keepdims=True)


def sparse_body(
    meta_ref, valid_ref, q_ref, o_ref, self_ref, before_ref, after_ref, g_ref, *rest
):
    dq_ref, own_ref, prev_ref, next_ref, sent_ref = rest[-14:-9]
    kc, vc, kt, st, dp, pb, ds, dk, dv = rest[-9:]
    b = meta_ref[0]

    @pl.when(b == 0)
    def _():
        dq_ref[...] = jnp.zeros_like(dq_ref)
        own_ref[...] = jnp.zeros_like(own_ref)
        prev_ref[...] = jnp.zeros_like(prev_ref)
        next_ref[...] = jnp.zeros_like(next_ref)
        sent_ref[...] = jnp.zeros_like(sent_ref)

    @pl.when(b != 0)
    def _():
        for kv, dst in ((0, kc), (1, vc)):
            for s, part in enumerate((before_ref, self_ref, after_ref)):
                dst[s * BLOCK : (s + 1) * BLOCK] = part[kv]
            for s in range(SENT):
                at = (FIRST_SENT + s) * BLOCK
                dst[at : at + BLOCK] = g_ref[0, kv, :, s].reshape(BLOCK, HEAD_SIZE)
        kt[...] = kc[...].T
        live = [valid_ref[b * NB + s] > 0 for s in range(NB)]

        def heads(ref, p):
            return two_heads(ref, p)

        def pair(p, w):
            qp = heads(q_ref, p)
            op = heads(o_ref, p)
            st[w] = dot(kc[...], qp, 1, 1)
            dp[w] = dot(vc[...], op, 1, 1)
            top = jnp.full((1, 2 * BLOCK), -FAR, F32)
            for s in range(NB):
                here = jnp.max(st[w, s * BLOCK : (s + 1) * BLOCK], axis=0, keepdims=True)
                top = jnp.maximum(top, jnp.where(live[s], here, -FAR))
            top = top * EXP_SCALE
            total = jnp.zeros((1, 2 * BLOCK), F32)
            cross = jnp.zeros((1, 2 * BLOCK), F32)
            for s in range(NB):
                rows = slice(s * BLOCK, (s + 1) * BLOCK)
                shift = jnp.where(live[s], top, FAR)
                raised = jnp.exp2(st[w, rows] * EXP_SCALE - shift)
                st[w, rows] = raised
                total = total + col_sum(raised)
                cross = cross + col_sum(raised * dp[w, rows])
            inverse = 1.0 / total
            delta = cross * inverse
            for s in range(NB):
                rows = slice(s * BLOCK, (s + 1) * BLOCK)
                weights = st[w, rows] * inverse
                pb[w, rows] = weights.astype(BF16)
                ds[w, rows] = (weights * (dp[w, rows] - delta)).astype(BF16)
            new_dv = dot(pb[w], op, 1, 0)
            new_dk = dot(ds[w], qp, 1, 0)
            dv[...] = new_dv if p == 0 else dv[...] + new_dv
            dk[...] = new_dk if p == 0 else dk[...] + new_dk
            dqt = dot(kt[...], ds[w], 1, 0) * SCALING
            out = jnp.concatenate([dqt[:, :BLOCK].T, dqt[:, BLOCK:].T], axis=1).astype(BF16)
            dq_ref[:, pl.ds(2 * p * HEAD_SIZE, 2 * HEAD_SIZE)] = out

        def two_pairs(i, carry):
            for w in range(2):
                pair(2 * i + w, w)
            return carry

        for i in range(GROUP_SIZE // 4):
            two_pairs(i, 0)
        for kv, acc, factor in ((0, dk, SCALING), (1, dv, 1.0)):
            prev_ref[kv] = (acc[0:BLOCK] * factor).astype(BF16)
            own_ref[kv] = acc[BLOCK : 2 * BLOCK] * factor
            next_ref[kv] = (acc[2 * BLOCK : 3 * BLOCK] * factor).astype(BF16)
            for s in range(SENT):
                at = (FIRST_SENT + s) * BLOCK
                sent_ref[0, kv, :, s] = (
                    (acc[at : at + BLOCK] * factor).astype(BF16).reshape(GROUPS, PIECE, HEAD_SIZE)
                )


def sparse_grads(call, meta, valid, q, o, own, before, after, got, earlier=()):
    first = call * CALL_HEADS
    inside = first % HALF

    wide = pl.BlockSpec((BLOCK, GROUP_SIZE * HEAD_SIZE), lambda h, m, t: (0, first + h))
    pair = pl.BlockSpec((2, BLOCK, HEAD_SIZE), lambda h, m, t: (0, 0, first + h))
    pieces = pl.BlockSpec(
        (1, 2, GROUPS, SENT, PIECE, HEAD_SIZE), lambda h, m, t: (inside + h, 0, 0, 0, 0, 0)
    )
    keys = NB * BLOCK
    width = KEY_HEADS * HEAD_SIZE
    return pl.pallas_call(
        sparse_body,
        out_shape=(
            jax.ShapeDtypeStruct(q.shape, BF16),
            jax.ShapeDtypeStruct((2, BLOCK, width), F32),
            jax.ShapeDtypeStruct((2, BLOCK, width), BF16),
            jax.ShapeDtypeStruct((2, BLOCK, width), BF16),
            jax.ShapeDtypeStruct((HALF, 2, GROUPS, SENT, PIECE, HEAD_SIZE), BF16),
        ),
        grid_spec=pltpu.PrefetchScalarGridSpec(
            num_scalar_prefetch=2,
            grid=(CALL_HEADS,),
            in_specs=[wide, wide, pair, pair, pair, pieces]
            + [pl.BlockSpec(memory_space=pl.ANY)] * len(earlier),
            out_specs=[wide, pair, pair, pair, pieces],
            scratch_shapes=[
                VM((keys, HEAD_SIZE), BF16),
                VM((keys, HEAD_SIZE), BF16),
                VM((HEAD_SIZE, keys), BF16),
                VM((2, keys, 2 * BLOCK), F32),
                VM((2, keys, 2 * BLOCK), F32),
                VM((2, keys, 2 * BLOCK), BF16),
                VM((2, keys, 2 * BLOCK), BF16),
                VM((keys, HEAD_SIZE), F32),
                VM((keys, HEAD_SIZE), F32),
            ],
        ),
        input_output_aliases={8 + n: n for n in range(len(earlier))},
        name="sparse_grads",
    )(meta, valid, q, o, own, before, after, got, *earlier)


def load_held(meta_ref, held_ref, other_ref, kc, vc):
    core = meta_ref[1]
    mine = held_ref[:, core].reshape(kc.shape)
    other = other_ref[...].reshape(kc.shape)

    @pl.when(core == 0)
    def _():
        kc[...] = mine
        vc[...] = other

    @pl.when(core != 0)
    def _():
        kc[...] = other
        vc[...] = mine


def stats_body(meta_ref, q_ref, held_ref, other_ref, out_ref, kc, vc):
    load_held(meta_ref, held_ref, other_ref, kc, vc)

    def pair(p, carry):
        scores = dot(kc[...], dynamic_heads(q_ref.at[0], p), 1, 1)
        grads = dot(vc[...], dynamic_heads(q_ref.at[1], p), 1, 1)
        top = jnp.max(scores, axis=0, keepdims=True) * EXP_SCALE
        raised = jnp.exp2(scores * EXP_SCALE - top)
        for n, row in enumerate((top, col_sum(raised), col_sum(raised * grads))):
            for j in range(2):
                at = n * GROUP_SIZE + 2 * p + j
                out_ref[pl.ds(at, 1)] = row[:, j * BLOCK : (j + 1) * BLOCK]
        return carry

    lax.fori_loop(0, GROUP_SIZE // 2, pair, 0)


def dense_stats(meta, qo, held, other):
    keys = held.shape[0] * PIECE
    return pl.pallas_call(
        stats_body,
        out_shape=jax.ShapeDtypeStruct((3 * GROUP_SIZE, BLOCK), F32),
        in_specs=[pl.BlockSpec(memory_space=pltpu.SMEM)] + [pl.BlockSpec(memory_space=VM)] * 3,
        out_specs=pl.BlockSpec(memory_space=VM),
        scratch_shapes=[VM((keys, HEAD_SIZE), BF16), VM((keys, HEAD_SIZE), BF16)],
        name="dense_stats",
    )(meta, qo, held, other)


def merge_stats(parts):
    n = GROUP_SIZE
    top = functools.reduce(jnp.maximum, [x[:n] for x in parts])
    factors = [jnp.exp2(x[:n] - top) for x in parts]
    total = sum(x[n : 2 * n] * f for x, f in zip(parts, factors))
    cross = sum(x[2 * n :] * f for x, f in zip(parts, factors))
    return jnp.concatenate([top, total, cross], axis=0)


def dense_body(
    meta_ref, q_ref, held_ref, other_ref, s0, s1, s2, s3, dkv_ref, d0, d1, d2, d3,
    kc, vc, kt, stats,
):
    load_held(meta_ref, held_ref, other_ref, kc, vc)
    kt[...] = kc[...].T
    stats[...] = merge_stats([s0[...], s1[...], s2[...], s3[...]])
    core = meta_ref[1]

    dkv_ref[...] = jnp.zeros_like(dkv_ref)

    def pair(m, carry):
        p = lax.rem(meta_ref[2] + m, 4)

        def row(n):
            at = n * GROUP_SIZE + 2 * p
            return jnp.concatenate([stats[pl.ds(at, 1)], stats[pl.ds(at + 1, 1)]], axis=1)

        top = row(0)
        inverse = 1.0 / row(1)
        delta = row(2) * inverse
        qp = dynamic_heads(q_ref.at[0], p)
        op = dynamic_heads(q_ref.at[1], p)
        scores = dot(kc[...], qp, 1, 1)
        grads = dot(vc[...], op, 1, 1)
        weights = jnp.exp2(scores * EXP_SCALE - top) * inverse
        rounded = weights.astype(BF16)
        score_grad = (weights * (grads - delta)).astype(BF16)
        dkv_ref[core] += dot(score_grad, qp, 1, 0) * SCALING
        dkv_ref[1 - core] += dot(rounded, op, 1, 0)
        dqt = dot(kt[...], score_grad, 1, 0) * SCALING
        out = jnp.concatenate([dqt[:, :BLOCK].T, dqt[:, BLOCK:].T], axis=1).astype(BF16)
        for n, dq_ref in enumerate((d0, d1, d2, d3)):

            @pl.when(m == n)
            def _():
                dq_ref[...] = out

        return carry

    lax.fori_loop(0, 4, pair, 0)


def dense_grads(meta, qo, held, other, stats):
    keys = held.shape[0] * PIECE
    quarter = jax.ShapeDtypeStruct((BLOCK, 2 * HEAD_SIZE), BF16)
    return pl.pallas_call(
        dense_body,
        out_shape=(jax.ShapeDtypeStruct((2, keys, HEAD_SIZE), F32),) + (quarter,) * 4,
        in_specs=[pl.BlockSpec(memory_space=pltpu.SMEM)] + [pl.BlockSpec(memory_space=VM)] * 7,
        out_specs=[pl.BlockSpec(memory_space=VM)] * 5,
        scratch_shapes=[
            VM((keys, HEAD_SIZE), BF16),
            VM((keys, HEAD_SIZE), BF16),
            VM((HEAD_SIZE, keys), BF16),
            VM((3 * GROUP_SIZE, BLOCK), F32),
        ],
        name="dense_grads",
    )(meta, qo, held, other, *stats)


def combine_body(own_ref, prev_ref, next_ref, got_ref, dk_ref, dv_ref):
    for kv, out in ((0, dk_ref), (1, dv_ref)):
        for h in range(KEY_HEADS):
            cols = pl.ds(h * HEAD_SIZE, HEAD_SIZE)
            total = own_ref[kv, :, cols] + prev_ref[kv, :, cols].astype(F32)
            total = total + next_ref[kv, :, cols].astype(F32)
            pieces = got_ref[h % HALF, kv, :, h // HALF].reshape(BLOCK, HEAD_SIZE)
            out[:, cols] = (total + pieces.astype(F32)).astype(BF16)


def combine(own, from_prev, from_next, got):
    width = KEY_HEADS * HEAD_SIZE
    return pl.pallas_call(
        combine_body,
        out_shape=(jax.ShapeDtypeStruct((BLOCK, width), BF16),) * 2,
        in_specs=[pl.BlockSpec(memory_space=VM)] * 4,
        out_specs=[pl.BlockSpec(memory_space=VM)] * 2,
        name="combine",
    )(own, from_prev, from_next, got)


def spread_body(meta_ref, q_ref, o_ref, *rest):
    outs, stage, sems = rest[:-2], rest[-2], rest[-1]

    @pl.when(meta_ref[0] == 0)
    def _():
        loads, stores = [], []
        for h, out in enumerate(outs):
            cols = pl.ds(h * GROUP_SIZE * HEAD_SIZE, GROUP_SIZE * HEAD_SIZE)
            for j, ref in enumerate((q_ref, o_ref)):
                loads.append(
                    pltpu.make_async_copy(ref.at[:, cols], stage.at[h, j], sems.at[0, h, j])
                )
                stores.append(pltpu.make_async_copy(stage.at[h, j], out.at[j], sems.at[1, h, j]))
        for copy in loads:
            copy.start()
        for load, store in zip(loads, stores):
            load.wait()
            store.start()
        for copy in stores:
            copy.wait()


def spread_heads(meta, q, o):
    hbm = pl.BlockSpec(memory_space=pl.ANY)
    shape = (2, BLOCK, GROUP_SIZE * HEAD_SIZE)
    return pl.pallas_call(
        spread_body,
        out_shape=(jax.ShapeDtypeStruct(shape, BF16),) * KEY_HEADS,
        in_specs=[pl.BlockSpec(memory_space=pltpu.SMEM), hbm, hbm],
        out_specs=[hbm] * KEY_HEADS,
        scratch_shapes=[
            VM((KEY_HEADS,) + shape, BF16),
            pltpu.SemaphoreType.DMA((2, KEY_HEADS, 2)),
        ],
        name="spread_heads",
    )(meta, q, o)


def first_body(meta_ref, dq_ref, *rest):
    parts, out, stage, sems = rest[:KEY_HEADS], rest[KEY_HEADS], rest[-2], rest[-1]

    @pl.when(meta_ref[0] == 0)
    def _():
        loads, stores = [], []
        for h, part in enumerate(parts):
            cols = pl.ds(h * GROUP_SIZE * HEAD_SIZE, GROUP_SIZE * HEAD_SIZE)
            loads.append(pltpu.make_async_copy(part, stage.at[h], sems.at[0, h]))
            stores.append(pltpu.make_async_copy(stage.at[h], out.at[:, cols], sems.at[1, h]))
        for copy in loads:
            copy.start()
        for load, store in zip(loads, stores):
            load.wait()
            store.start()
        for copy in stores:
            copy.wait()


def put_first(meta, dq, parts):
    hbm = pl.BlockSpec(memory_space=pl.ANY)
    return pl.pallas_call(
        first_body,
        out_shape=jax.ShapeDtypeStruct(dq.shape, dq.dtype),
        in_specs=[pl.BlockSpec(memory_space=pltpu.SMEM)] + [hbm] * (KEY_HEADS + 1),
        out_specs=hbm,
        input_output_aliases={1: 0},
        scratch_shapes=[
            VM((KEY_HEADS, BLOCK, GROUP_SIZE * HEAD_SIZE), BF16),
            pltpu.SemaphoreType.DMA((2, KEY_HEADS)),
        ],
        name="put_first",
    )(meta, dq, *parts)


def tp_pairs(pairs, ctx_size, tp_size):
    return [(c * tp_size + a, c * tp_size + b) for c in range(ctx_size) for a, b in pairs]


def add(*xs):
    return sum(x.astype(F32) for x in xs).astype(BF16)


def per_device(queries, key_tensor, value_tensor, output_gradient, key_blocks, slot_valid):
    tp_size, ctx_size = lax.axis_size("tp"), lax.axis_size("ctx")
    blocks = ctx_size * tp_size
    b_index = lax.axis_index("ctx") * tp_size + lax.axis_index("tp")
    core = lax.axis_index("ctx") % 2
    meta = jnp.stack([b_index, core, lax.axis_index("tp") % 4]).astype(jnp.int32)
    table = key_blocks.reshape(-1)
    valid = slot_valid.reshape(-1)
    up = [(i, (i + 1) % blocks) for i in range(blocks)]
    down = [(i, (i - 1) % blocks) for i in range(blocks)]
    partner = [(i, (i // tp_size ^ 1) * tp_size + i % tp_size) for i in range(blocks)]
    four = range(4)

    def swap(x):
        return lax.all_to_all(x, BOTH, split_axis=0, concat_axis=0, tiled=True)

    def send(x, pairs):
        return lax.ppermute(x, BOTH, pairs)

    def send_tp(x, pairs):
        return send(x, tp_pairs(pairs, ctx_size, tp_size))

    def along_x(n):
        return [(4 * z + x, 4 * z + (x + n) % 4) for z in four for x in four]

    def along_z(n):
        return [(4 * z + x, 4 * ((z + n) % 4) + x) for z in four for x in four]

    pieces, both = pack_pieces(key_tensor, value_tensor)
    held = swap(pieces.reshape(blocks, CHUNKS, PIECE, HEAD_SIZE))
    before, after = send(both, up), send(both, down)
    slices = spread_heads(meta, queries, output_gradient)
    qo = jnp.where(b_index == 0, slices[0], jnp.zeros_like(slices[0]))
    for c in (4, 2, 6, 3, 5, 7, 1):
        moved = send(slices[c // 2 + HALF * (c % 2)], [(0, c * tp_size)])
        qo = qo + moved

    listed = []
    for j in range(CHUNKS):
        listed.append(gather_pieces(table, held, blocks, j))
    given = give_pieces(meta, held)
    given = send(given, partner)
    shape = (HALF, 2, GROUPS, SENT, PIECE, HEAD_SIZE)
    got = []
    for j in range(CHUNKS):
        got.append(swap(listed[j]).reshape(shape))

    moved = send_tp(qo, [(0, 1)])
    qo = qo + moved
    moved = send_tp(qo, [(0, 3), (1, 2)])
    qo = qo + moved
    moved = send_tp(qo, [(x, 4 + x) for x in four])
    qo = qo + moved
    moved = send_tp(qo, [(x, 12 + x) for x in four] + [(4 + x, 8 + x) for x in four])
    qo = qo + moved

    grads, back = (), []
    calls = HALF // CALL_HEADS
    for j in range(CHUNKS):
        for n in range(calls):
            call = calls * j + n
            grads = sparse_grads(
                call, meta, valid, queries, output_gradient, both, before, after, got[j],
                grads if n > 0 else grads[:4],
            )
        back.append(swap(grads[4].reshape(blocks, SENT, PIECE, HEAD_SIZE)))
    dq, own, to_prev, to_next = grads[:4]
    from_next, from_prev = send(to_prev, down), send(to_next, up)

    stats = dense_stats(meta, qo, held, given)
    others = [send_tp(stats, along_x(n)) for n in range(1, 4)]
    stats = merge_stats([stats] + others)
    others = [send_tp(stats, along_z(n)) for n in range(1, 4)]
    dense, *part = dense_grads(meta, qo, held, given, [stats] + others)
    dense_other = send(dense[1], partner)
    others = [send_tp(part[n], along_x(n)) for n in range(1, 4)]
    total = add(part[0], *others)
    others = [send_tp(total, [(4 * n + x, x) for x in four]) for n in range(1, 4)]
    total = add(total, *others)
    others = [send_tp(total, [(n, 0)]) for n in range(1, 4)]
    total = jnp.concatenate([total] + others, axis=1)
    parts = [total] * KEY_HEADS
    for c in range(1, ctx_size):
        parts[c // 2 + HALF * (c % 2)] = send(total, [(c * tp_size, 0)])
    d_q = put_first(meta, dq, parts)

    first = scatter_pieces(table, back[0], blocks)
    summed = scatter_last(table, meta, back[1], first, dense, dense_other, blocks)
    home = swap(summed).reshape(HALF, 2, GROUPS, CHUNKS, PIECE, HEAD_SIZE)
    d_k, d_v = combine(own, from_prev, from_next, home)
    return d_q, d_k, d_v


def solution(mesh):
    spec = P(BOTH, None)

    return jax.shard_map(
        per_device,
        mesh=mesh,
        in_specs=(spec, spec, spec, spec, P(), P()),
        out_specs=(spec, spec, spec),
        check_vma=False,
    )
```

```python
import functools
import math

import jax
import jax.numpy as jnp
from jax import lax
from jax.experimental import pallas as pl
from jax.experimental.pallas import tpu as pltpu
from jax.sharding import PartitionSpec as P


KEY_HEADS = 8
GROUP_SIZE = 8
HEAD_SIZE = 128
BLOCK = 128
NB = 8
GROUPS = 16
PIECE = 8
SENT = 5
FIRST_SENT = NB - SENT
CHUNKS = 2
HALF = KEY_HEADS // CHUNKS
CALL_HEADS = 4
BOTH = ("ctx", "tp")
SCALING = 1.0 / math.sqrt(HEAD_SIZE)
EXP_SCALE = SCALING * math.log2(math.e)
FAR = 1e30
F32 = jnp.float32
BF16 = jnp.bfloat16
VM = pltpu.VMEM


def dot(a, b, ca, cb):
    return lax.dot_general(a, b, (((ca,), (cb,)), ((), ())), preferred_element_type=F32)


def pack_body(k_ref, v_ref, out_ref, both_ref):
    for kv, ref in enumerate((k_ref, v_ref)):
        both_ref[kv] = ref[...]
        for j in range(CHUNKS):
            for y in range(HALF):
                cols = pl.ds((j * HALF + y) * HEAD_SIZE, HEAD_SIZE)
                out_ref[y, kv, :, j] = ref[:, cols].reshape(GROUPS, PIECE, HEAD_SIZE)


def pack_pieces(k, v):
    return pl.pallas_call(
        pack_body,
        out_shape=(
            jax.ShapeDtypeStruct((HALF, 2, GROUPS, CHUNKS, PIECE, HEAD_SIZE), BF16),
            jax.ShapeDtypeStruct((2,) + k.shape, BF16),
        ),
        in_specs=[pl.BlockSpec(memory_space=VM)] * 2,
        out_specs=[pl.BlockSpec(memory_space=VM)] * 2,
        name="pack_pieces",
    )(k, v)


def gather_body(table_ref, held_ref, out_ref, *, rows, chunk):
    base = pl.program_id(0) * rows

    def one(d, carry):
        for s in range(SENT):
            block = table_ref[(base + d) * NB + FIRST_SENT + s]
            out_ref[d, s] = held_ref[block, chunk]
        return carry

    lax.fori_loop(0, rows, one, 0, unroll=8)


def gather_pieces(table, held, blocks, chunk):
    steps = 2
    rows = blocks // steps
    return pl.pallas_call(
        functools.partial(gather_body, rows=rows, chunk=chunk),
        out_shape=jax.ShapeDtypeStruct((blocks, SENT, PIECE, HEAD_SIZE), BF16),
        grid_spec=pltpu.PrefetchScalarGridSpec(
            num_scalar_prefetch=1,
            grid=(steps,),
            in_specs=[
                pl.BlockSpec((blocks, CHUNKS, PIECE, HEAD_SIZE), lambda i, t: (0, 0, 0, 0))
            ],
            out_specs=pl.BlockSpec((rows, SENT, PIECE, HEAD_SIZE), lambda i, t: (i, 0, 0, 0)),
        ),
        name="gather_pieces",
    )(table, held)


def give_body(meta_ref, held_ref, out_ref):
    out_ref[...] = held_ref[:, 1 - meta_ref[1]]


def give_pieces(meta, held):
    return pl.pallas_call(
        give_body,
        out_shape=jax.ShapeDtypeStruct(held.shape[:1] + held.shape[2:], BF16),
        in_specs=[pl.BlockSpec(memory_space=pltpu.SMEM), pl.BlockSpec(memory_space=VM)],
        out_specs=pl.BlockSpec(memory_space=VM),
        name="give_pieces",
    )(meta, held)


def add_listed(table_ref, got_ref, accs, rows):
    base = pl.program_id(0) * rows

    @pl.when(pl.program_id(0) == 0)
    def _():
        for acc in accs:
            acc[...] = jnp.zeros_like(acc)

    def one(d, total):
        for s in range(1, SENT):
            block = table_ref[(base + d) * NB + FIRST_SENT + s]
            accs[s][block] += got_ref[d, s].astype(F32)
        return total + got_ref[d, 0].astype(F32)

    zero = jnp.zeros((PIECE, HEAD_SIZE), F32)
    accs[0][...] += lax.fori_loop(0, rows, one, zero, unroll=8)


def listed_total(accs):
    accs[1][0] += accs[0][...]
    return (accs[1][...] + accs[2][...]) + (accs[3][...] + accs[4][...])


def scatter_body(table_ref, got_ref, out_ref, *accs, rows):
    add_listed(table_ref, got_ref, accs, rows)

    @pl.when(pl.program_id(0) == pl.num_programs(0) - 1)
    def _():
        out_ref[...] = listed_total(accs)


def scatter_last_body(
    table_ref, meta_ref, got_ref, first_ref, dense_ref, other_ref, out_ref, *accs, rows
):
    add_listed(table_ref, got_ref, accs, rows)

    @pl.when(pl.program_id(0) == pl.num_programs(0) - 1)
    def _():
        core = meta_ref[1]
        second = listed_total(accs)
        mine = dense_ref[0].reshape(second.shape)
        other = other_ref[...].reshape(second.shape)
        out_ref[:, core] = (jnp.where(core == 0, first_ref[...], second) + mine).astype(BF16)
        out_ref[:, 1 - core] = (jnp.where(core == 0, second, first_ref[...]) + other).astype(BF16)


def slot_sums(blocks):
    whole = VM((blocks, PIECE, HEAD_SIZE), F32)
    return [VM((PIECE, HEAD_SIZE), F32)] + [whole] * (SENT - 1)


def scatter_pieces(table, got, blocks):
    steps = 2
    rows = blocks // steps
    return pl.pallas_call(
        functools.partial(scatter_body, rows=rows),
        out_shape=jax.ShapeDtypeStruct((blocks, PIECE, HEAD_SIZE), F32),
        grid_spec=pltpu.PrefetchScalarGridSpec(
            num_scalar_prefetch=1,
            grid=(steps,),
            in_specs=[pl.BlockSpec((rows, SENT, PIECE, HEAD_SIZE), lambda i, t: (i, 0, 0, 0))],
            out_specs=pl.BlockSpec((blocks, PIECE, HEAD_SIZE), lambda i, t: (0, 0, 0)),
            scratch_shapes=slot_sums(blocks),
        ),
        name="scatter_pieces",
    )(table, got)


def scatter_last(table, meta, got, first, dense, other, blocks):
    steps = 2
    rows = blocks // steps
    whole = pl.BlockSpec((blocks, PIECE, HEAD_SIZE), lambda i, t, m: (0, 0, 0))
    return pl.pallas_call(
        functools.partial(scatter_last_body, rows=rows),
        out_shape=jax.ShapeDtypeStruct((blocks, CHUNKS, PIECE, HEAD_SIZE), BF16),
        grid_spec=pltpu.PrefetchScalarGridSpec(
            num_scalar_prefetch=2,
            grid=(steps,),
            in_specs=[
                pl.BlockSpec((rows, SENT, PIECE, HEAD_SIZE), lambda i, t, m: (i, 0, 0, 0)),
                whole,
                pl.BlockSpec((1, blocks * PIECE, HEAD_SIZE), lambda i, t, m: (0, 0, 0)),
                pl.BlockSpec((blocks * PIECE, HEAD_SIZE), lambda i, t, m: (0, 0)),
            ],
            out_specs=pl.BlockSpec(
                (blocks, CHUNKS, PIECE, HEAD_SIZE), lambda i, t, m: (0, 0, 0, 0)
            ),
            scratch_shapes=slot_sums(blocks),
        ),
        name="scatter_last",
    )(table, meta, got, first, dense, other)


def two_heads(ref, p):
    first = ref[:, pl.ds(2 * p * HEAD_SIZE, HEAD_SIZE)]
    second = ref[:, pl.ds((2 * p + 1) * HEAD_SIZE, HEAD_SIZE)]
    return jnp.concatenate([first, second], axis=0)


def col_sum(x):
    return jnp.sum(x, axis=0, keepdims=True)


def sparse_body(
    meta_ref, valid_ref, q_ref, o_ref, self_ref, before_ref, after_ref, g_ref, *rest
):
    dq_ref, own_ref, prev_ref, next_ref, sent_ref = rest[-14:-9]
    kc, vc, kt, st, dp, pb, ds, dk, dv = rest[-9:]
    b = meta_ref[0]

    @pl.when(b == 0)
    def _():
        dq_ref[...] = jnp.zeros_like(dq_ref)
        own_ref[...] = jnp.zeros_like(own_ref)
        prev_ref[...] = jnp.zeros_like(prev_ref)
        next_ref[...] = jnp.zeros_like(next_ref)
        sent_ref[...] = jnp.zeros_like(sent_ref)

    @pl.when(b != 0)
    def _():
        for kv, dst in ((0, kc), (1, vc)):
            for s, part in enumerate((before_ref, self_ref, after_ref)):
                dst[s * BLOCK : (s + 1) * BLOCK] = part[kv]
            for s in range(SENT):
                at = (FIRST_SENT + s) * BLOCK
                dst[at : at + BLOCK] = g_ref[0, kv, :, s].reshape(BLOCK, HEAD_SIZE)
        kt[...] = kc[...].T
        live = [valid_ref[b * NB + s] > 0 for s in range(NB)]

        def heads(ref, p):
            return two_heads(ref, p)

        def pair(p, w):
            qp = heads(q_ref, p)
            op = heads(o_ref, p)
            st[w] = dot(kc[...], qp, 1, 1)
            dp[w] = dot(vc[...], op, 1, 1)
            top = jnp.full((1, 2 * BLOCK), -FAR, F32)
            for s in range(NB):
                here = jnp.max(st[w, s * BLOCK : (s + 1) * BLOCK], axis=0, keepdims=True)
                top = jnp.maximum(top, jnp.where(live[s], here, -FAR))
            top = top * EXP_SCALE
            total = jnp.zeros((1, 2 * BLOCK), F32)
            cross = jnp.zeros((1, 2 * BLOCK), F32)
            for s in range(NB):
                rows = slice(s * BLOCK, (s + 1) * BLOCK)
                shift = jnp.where(live[s], top, FAR)
                raised = jnp.exp2(st[w, rows] * EXP_SCALE - shift)
                st[w, rows] = raised
                total = total + col_sum(raised)
                cross = cross + col_sum(raised * dp[w, rows])
            inverse = 1.0 / total
            delta = cross * inverse
            for s in range(NB):
                rows = slice(s * BLOCK, (s + 1) * BLOCK)
                weights = st[w, rows] * inverse
                pb[w, rows] = weights.astype(BF16)
                ds[w, rows] = (weights * (dp[w, rows] - delta)).astype(BF16)
            new_dv = dot(pb[w], op, 1, 0)
            new_dk = dot(ds[w], qp, 1, 0)
            dv[...] = new_dv if p == 0 else dv[...] + new_dv
            dk[...] = new_dk if p == 0 else dk[...] + new_dk
            dqt = dot(kt[...], ds[w], 1, 0) * SCALING
            out = jnp.concatenate([dqt[:, :BLOCK].T, dqt[:, BLOCK:].T], axis=1).astype(BF16)
            dq_ref[:, pl.ds(2 * p * HEAD_SIZE, 2 * HEAD_SIZE)] = out

        def two_pairs(i, carry):
            for w in range(2):
                pair(2 * i + w, w)
            return carry

        for i in range(GROUP_SIZE // 4):
            two_pairs(i, 0)
        for kv, acc, factor in ((0, dk, SCALING), (1, dv, 1.0)):
            prev_ref[kv] = (acc[0:BLOCK] * factor).astype(BF16)
            own_ref[kv] = acc[BLOCK : 2 * BLOCK] * factor
            next_ref[kv] = (acc[2 * BLOCK : 3 * BLOCK] * factor).astype(BF16)
            for s in range(SENT):
                at = (FIRST_SENT + s) * BLOCK
                sent_ref[0, kv, :, s] = (
                    (acc[at : at + BLOCK] * factor).astype(BF16).reshape(GROUPS, PIECE, HEAD_SIZE)
                )


def sparse_grads(call, meta, valid, q, o, own, before, after, got, earlier=()):
    first = call * CALL_HEADS
    inside = first % HALF

    wide = pl.BlockSpec((BLOCK, GROUP_SIZE * HEAD_SIZE), lambda h, m, t: (0, first + h))
    pair = pl.BlockSpec((2, BLOCK, HEAD_SIZE), lambda h, m, t: (0, 0, first + h))
    pieces = pl.BlockSpec(
        (1, 2, GROUPS, SENT, PIECE, HEAD_SIZE), lambda h, m, t: (inside + h, 0, 0, 0, 0, 0)
    )
    keys = NB * BLOCK
    width = KEY_HEADS * HEAD_SIZE
    return pl.pallas_call(
        sparse_body,
        out_shape=(
            jax.ShapeDtypeStruct(q.shape, BF16),
            jax.ShapeDtypeStruct((2, BLOCK, width), F32),
            jax.ShapeDtypeStruct((2, BLOCK, width), BF16),
            jax.ShapeDtypeStruct((2, BLOCK, width), BF16),
            jax.ShapeDtypeStruct((HALF, 2, GROUPS, SENT, PIECE, HEAD_SIZE), BF16),
        ),
        grid_spec=pltpu.PrefetchScalarGridSpec(
            num_scalar_prefetch=2,
            grid=(CALL_HEADS,),
            in_specs=[wide, wide, pair, pair, pair, pieces]
            + [pl.BlockSpec(memory_space=pl.ANY)] * len(earlier),
            out_specs=[wide, pair, pair, pair, pieces],
            scratch_shapes=[
                VM((keys, HEAD_SIZE), BF16),
                VM((keys, HEAD_SIZE), BF16),
                VM((HEAD_SIZE, keys), BF16),
                VM((2, keys, 2 * BLOCK), F32),
                VM((2, keys, 2 * BLOCK), F32),
                VM((2, keys, 2 * BLOCK), BF16),
                VM((2, keys, 2 * BLOCK), BF16),
                VM((keys, HEAD_SIZE), F32),
                VM((keys, HEAD_SIZE), F32),
            ],
        ),
        input_output_aliases={8 + n: n for n in range(len(earlier))},
        name="sparse_grads",
    )(meta, valid, q, o, own, before, after, got, *earlier)


def load_held(meta_ref, held_ref, other_ref, kc, vc):
    core = meta_ref[1]
    mine = held_ref[:, core].reshape(kc.shape)
    other = other_ref[...].reshape(kc.shape)

    @pl.when(core == 0)
    def _():
        kc[...] = mine
        vc[...] = other

    @pl.when(core != 0)
    def _():
        kc[...] = other
        vc[...] = mine


def stats_body(meta_ref, q_ref, held_ref, other_ref, out_ref, kc, vc):
    load_held(meta_ref, held_ref, other_ref, kc, vc)
    for p in range(GROUP_SIZE // 2):
        scores = dot(kc[...], two_heads(q_ref.at[0], p), 1, 1)
        grads = dot(vc[...], two_heads(q_ref.at[1], p), 1, 1)
        top = jnp.max(scores, axis=0, keepdims=True) * EXP_SCALE
        raised = jnp.exp2(scores * EXP_SCALE - top)
        for n, row in enumerate((top, col_sum(raised), col_sum(raised * grads))):
            for j in range(2):
                at = n * GROUP_SIZE + 2 * p + j
                out_ref[at : at + 1] = row[:, j * BLOCK : (j + 1) * BLOCK]


def dense_stats(meta, qo, held, other):
    keys = held.shape[0] * PIECE
    return pl.pallas_call(
        stats_body,
        out_shape=jax.ShapeDtypeStruct((3 * GROUP_SIZE, BLOCK), F32),
        in_specs=[pl.BlockSpec(memory_space=pltpu.SMEM)] + [pl.BlockSpec(memory_space=VM)] * 3,
        out_specs=pl.BlockSpec(memory_space=VM),
        scratch_shapes=[VM((keys, HEAD_SIZE), BF16), VM((keys, HEAD_SIZE), BF16)],
        name="dense_stats",
    )(meta, qo, held, other)


def merge_stats(parts):
    n = GROUP_SIZE
    top = functools.reduce(jnp.maximum, [x[:n] for x in parts])
    factors = [jnp.exp2(x[:n] - top) for x in parts]
    total = sum(x[n : 2 * n] * f for x, f in zip(parts, factors))
    cross = sum(x[2 * n :] * f for x, f in zip(parts, factors))
    return jnp.concatenate([top, total, cross], axis=0)


def dense_body(
    meta_ref, q_ref, held_ref, other_ref, s0, s1, s2, s3, dkv_ref, dq_ref, kc, vc, kt, stats
):
    load_held(meta_ref, held_ref, other_ref, kc, vc)
    kt[...] = kc[...].T
    stats[...] = merge_stats([s0[...], s1[...], s2[...], s3[...]])
    core = meta_ref[1]

    def row(n, p):
        at = n * GROUP_SIZE + 2 * p
        return jnp.concatenate([stats[at : at + 1], stats[at + 1 : at + 2]], axis=1)

    for p in range(GROUP_SIZE // 2):
        top = row(0, p)
        inverse = 1.0 / row(1, p)
        delta = row(2, p) * inverse
        qp = two_heads(q_ref.at[0], p)
        op = two_heads(q_ref.at[1], p)
        scores = dot(kc[...], qp, 1, 1)
        grads = dot(vc[...], op, 1, 1)
        weights = jnp.exp2(scores * EXP_SCALE - top) * inverse
        rounded = weights.astype(BF16)
        score_grad = (weights * (grads - delta)).astype(BF16)
        new_dk = dot(score_grad, qp, 1, 0) * SCALING
        new_dv = dot(rounded, op, 1, 0)
        dkv_ref[core] = new_dk if p == 0 else dkv_ref[core] + new_dk
        dkv_ref[1 - core] = new_dv if p == 0 else dkv_ref[1 - core] + new_dv
        dqt = dot(kt[...], score_grad, 1, 0) * SCALING
        for j in range(2):
            dq_ref[:, pl.ds((2 * p + j) * HEAD_SIZE, HEAD_SIZE)] = (
                dqt[:, j * BLOCK : (j + 1) * BLOCK].T.astype(BF16)
            )


def dense_grads(meta, qo, held, other, stats):
    keys = held.shape[0] * PIECE
    return pl.pallas_call(
        dense_body,
        out_shape=(
            jax.ShapeDtypeStruct((2, keys, HEAD_SIZE), F32),
            jax.ShapeDtypeStruct((BLOCK, GROUP_SIZE * HEAD_SIZE), BF16),
        ),
        in_specs=[pl.BlockSpec(memory_space=pltpu.SMEM)] + [pl.BlockSpec(memory_space=VM)] * 7,
        out_specs=[pl.BlockSpec(memory_space=VM)] * 2,
        scratch_shapes=[
            VM((keys, HEAD_SIZE), BF16),
            VM((keys, HEAD_SIZE), BF16),
            VM((HEAD_SIZE, keys), BF16),
            VM((3 * GROUP_SIZE, BLOCK), F32),
        ],
        name="dense_grads",
    )(meta, qo, held, other, *stats)


def combine_body(own_ref, prev_ref, next_ref, got_ref, dk_ref, dv_ref):
    for kv, out in ((0, dk_ref), (1, dv_ref)):
        for h in range(KEY_HEADS):
            cols = pl.ds(h * HEAD_SIZE, HEAD_SIZE)
            total = own_ref[kv, :, cols] + prev_ref[kv, :, cols].astype(F32)
            total = total + next_ref[kv, :, cols].astype(F32)
            pieces = got_ref[h % HALF, kv, :, h // HALF].reshape(BLOCK, HEAD_SIZE)
            out[:, cols] = (total + pieces.astype(F32)).astype(BF16)


def combine(own, from_prev, from_next, got):
    width = KEY_HEADS * HEAD_SIZE
    return pl.pallas_call(
        combine_body,
        out_shape=(jax.ShapeDtypeStruct((BLOCK, width), BF16),) * 2,
        in_specs=[pl.BlockSpec(memory_space=VM)] * 4,
        out_specs=[pl.BlockSpec(memory_space=VM)] * 2,
        name="combine",
    )(own, from_prev, from_next, got)


def spread_body(meta_ref, q_ref, o_ref, *rest):
    outs, stage, sems = rest[:-2], rest[-2], rest[-1]

    @pl.when(meta_ref[0] == 0)
    def _():
        loads, stores = [], []
        for h, out in enumerate(outs):
            cols = pl.ds(h * GROUP_SIZE * HEAD_SIZE, GROUP_SIZE * HEAD_SIZE)
            for j, ref in enumerate((q_ref, o_ref)):
                loads.append(
                    pltpu.make_async_copy(ref.at[:, cols], stage.at[h, j], sems.at[0, h, j])
                )
                stores.append(pltpu.make_async_copy(stage.at[h, j], out.at[j], sems.at[1, h, j]))
        for copy in loads:
            copy.start()
        for load, store in zip(loads, stores):
            load.wait()
            store.start()
        for copy in stores:
            copy.wait()


def spread_heads(meta, q, o):
    hbm = pl.BlockSpec(memory_space=pl.ANY)
    shape = (2, BLOCK, GROUP_SIZE * HEAD_SIZE)
    return pl.pallas_call(
        spread_body,
        out_shape=(jax.ShapeDtypeStruct(shape, BF16),) * KEY_HEADS,
        in_specs=[pl.BlockSpec(memory_space=pltpu.SMEM), hbm, hbm],
        out_specs=[hbm] * KEY_HEADS,
        scratch_shapes=[
            VM((KEY_HEADS,) + shape, BF16),
            pltpu.SemaphoreType.DMA((2, KEY_HEADS, 2)),
        ],
        name="spread_heads",
    )(meta, q, o)


def first_body(meta_ref, dq_ref, *rest):
    parts, out, stage, sems = rest[:KEY_HEADS], rest[KEY_HEADS], rest[-2], rest[-1]

    @pl.when(meta_ref[0] == 0)
    def _():
        loads, stores = [], []
        for h, part in enumerate(parts):
            cols = pl.ds(h * GROUP_SIZE * HEAD_SIZE, GROUP_SIZE * HEAD_SIZE)
            loads.append(pltpu.make_async_copy(part, stage.at[h], sems.at[0, h]))
            stores.append(pltpu.make_async_copy(stage.at[h], out.at[:, cols], sems.at[1, h]))
        for copy in loads:
            copy.start()
        for load, store in zip(loads, stores):
            load.wait()
            store.start()
        for copy in stores:
            copy.wait()


def put_first(meta, dq, parts):
    hbm = pl.BlockSpec(memory_space=pl.ANY)
    return pl.pallas_call(
        first_body,
        out_shape=jax.ShapeDtypeStruct(dq.shape, dq.dtype),
        in_specs=[pl.BlockSpec(memory_space=pltpu.SMEM)] + [hbm] * (KEY_HEADS + 1),
        out_specs=hbm,
        input_output_aliases={1: 0},
        scratch_shapes=[
            VM((KEY_HEADS, BLOCK, GROUP_SIZE * HEAD_SIZE), BF16),
            pltpu.SemaphoreType.DMA((2, KEY_HEADS)),
        ],
        name="put_first",
    )(meta, dq, *parts)


def pick_body(meta_ref, *rest, at):
    parts, out_ref, sem = rest[:-2], rest[-2], rest[-1]
    for n, part in enumerate(parts):

        @pl.when(meta_ref[at] == n)
        def _():
            copy = pltpu.make_async_copy(part, out_ref, sem)
            copy.start()
            copy.wait()


def pick(meta, at, parts):
    return pl.pallas_call(
        functools.partial(pick_body, at=at),
        out_shape=jax.ShapeDtypeStruct(parts[0].shape, parts[0].dtype),
        in_specs=[pl.BlockSpec(memory_space=pltpu.SMEM)]
        + [pl.BlockSpec(memory_space=pl.ANY)] * len(parts),
        out_specs=pl.BlockSpec(memory_space=VM),
        scratch_shapes=[pltpu.SemaphoreType.DMA(())],
        name="pick",
    )(meta, *parts)


def tp_pairs(pairs, ctx_size, tp_size):
    return [(c * tp_size + a, c * tp_size + b) for c in range(ctx_size) for a, b in pairs]


def add(*xs):
    return sum(x.astype(F32) for x in xs).astype(BF16)


def per_device(queries, key_tensor, value_tensor, output_gradient, key_blocks, slot_valid):
    tp_size, ctx_size = lax.axis_size("tp"), lax.axis_size("ctx")
    blocks = ctx_size * tp_size
    b_index = lax.axis_index("ctx") * tp_size + lax.axis_index("tp")
    core = lax.axis_index("ctx") % 2
    t_index = lax.axis_index("tp")
    meta = jnp.stack([b_index, core, t_index % 4, t_index // 4, lax.axis_index("ctx")])
    meta = meta.astype(jnp.int32)
    table = key_blocks.reshape(-1)
    valid = slot_valid.reshape(-1)
    up = [(i, (i + 1) % blocks) for i in range(blocks)]
    down = [(i, (i - 1) % blocks) for i in range(blocks)]
    partner = [(i, (i // tp_size ^ 1) * tp_size + i % tp_size) for i in range(blocks)]
    four = range(4)

    def swap(x):
        return lax.all_to_all(x, BOTH, split_axis=0, concat_axis=0, tiled=True)

    def send(x, pairs):
        return lax.ppermute(x, BOTH, pairs)

    def send_tp(x, pairs):
        return send(x, tp_pairs(pairs, ctx_size, tp_size))

    def along_x(n):
        return [(4 * z + x, 4 * z + (x + n) % 4) for z in four for x in four]

    def along_z(n):
        return [(4 * z + x, 4 * ((z + n) % 4) + x) for z in four for x in four]

    pieces, both = pack_pieces(key_tensor, value_tensor)
    held = swap(pieces.reshape(blocks, CHUNKS, PIECE, HEAD_SIZE))
    before, after = send(both, up), send(both, down)
    slices = spread_heads(meta, queries, output_gradient)
    moved = [slices[0]] * ctx_size
    for c in (4, 2, 6, 3, 5, 7, 1):
        moved[c] = send(slices[c // 2 + HALF * (c % 2)], [(0, c * tp_size)])

    listed = []
    for j in range(CHUNKS):
        listed.append(gather_pieces(table, held, blocks, j))
    given = give_pieces(meta, held)
    given = send(given, partner)
    shape = (HALF, 2, GROUPS, SENT, PIECE, HEAD_SIZE)
    got = []
    for j in range(CHUNKS):
        got.append(swap(listed[j]).reshape(shape))

    qo = pick(meta, 4, moved)
    moved = [qo] + [send_tp(qo, [(0, n)]) for n in range(1, 4)]
    qo = pick(meta, 2, moved)
    moved = [qo] + [send_tp(qo, [(x, 4 * n + x) for x in four]) for n in range(1, 4)]
    qo = pick(meta, 3, moved)

    grads, back = (), []
    calls = HALF // CALL_HEADS
    for j in range(CHUNKS):
        for n in range(calls):
            call = calls * j + n
            grads = sparse_grads(
                call, meta, valid, queries, output_gradient, both, before, after, got[j],
                grads if n > 0 else grads[:4],
            )
        back.append(swap(grads[4].reshape(blocks, SENT, PIECE, HEAD_SIZE)))
    dq, own, to_prev, to_next = grads[:4]
    from_next, from_prev = send(to_prev, down), send(to_next, up)

    stats = dense_stats(meta, qo, held, given)
    others = [send_tp(stats, along_x(n)) for n in range(1, 4)]
    stats = merge_stats([stats] + others)
    others = [send_tp(stats, along_z(n)) for n in range(1, 4)]
    dense, part = dense_grads(meta, qo, held, given, [stats] + others)
    dense_other = send(dense[1], partner)
    others = [send_tp(part, [(4 * n + x, x) for x in four]) for n in range(1, 4)]
    total = add(part, *others)
    others = [send_tp(total, [(n, 0)]) for n in range(1, 4)]
    total = add(total, *others)
    parts = [total] * KEY_HEADS
    for c in range(1, ctx_size):
        parts[c // 2 + HALF * (c % 2)] = send(total, [(c * tp_size, 0)])
    d_q = put_first(meta, dq, parts)

    first = scatter_pieces(table, back[0], blocks)
    summed = scatter_last(table, meta, back[1], first, dense, dense_other, blocks)
    home = swap(summed).reshape(HALF, 2, GROUPS, CHUNKS, PIECE, HEAD_SIZE)
    d_k, d_v = combine(own, from_prev, from_next, home)
    return d_q, d_k, d_v


def solution(mesh):
    spec = P(BOTH, None)

    return jax.shard_map(
        per_device,
        mesh=mesh,
        in_specs=(spec, spec, spec, spec, P(), P()),
        out_specs=(spec, spec, spec),
        check_vma=False,
    )
```

```python
import functools
import math

import jax
import jax.numpy as jnp
from jax import lax
from jax.experimental import pallas as pl
from jax.experimental.pallas import tpu as pltpu
from jax.sharding import PartitionSpec as P


KEY_HEADS = 8
GROUP_SIZE = 8
HEAD_SIZE = 128
BLOCK = 128
NB = 8
GROUPS = 16
PIECE = 8
SENT = 5
FIRST_SENT = NB - SENT
CHUNKS = 2
HALF = KEY_HEADS // CHUNKS
CALL_HEADS = 4
BOTH = ("ctx", "tp")
SCALING = 1.0 / math.sqrt(HEAD_SIZE)
EXP_SCALE = SCALING * math.log2(math.e)
FAR = 1e30
F32 = jnp.float32
BF16 = jnp.bfloat16
VM = pltpu.VMEM


def dot(a, b, ca, cb):
    return lax.dot_general(a, b, (((ca,), (cb,)), ((), ())), preferred_element_type=F32)


def pack_body(k_ref, v_ref, out_ref, both_ref):
    for kv, ref in enumerate((k_ref, v_ref)):
        both_ref[kv] = ref[...]
        for j in range(CHUNKS):
            for y in range(HALF):
                cols = pl.ds((j * HALF + y) * HEAD_SIZE, HEAD_SIZE)
                out_ref[y, kv, :, j] = ref[:, cols].reshape(GROUPS, PIECE, HEAD_SIZE)


def pack_pieces(k, v):
    return pl.pallas_call(
        pack_body,
        out_shape=(
            jax.ShapeDtypeStruct((HALF, 2, GROUPS, CHUNKS, PIECE, HEAD_SIZE), BF16),
            jax.ShapeDtypeStruct((2,) + k.shape, BF16),
        ),
        in_specs=[pl.BlockSpec(memory_space=VM)] * 2,
        out_specs=[pl.BlockSpec(memory_space=VM)] * 2,
        name="pack_pieces",
    )(k, v)


def gather_body(table_ref, held_ref, out_ref, *, rows, chunk):
    base = pl.program_id(0) * rows

    def one(d, carry):
        for s in range(SENT):
            block = table_ref[(base + d) * NB + FIRST_SENT + s]
            out_ref[d, s] = held_ref[block, chunk]
        return carry

    lax.fori_loop(0, rows, one, 0, unroll=8)


def gather_pieces(table, held, blocks, chunk):
    steps = 2
    rows = blocks // steps
    return pl.pallas_call(
        functools.partial(gather_body, rows=rows, chunk=chunk),
        out_shape=jax.ShapeDtypeStruct((blocks, SENT, PIECE, HEAD_SIZE), BF16),
        grid_spec=pltpu.PrefetchScalarGridSpec(
            num_scalar_prefetch=1,
            grid=(steps,),
            in_specs=[
                pl.BlockSpec((blocks, CHUNKS, PIECE, HEAD_SIZE), lambda i, t: (0, 0, 0, 0))
            ],
            out_specs=pl.BlockSpec((rows, SENT, PIECE, HEAD_SIZE), lambda i, t: (i, 0, 0, 0)),
        ),
        name="gather_pieces",
    )(table, held)


def gather_give_body(table_ref, meta_ref, held_ref, out_ref, give_ref, *, rows, chunk):
    gather_body(table_ref, held_ref, out_ref, rows=rows, chunk=chunk)

    @pl.when(pl.program_id(0) == 0)
    def _():
        give_ref[...] = held_ref[:, 1 - meta_ref[1]]


def gather_give(table, meta, held, blocks, chunk):
    steps = 2
    rows = blocks // steps
    return pl.pallas_call(
        functools.partial(gather_give_body, rows=rows, chunk=chunk),
        out_shape=(
            jax.ShapeDtypeStruct((blocks, SENT, PIECE, HEAD_SIZE), BF16),
            jax.ShapeDtypeStruct((blocks, PIECE, HEAD_SIZE), BF16),
        ),
        grid_spec=pltpu.PrefetchScalarGridSpec(
            num_scalar_prefetch=2,
            grid=(steps,),
            in_specs=[
                pl.BlockSpec((blocks, CHUNKS, PIECE, HEAD_SIZE), lambda i, t, m: (0, 0, 0, 0))
            ],
            out_specs=[
                pl.BlockSpec((rows, SENT, PIECE, HEAD_SIZE), lambda i, t, m: (i, 0, 0, 0)),
                pl.BlockSpec((blocks, PIECE, HEAD_SIZE), lambda i, t, m: (0, 0, 0)),
            ],
        ),
        name="gather_give",
    )(table, meta, held)


def add_listed(table_ref, got_ref, accs, rows):
    base = pl.program_id(0) * rows

    @pl.when(pl.program_id(0) == 0)
    def _():
        for acc in accs:
            acc[...] = jnp.zeros_like(acc)

    def one(d, total):
        for s in range(1, SENT):
            block = table_ref[(base + d) * NB + FIRST_SENT + s]
            accs[s][block] += got_ref[d, s].astype(F32)
        return total + got_ref[d, 0].astype(F32)

    zero = jnp.zeros((PIECE, HEAD_SIZE), F32)
    accs[0][...] += lax.fori_loop(0, rows, one, zero, unroll=8)


def listed_total(accs):
    accs[1][0] += accs[0][...]
    return (accs[1][...] + accs[2][...]) + (accs[3][...] + accs[4][...])


def scatter_body(table_ref, got_ref, out_ref, *accs, rows):
    add_listed(table_ref, got_ref, accs, rows)

    @pl.when(pl.program_id(0) == pl.num_programs(0) - 1)
    def _():
        out_ref[...] = listed_total(accs)


def scatter_last_body(
    table_ref, meta_ref, got_ref, first_ref, dense_ref, other_ref, out_ref, *accs, rows
):
    add_listed(table_ref, got_ref, accs, rows)

    @pl.when(pl.program_id(0) == pl.num_programs(0) - 1)
    def _():
        core = meta_ref[1]
        second = listed_total(accs)
        mine = dense_ref[...].reshape(second.shape)
        other = other_ref[...].astype(F32).reshape(second.shape)
        out_ref[:, core] = (jnp.where(core == 0, first_ref[...], second) + mine).astype(BF16)
        out_ref[:, 1 - core] = (jnp.where(core == 0, second, first_ref[...]) + other).astype(BF16)


def slot_sums(blocks):
    whole = VM((blocks, PIECE, HEAD_SIZE), F32)
    return [VM((PIECE, HEAD_SIZE), F32)] + [whole] * (SENT - 1)


def scatter_pieces(table, got, blocks):
    steps = 2
    rows = blocks // steps
    return pl.pallas_call(
        functools.partial(scatter_body, rows=rows),
        out_shape=jax.ShapeDtypeStruct((blocks, PIECE, HEAD_SIZE), F32),
        grid_spec=pltpu.PrefetchScalarGridSpec(
            num_scalar_prefetch=1,
            grid=(steps,),
            in_specs=[pl.BlockSpec((rows, SENT, PIECE, HEAD_SIZE), lambda i, t: (i, 0, 0, 0))],
            out_specs=pl.BlockSpec((blocks, PIECE, HEAD_SIZE), lambda i, t: (0, 0, 0)),
            scratch_shapes=slot_sums(blocks),
        ),
        name="scatter_pieces",
    )(table, got)


def scatter_last(table, meta, got, first, dense, other, blocks):
    steps = 2
    rows = blocks // steps
    whole = pl.BlockSpec((blocks, PIECE, HEAD_SIZE), lambda i, t, m: (0, 0, 0))
    return pl.pallas_call(
        functools.partial(scatter_last_body, rows=rows),
        out_shape=jax.ShapeDtypeStruct((blocks, CHUNKS, PIECE, HEAD_SIZE), BF16),
        grid_spec=pltpu.PrefetchScalarGridSpec(
            num_scalar_prefetch=2,
            grid=(steps,),
            in_specs=[
                pl.BlockSpec((rows, SENT, PIECE, HEAD_SIZE), lambda i, t, m: (i, 0, 0, 0)),
                whole,
                pl.BlockSpec((blocks * PIECE, HEAD_SIZE), lambda i, t, m: (0, 0)),
                pl.BlockSpec((blocks * PIECE, HEAD_SIZE), lambda i, t, m: (0, 0)),
            ],
            out_specs=pl.BlockSpec(
                (blocks, CHUNKS, PIECE, HEAD_SIZE), lambda i, t, m: (0, 0, 0, 0)
            ),
            scratch_shapes=slot_sums(blocks),
        ),
        name="scatter_last",
    )(table, meta, got, first, dense, other)


def two_heads(ref, p):
    first = ref[:, pl.ds(2 * p * HEAD_SIZE, HEAD_SIZE)]
    second = ref[:, pl.ds((2 * p + 1) * HEAD_SIZE, HEAD_SIZE)]
    return jnp.concatenate([first, second], axis=0)


def col_sum(x):
    return jnp.sum(x, axis=0, keepdims=True)


def sparse_body(
    meta_ref, valid_ref, q_ref, o_ref, self_ref, before_ref, after_ref, g_ref, *rest
):
    dq_ref, own_ref, prev_ref, next_ref, sent_ref = rest[-14:-9]
    kc, vc, kt, st, dp, pb, ds, dk, dv = rest[-9:]
    b = meta_ref[0]

    @pl.when(b == 0)
    def _():
        dq_ref[...] = jnp.zeros_like(dq_ref)
        own_ref[...] = jnp.zeros_like(own_ref)
        prev_ref[...] = jnp.zeros_like(prev_ref)
        next_ref[...] = jnp.zeros_like(next_ref)
        sent_ref[...] = jnp.zeros_like(sent_ref)

    @pl.when(b != 0)
    def _():
        for kv, dst in ((0, kc), (1, vc)):
            for s, part in enumerate((before_ref, self_ref, after_ref)):
                dst[s * BLOCK : (s + 1) * BLOCK] = part[kv]
            for s in range(SENT):
                at = (FIRST_SENT + s) * BLOCK
                dst[at : at + BLOCK] = g_ref[0, kv, :, s].reshape(BLOCK, HEAD_SIZE)
        kt[...] = kc[...].T
        live = [valid_ref[b * NB + s] > 0 for s in range(NB)]

        def heads(ref, p):
            return two_heads(ref, p)

        def pair(p, w):
            qp = heads(q_ref, p)
            op = heads(o_ref, p)
            st[w] = dot(kc[...], qp, 1, 1)
            dp[w] = dot(vc[...], op, 1, 1)
            top = jnp.full((1, 2 * BLOCK), -FAR, F32)
            for s in range(NB):
                here = jnp.max(st[w, s * BLOCK : (s + 1) * BLOCK], axis=0, keepdims=True)
                top = jnp.maximum(top, jnp.where(live[s], here, -FAR))
            top = top * EXP_SCALE
            total = jnp.zeros((1, 2 * BLOCK), F32)
            cross = jnp.zeros((1, 2 * BLOCK), F32)
            for s in range(NB):
                rows = slice(s * BLOCK, (s + 1) * BLOCK)
                shift = jnp.where(live[s], top, FAR)
                raised = jnp.exp2(st[w, rows] * EXP_SCALE - shift)
                st[w, rows] = raised
                total = total + col_sum(raised)
                cross = cross + col_sum(raised * dp[w, rows])
            inverse = 1.0 / total
            delta = cross * inverse
            for s in range(NB):
                rows = slice(s * BLOCK, (s + 1) * BLOCK)
                weights = st[w, rows] * inverse
                pb[w, rows] = weights.astype(BF16)
                ds[w, rows] = (weights * (dp[w, rows] - delta)).astype(BF16)
            new_dv = dot(pb[w], op, 1, 0)
            new_dk = dot(ds[w], qp, 1, 0)
            dv[...] = new_dv if p == 0 else dv[...] + new_dv
            dk[...] = new_dk if p == 0 else dk[...] + new_dk
            dqt = dot(kt[...], ds[w], 1, 0) * SCALING
            out = jnp.concatenate([dqt[:, :BLOCK].T, dqt[:, BLOCK:].T], axis=1).astype(BF16)
            dq_ref[:, pl.ds(2 * p * HEAD_SIZE, 2 * HEAD_SIZE)] = out

        def two_pairs(i, carry):
            for w in range(2):
                pair(2 * i + w, w)
            return carry

        for i in range(GROUP_SIZE // 4):
            two_pairs(i, 0)
        for kv, acc, factor in ((0, dk, SCALING), (1, dv, 1.0)):
            prev_ref[kv] = (acc[0:BLOCK] * factor).astype(BF16)
            own_ref[kv] = acc[BLOCK : 2 * BLOCK] * factor
            next_ref[kv] = (acc[2 * BLOCK : 3 * BLOCK] * factor).astype(BF16)
            for s in range(SENT):
                at = (FIRST_SENT + s) * BLOCK
                sent_ref[0, kv, :, s] = (
                    (acc[at : at + BLOCK] * factor).astype(BF16).reshape(GROUPS, PIECE, HEAD_SIZE)
                )


def sparse_grads(call, meta, valid, q, o, own, before, after, got, earlier=()):
    first = call * CALL_HEADS
    inside = first % HALF

    wide = pl.BlockSpec((BLOCK, GROUP_SIZE * HEAD_SIZE), lambda h, m, t: (0, first + h))
    pair = pl.BlockSpec((2, BLOCK, HEAD_SIZE), lambda h, m, t: (0, 0, first + h))
    pieces = pl.BlockSpec(
        (1, 2, GROUPS, SENT, PIECE, HEAD_SIZE), lambda h, m, t: (inside + h, 0, 0, 0, 0, 0)
    )
    keys = NB * BLOCK
    width = KEY_HEADS * HEAD_SIZE
    return pl.pallas_call(
        sparse_body,
        out_shape=(
            jax.ShapeDtypeStruct(q.shape, BF16),
            jax.ShapeDtypeStruct((2, BLOCK, width), F32),
            jax.ShapeDtypeStruct((2, BLOCK, width), BF16),
            jax.ShapeDtypeStruct((2, BLOCK, width), BF16),
            jax.ShapeDtypeStruct((HALF, 2, GROUPS, SENT, PIECE, HEAD_SIZE), BF16),
        ),
        grid_spec=pltpu.PrefetchScalarGridSpec(
            num_scalar_prefetch=2,
            grid=(CALL_HEADS,),
            in_specs=[wide, wide, pair, pair, pair, pieces]
            + [pl.BlockSpec(memory_space=pl.ANY)] * len(earlier),
            out_specs=[wide, pair, pair, pair, pieces],
            scratch_shapes=[
                VM((keys, HEAD_SIZE), BF16),
                VM((keys, HEAD_SIZE), BF16),
                VM((HEAD_SIZE, keys), BF16),
                VM((2, keys, 2 * BLOCK), F32),
                VM((2, keys, 2 * BLOCK), F32),
                VM((2, keys, 2 * BLOCK), BF16),
                VM((2, keys, 2 * BLOCK), BF16),
                VM((keys, HEAD_SIZE), F32),
                VM((keys, HEAD_SIZE), F32),
            ],
        ),
        input_output_aliases={8 + n: n for n in range(len(earlier))},
        name="sparse_grads",
    )(meta, valid, q, o, own, before, after, got, *earlier)


def load_held(meta_ref, held_ref, other_ref, kc, vc):
    core = meta_ref[1]
    mine = held_ref[:, core].reshape(kc.shape)
    other = other_ref[...].reshape(kc.shape)

    @pl.when(core == 0)
    def _():
        kc[...] = mine
        vc[...] = other

    @pl.when(core != 0)
    def _():
        kc[...] = other
        vc[...] = mine


def stats_body(
    meta_ref, p0, p1, p2, p3, held_ref, other_ref, out_ref, q_ref, kc, vc, sem
):
    parts = (p0, p1, p2, p3)
    for n, part in enumerate(parts):

        @pl.when(meta_ref[3] == n)
        def _():
            copy = pltpu.make_async_copy(part, q_ref, sem)
            copy.start()
            copy.wait()

    load_held(meta_ref, held_ref, other_ref, kc, vc)
    for p in range(GROUP_SIZE // 2):
        scores = dot(kc[...], two_heads(q_ref.at[0], p), 1, 1)
        grads = dot(vc[...], two_heads(q_ref.at[1], p), 1, 1)
        top = jnp.max(scores, axis=0, keepdims=True) * EXP_SCALE
        raised = jnp.exp2(scores * EXP_SCALE - top)
        for n, row in enumerate((top, col_sum(raised), col_sum(raised * grads))):
            for j in range(2):
                at = n * GROUP_SIZE + 2 * p + j
                out_ref[at : at + 1] = row[:, j * BLOCK : (j + 1) * BLOCK]


def dense_stats(meta, parts, held, other):
    keys = held.shape[0] * PIECE
    return pl.pallas_call(
        stats_body,
        out_shape=(
            jax.ShapeDtypeStruct((3 * GROUP_SIZE, BLOCK), F32),
            jax.ShapeDtypeStruct(parts[0].shape, BF16),
        ),
        in_specs=[pl.BlockSpec(memory_space=pltpu.SMEM)]
        + [pl.BlockSpec(memory_space=pl.ANY)] * 4
        + [pl.BlockSpec(memory_space=VM)] * 2,
        out_specs=[pl.BlockSpec(memory_space=VM)] * 2,
        scratch_shapes=[
            VM((keys, HEAD_SIZE), BF16),
            VM((keys, HEAD_SIZE), BF16),
            pltpu.SemaphoreType.DMA(()),
        ],
        name="dense_stats",
    )(meta, *parts, held, other)


def merge_stats(parts):
    n = GROUP_SIZE
    top = functools.reduce(jnp.maximum, [x[:n] for x in parts])
    factors = [jnp.exp2(x[:n] - top) for x in parts]
    total = sum(x[n : 2 * n] * f for x, f in zip(parts, factors))
    cross = sum(x[2 * n :] * f for x, f in zip(parts, factors))
    return jnp.concatenate([top, total, cross], axis=0)


def dense_body(
    meta_ref, q_ref, held_ref, other_ref, s0, s1, s2, s3, keep_ref, give_ref, dq_ref,
    kc, vc, kt, stats, dkv_ref,
):
    load_held(meta_ref, held_ref, other_ref, kc, vc)
    kt[...] = kc[...].T
    stats[...] = merge_stats([s0[...], s1[...], s2[...], s3[...]])
    core = meta_ref[1]

    def row(n, p):
        at = n * GROUP_SIZE + 2 * p
        return jnp.concatenate([stats[at : at + 1], stats[at + 1 : at + 2]], axis=1)

    for p in range(GROUP_SIZE // 2):
        top = row(0, p)
        inverse = 1.0 / row(1, p)
        delta = row(2, p) * inverse
        qp = two_heads(q_ref.at[0], p)
        op = two_heads(q_ref.at[1], p)
        scores = dot(kc[...], qp, 1, 1)
        grads = dot(vc[...], op, 1, 1)
        weights = jnp.exp2(scores * EXP_SCALE - top) * inverse
        rounded = weights.astype(BF16)
        score_grad = (weights * (grads - delta)).astype(BF16)
        new_dk = dot(score_grad, qp, 1, 0) * SCALING
        new_dv = dot(rounded, op, 1, 0)
        dkv_ref[core] = new_dk if p == 0 else dkv_ref[core] + new_dk
        dkv_ref[1 - core] = new_dv if p == 0 else dkv_ref[1 - core] + new_dv
        dqt = dot(kt[...], score_grad, 1, 0) * SCALING
        for j in range(2):
            dq_ref[:, pl.ds((2 * p + j) * HEAD_SIZE, HEAD_SIZE)] = (
                dqt[:, j * BLOCK : (j + 1) * BLOCK].T.astype(BF16)
            )
    keep_ref[...] = dkv_ref[0]
    give_ref[...] = dkv_ref[1].astype(BF16)


def dense_grads(meta, qo, held, other, stats):
    keys = held.shape[0] * PIECE
    return pl.pallas_call(
        dense_body,
        out_shape=(
            jax.ShapeDtypeStruct((keys, HEAD_SIZE), F32),
            jax.ShapeDtypeStruct((keys, HEAD_SIZE), BF16),
            jax.ShapeDtypeStruct((BLOCK, GROUP_SIZE * HEAD_SIZE), BF16),
        ),
        in_specs=[pl.BlockSpec(memory_space=pltpu.SMEM)] + [pl.BlockSpec(memory_space=VM)] * 7,
        out_specs=[pl.BlockSpec(memory_space=VM)] * 3,
        scratch_shapes=[
            VM((keys, HEAD_SIZE), BF16),
            VM((keys, HEAD_SIZE), BF16),
            VM((HEAD_SIZE, keys), BF16),
            VM((3 * GROUP_SIZE, BLOCK), F32),
            VM((2, keys, HEAD_SIZE), F32),
        ],
        name="dense_grads",
    )(meta, qo, held, other, *stats)


def combine_body(own_ref, prev_ref, next_ref, got_ref, dk_ref, dv_ref):
    for kv, out in ((0, dk_ref), (1, dv_ref)):
        for h in range(KEY_HEADS):
            cols = pl.ds(h * HEAD_SIZE, HEAD_SIZE)
            total = own_ref[kv, :, cols] + prev_ref[kv, :, cols].astype(F32)
            total = total + next_ref[kv, :, cols].astype(F32)
            pieces = got_ref[h % HALF, kv, :, h // HALF].reshape(BLOCK, HEAD_SIZE)
            out[:, cols] = (total + pieces.astype(F32)).astype(BF16)


def combine(own, from_prev, from_next, got):
    width = KEY_HEADS * HEAD_SIZE
    return pl.pallas_call(
        combine_body,
        out_shape=(jax.ShapeDtypeStruct((BLOCK, width), BF16),) * 2,
        in_specs=[pl.BlockSpec(memory_space=VM)] * 4,
        out_specs=[pl.BlockSpec(memory_space=VM)] * 2,
        name="combine",
    )(own, from_prev, from_next, got)


def spread_body(meta_ref, q_ref, o_ref, *rest):
    outs, stage, sems = rest[:-2], rest[-2], rest[-1]

    @pl.when(meta_ref[0] == 0)
    def _():
        loads, stores = [], []
        for h, out in enumerate(outs):
            cols = pl.ds(h * GROUP_SIZE * HEAD_SIZE, GROUP_SIZE * HEAD_SIZE)
            for j, ref in enumerate((q_ref, o_ref)):
                loads.append(
                    pltpu.make_async_copy(ref.at[:, cols], stage.at[h, j], sems.at[0, h, j])
                )
                stores.append(pltpu.make_async_copy(stage.at[h, j], out.at[j], sems.at[1, h, j]))
        for copy in loads:
            copy.start()
        for load, store in zip(loads, stores):
            load.wait()
            store.start()
        for copy in stores:
            copy.wait()


def spread_heads(meta, q, o):
    hbm = pl.BlockSpec(memory_space=pl.ANY)
    shape = (2, BLOCK, GROUP_SIZE * HEAD_SIZE)
    return pl.pallas_call(
        spread_body,
        out_shape=(jax.ShapeDtypeStruct(shape, BF16),) * KEY_HEADS,
        in_specs=[pl.BlockSpec(memory_space=pltpu.SMEM), hbm, hbm],
        out_specs=[hbm] * KEY_HEADS,
        scratch_shapes=[
            VM((KEY_HEADS,) + shape, BF16),
            pltpu.SemaphoreType.DMA((2, KEY_HEADS, 2)),
        ],
        name="spread_heads",
    )(meta, q, o)


def first_body(meta_ref, dq_ref, *rest):
    parts, out, stage, sems = rest[:KEY_HEADS], rest[KEY_HEADS], rest[-2], rest[-1]

    @pl.when(meta_ref[0] == 0)
    def _():
        loads, stores = [], []
        for h, part in enumerate(parts):
            cols = pl.ds(h * GROUP_SIZE * HEAD_SIZE, GROUP_SIZE * HEAD_SIZE)
            loads.append(pltpu.make_async_copy(part, stage.at[h], sems.at[0, h]))
            stores.append(pltpu.make_async_copy(stage.at[h], out.at[:, cols], sems.at[1, h]))
        for copy in loads:
            copy.start()
        for load, store in zip(loads, stores):
            load.wait()
            store.start()
        for copy in stores:
            copy.wait()


def put_first(meta, dq, parts):
    hbm = pl.BlockSpec(memory_space=pl.ANY)
    return pl.pallas_call(
        first_body,
        out_shape=jax.ShapeDtypeStruct(dq.shape, dq.dtype),
        in_specs=[pl.BlockSpec(memory_space=pltpu.SMEM)] + [hbm] * (KEY_HEADS + 1),
        out_specs=hbm,
        input_output_aliases={1: 0},
        scratch_shapes=[
            VM((KEY_HEADS, BLOCK, GROUP_SIZE * HEAD_SIZE), BF16),
            pltpu.SemaphoreType.DMA((2, KEY_HEADS)),
        ],
        name="put_first",
    )(meta, dq, *parts)


def pick_body(meta_ref, *rest, at):
    parts, out_ref, sem = rest[:-2], rest[-2], rest[-1]
    for n, part in enumerate(parts):

        @pl.when(meta_ref[at] == n)
        def _():
            copy = pltpu.make_async_copy(part, out_ref, sem)
            copy.start()
            copy.wait()


def pick(meta, at, parts):
    return pl.pallas_call(
        functools.partial(pick_body, at=at),
        out_shape=jax.ShapeDtypeStruct(parts[0].shape, parts[0].dtype),
        in_specs=[pl.BlockSpec(memory_space=pltpu.SMEM)]
        + [pl.BlockSpec(memory_space=pl.ANY)] * len(parts),
        out_specs=pl.BlockSpec(memory_space=VM),
        scratch_shapes=[pltpu.SemaphoreType.DMA(())],
        name="pick",
    )(meta, *parts)


def tp_pairs(pairs, ctx_size, tp_size):
    return [(c * tp_size + a, c * tp_size + b) for c in range(ctx_size) for a, b in pairs]


def add(*xs):
    return sum(x.astype(F32) for x in xs).astype(BF16)


def per_device(queries, key_tensor, value_tensor, output_gradient, key_blocks, slot_valid):
    tp_size, ctx_size = lax.axis_size("tp"), lax.axis_size("ctx")
    blocks = ctx_size * tp_size
    b_index = lax.axis_index("ctx") * tp_size + lax.axis_index("tp")
    core = lax.axis_index("ctx") % 2
    t_index = lax.axis_index("tp")
    meta = jnp.stack([b_index, core, t_index % 4, t_index // 4, lax.axis_index("ctx")])
    meta = meta.astype(jnp.int32)
    table = key_blocks.reshape(-1)
    valid = slot_valid.reshape(-1)
    up = [(i, i + 1) for i in range(1, blocks - 1)]
    down = [(i + 1, i) for i in range(1, blocks - 1)]
    partner = [(i, (i // tp_size ^ 1) * tp_size + i % tp_size) for i in range(blocks)]
    four = range(4)

    def swap(x):
        return lax.all_to_all(x, BOTH, split_axis=0, concat_axis=0, tiled=True)

    def send(x, pairs):
        return lax.ppermute(x, BOTH, pairs)

    def send_tp(x, pairs):
        return send(x, tp_pairs(pairs, ctx_size, tp_size))

    def along_x(n):
        return [(4 * z + x, 4 * z + (x + n) % 4) for z in four for x in four]

    def along_z(n):
        return [(4 * z + x, 4 * ((z + n) % 4) + x) for z in four for x in four]

    pieces, both = pack_pieces(key_tensor, value_tensor)
    held = swap(pieces.reshape(blocks, CHUNKS, PIECE, HEAD_SIZE))
    before, after = send(both, up), send(both, down)
    slices = spread_heads(meta, queries, output_gradient)
    moved = [slices[0]] * ctx_size
    for c in (4, 2, 6, 3, 5, 7, 1):
        moved[c] = send(slices[c // 2 + HALF * (c % 2)], [(0, c * tp_size)])

    listed = [gather_pieces(table, held, blocks, 0)]
    more, given = gather_give(table, meta, held, blocks, 1)
    listed.append(more)
    given = send(given, partner)
    shape = (HALF, 2, GROUPS, SENT, PIECE, HEAD_SIZE)
    got = []
    for j in range(CHUNKS):
        got.append(swap(listed[j]).reshape(shape))

    qo = pick(meta, 4, moved)
    moved = [qo] + [send_tp(qo, [(0, n)]) for n in range(1, 4)]
    qo = pick(meta, 2, moved)
    moved = [qo] + [send_tp(qo, [(x, 4 * n + x) for x in four]) for n in range(1, 4)]

    grads, back = (), []
    calls = HALF // CALL_HEADS
    for j in range(CHUNKS):
        for n in range(calls):
            call = calls * j + n
            grads = sparse_grads(
                call, meta, valid, queries, output_gradient, both, before, after, got[j],
                grads if n > 0 else grads[:4],
            )
        back.append(swap(grads[4].reshape(blocks, SENT, PIECE, HEAD_SIZE)))
    dq, own, to_prev, to_next = grads[:4]
    from_next, from_prev = send(to_prev, down), send(to_next, up)

    stats, qo = dense_stats(meta, moved, held, given)
    others = [send_tp(stats, along_x(n)) for n in range(1, 4)]
    stats = merge_stats([stats] + others)
    others = [send_tp(stats, along_z(n)) for n in range(1, 4)]
    dense, to_partner, part = dense_grads(meta, qo, held, given, [stats] + others)
    dense_other = send(to_partner, partner)
    others = [send_tp(part, [(4 * n + x, x) for x in four]) for n in range(1, 4)]
    total = add(part, *others)
    others = [send_tp(total, [(n, 0)]) for n in range(1, 4)]
    total = add(total, *others)
    parts = [total] * KEY_HEADS
    for c in range(1, ctx_size):
        parts[c // 2 + HALF * (c % 2)] = send(total, [(c * tp_size, 0)])
    d_q = put_first(meta, dq, parts)

    first = scatter_pieces(table, back[0], blocks)
    summed = scatter_last(table, meta, back[1], first, dense, dense_other, blocks)
    home = swap(summed).reshape(HALF, 2, GROUPS, CHUNKS, PIECE, HEAD_SIZE)
    d_k, d_v = combine(own, from_prev, from_next, home)
    return d_q, d_k, d_v


def solution(mesh):
    spec = P(BOTH, None)

    return jax.shard_map(
        per_device,
        mesh=mesh,
        in_specs=(spec, spec, spec, spec, P(), P()),
        out_specs=(spec, spec, spec),
        check_vma=False,
    )
```

```python
import functools
import math

import jax
import jax.numpy as jnp
from jax import lax
from jax.experimental import pallas as pl
from jax.experimental.pallas import tpu as pltpu
from jax.sharding import PartitionSpec as P


KEY_HEADS = 8
GROUP_SIZE = 8
HEAD_SIZE = 128
BLOCK = 128
NB = 8
GROUPS = 16
PIECE = 8
SENT = 5
FIRST_SENT = NB - SENT
CHUNKS = 2
HALF = KEY_HEADS // CHUNKS
CALL_HEADS = 4
BOTH = ("ctx", "tp")
SCALING = 1.0 / math.sqrt(HEAD_SIZE)
EXP_SCALE = SCALING * math.log2(math.e)
FAR = 1e30
F32 = jnp.float32
BF16 = jnp.bfloat16
VM = pltpu.VMEM


def dot(a, b, ca, cb):
    return lax.dot_general(a, b, (((ca,), (cb,)), ((), ())), preferred_element_type=F32)


def pack_body(k_ref, v_ref, out_ref, both_ref):
    for kv, ref in enumerate((k_ref, v_ref)):
        both_ref[kv] = ref[...]
        for j in range(CHUNKS):
            for y in range(HALF):
                cols = pl.ds((j * HALF + y) * HEAD_SIZE, HEAD_SIZE)
                out_ref[y, kv, :, j] = ref[:, cols].reshape(GROUPS, PIECE, HEAD_SIZE)


def pack_pieces(k, v):
    return pl.pallas_call(
        pack_body,
        out_shape=(
            jax.ShapeDtypeStruct((HALF, 2, GROUPS, CHUNKS, PIECE, HEAD_SIZE), BF16),
            jax.ShapeDtypeStruct((2,) + k.shape, BF16),
        ),
        in_specs=[pl.BlockSpec(memory_space=VM)] * 2,
        out_specs=[pl.BlockSpec(memory_space=VM)] * 2,
        name="pack_pieces",
        compiler_params=pltpu.CompilerParams(vmem_limit_bytes=12 << 20),
    )(k, v)


def gather_body(table_ref, meta_ref, held_ref, out_ref, *give_ref, rows, chunk):
    base = pl.program_id(0) * rows

    def one(d, carry):
        for s in range(SENT):
            block = table_ref[(base + d) * NB + FIRST_SENT + s]
            out_ref[d, s] = held_ref[block, chunk]
        return carry

    lax.fori_loop(0, rows, one, 0, unroll=8)
    if give_ref:

        @pl.when(pl.program_id(0) == 0)
        def _():
            give_ref[0][...] = held_ref[:, 1 - meta_ref[1]]


def gather_pieces(table, meta, held, blocks, chunk, give):
    steps = 2
    rows = blocks // steps
    shapes = [jax.ShapeDtypeStruct((blocks, SENT, PIECE, HEAD_SIZE), BF16)]
    specs = [pl.BlockSpec((rows, SENT, PIECE, HEAD_SIZE), lambda i, t, m: (i, 0, 0, 0))]
    if give:
        shapes.append(jax.ShapeDtypeStruct((blocks, PIECE, HEAD_SIZE), BF16))
        specs.append(pl.BlockSpec((blocks, PIECE, HEAD_SIZE), lambda i, t, m: (0, 0, 0)))
    return pl.pallas_call(
        functools.partial(gather_body, rows=rows, chunk=chunk),
        out_shape=shapes,
        grid_spec=pltpu.PrefetchScalarGridSpec(
            num_scalar_prefetch=2,
            grid=(steps,),
            in_specs=[pl.BlockSpec(memory_space=VM)],
            out_specs=specs,
        ),
        name="gather_pieces",
        compiler_params=pltpu.CompilerParams(vmem_limit_bytes=12 << 20),
    )(table, meta, held)


def add_listed(table_ref, got_ref, accs, blocks):
    for acc in accs:
        acc[...] = jnp.zeros_like(acc)

    def one(d, total):
        for s in range(1, SENT):
            block = table_ref[d * NB + FIRST_SENT + s]
            accs[s - 1][block] += got_ref[d, s].astype(F32)
        return total + got_ref[d, 0].astype(F32)

    zero = jnp.zeros((PIECE, HEAD_SIZE), F32)
    accs[0][0] += lax.fori_loop(0, blocks, one, zero, unroll=8)
    return (accs[0][...] + accs[1][...]) + (accs[2][...] + accs[3][...])


def scatter_body(table_ref, got_ref, out_ref, *accs, blocks):
    out_ref[...] = add_listed(table_ref, got_ref, accs, blocks)


def scatter_last_body(
    table_ref, meta_ref, got_ref, first_ref, dense_ref, other_ref, out_ref, *accs, blocks
):
    core = meta_ref[1]
    second = add_listed(table_ref, got_ref, accs, blocks)
    mine = dense_ref[...].reshape(second.shape)
    other = other_ref[...].astype(F32).reshape(second.shape)
    out_ref[:, core] = (jnp.where(core == 0, first_ref[...], second) + mine).astype(BF16)
    out_ref[:, 1 - core] = (jnp.where(core == 0, second, first_ref[...]) + other).astype(BF16)


def slot_sums(blocks):
    return [VM((blocks, PIECE, HEAD_SIZE), F32)] * (SENT - 1)


def scatter_pieces(table, got, blocks):
    return pl.pallas_call(
        functools.partial(scatter_body, blocks=blocks),
        out_shape=jax.ShapeDtypeStruct((blocks, PIECE, HEAD_SIZE), F32),
        in_specs=[pl.BlockSpec(memory_space=pltpu.SMEM), pl.BlockSpec(memory_space=VM)],
        out_specs=pl.BlockSpec(memory_space=VM),
        scratch_shapes=slot_sums(blocks),
        name="scatter_pieces",
        compiler_params=pltpu.CompilerParams(vmem_limit_bytes=12 << 20),
    )(table, got)


def scatter_last(table, meta, got, first, dense, other, blocks):
    return pl.pallas_call(
        functools.partial(scatter_last_body, blocks=blocks),
        out_shape=jax.ShapeDtypeStruct((blocks, CHUNKS, PIECE, HEAD_SIZE), BF16),
        in_specs=[pl.BlockSpec(memory_space=pltpu.SMEM)] * 2 + [pl.BlockSpec(memory_space=VM)] * 4,
        out_specs=pl.BlockSpec(memory_space=VM),
        scratch_shapes=slot_sums(blocks),
        name="scatter_last",
        compiler_params=pltpu.CompilerParams(vmem_limit_bytes=12 << 20),
    )(table, meta, got, first, dense, other)


def two_heads(ref, p):
    first = ref[:, pl.ds(2 * p * HEAD_SIZE, HEAD_SIZE)]
    second = ref[:, pl.ds((2 * p + 1) * HEAD_SIZE, HEAD_SIZE)]
    return jnp.concatenate([first, second], axis=0)


def col_sum(x):
    return jnp.sum(x, axis=0, keepdims=True)


def sparse_body(
    meta_ref, valid_ref, q_ref, o_ref, self_ref, before_ref, after_ref, g_ref, *rest
):
    dq_ref, own_ref, prev_ref, next_ref, sent_ref = rest[-14:-9]
    kc, vc, kt, st, dp, pb, ds, dk, dv = rest[-9:]
    b = meta_ref[0]

    @pl.when(b == 0)
    def _():
        dq_ref[...] = jnp.zeros_like(dq_ref)
        own_ref[...] = jnp.zeros_like(own_ref)
        prev_ref[...] = jnp.zeros_like(prev_ref)
        next_ref[...] = jnp.zeros_like(next_ref)
        sent_ref[...] = jnp.zeros_like(sent_ref)

    @pl.when(b != 0)
    def _():
        for kv, dst in ((0, kc), (1, vc)):
            for s, part in enumerate((before_ref, self_ref, after_ref)):
                dst[s * BLOCK : (s + 1) * BLOCK] = part[kv]
            for s in range(SENT):
                at = (FIRST_SENT + s) * BLOCK
                dst[at : at + BLOCK] = g_ref[pl.program_id(0), kv, :, s].reshape(BLOCK, HEAD_SIZE)
        kt[...] = kc[...].T
        live = [valid_ref[b * NB + s] > 0 for s in range(NB)]

        def heads(ref, p):
            return two_heads(ref, p)

        def pair(p, w):
            qp = heads(q_ref, p)
            op = heads(o_ref, p)
            st[w] = dot(kc[...], qp, 1, 1)
            dp[w] = dot(vc[...], op, 1, 1)
            top = jnp.full((1, 2 * BLOCK), -FAR, F32)
            for s in range(NB):
                here = jnp.max(st[w, s * BLOCK : (s + 1) * BLOCK], axis=0, keepdims=True)
                top = jnp.maximum(top, jnp.where(live[s], here, -FAR))
            top = top * EXP_SCALE
            total = jnp.zeros((1, 2 * BLOCK), F32)
            cross = jnp.zeros((1, 2 * BLOCK), F32)
            for s in range(NB):
                rows = slice(s * BLOCK, (s + 1) * BLOCK)
                shift = jnp.where(live[s], top, FAR)
                raised = jnp.exp2(st[w, rows] * EXP_SCALE - shift)
                st[w, rows] = raised
                total = total + col_sum(raised)
                cross = cross + col_sum(raised * dp[w, rows])
            inverse = 1.0 / total
            delta = cross * inverse
            for s in range(NB):
                rows = slice(s * BLOCK, (s + 1) * BLOCK)
                weights = st[w, rows] * inverse
                pb[w, rows] = weights.astype(BF16)
                ds[w, rows] = (weights * (dp[w, rows] - delta)).astype(BF16)
            new_dv = dot(pb[w], op, 1, 0)
            new_dk = dot(ds[w], qp, 1, 0)
            dv[...] = new_dv if p == 0 else dv[...] + new_dv
            dk[...] = new_dk if p == 0 else dk[...] + new_dk
            dqt = dot(kt[...], ds[w], 1, 0) * SCALING
            out = jnp.concatenate([dqt[:, :BLOCK].T, dqt[:, BLOCK:].T], axis=1).astype(BF16)
            dq_ref[:, pl.ds(2 * p * HEAD_SIZE, 2 * HEAD_SIZE)] = out

        def two_pairs(i, carry):
            for w in range(2):
                pair(2 * i + w, w)
            return carry

        for i in range(GROUP_SIZE // 4):
            two_pairs(i, 0)
        for kv, acc, factor in ((0, dk, SCALING), (1, dv, 1.0)):
            prev_ref[kv] = (acc[0:BLOCK] * factor).astype(BF16)
            own_ref[kv] = acc[BLOCK : 2 * BLOCK] * factor
            next_ref[kv] = (acc[2 * BLOCK : 3 * BLOCK] * factor).astype(BF16)
            for s in range(SENT):
                at = (FIRST_SENT + s) * BLOCK
                sent_ref[0, kv, :, s] = (
                    (acc[at : at + BLOCK] * factor).astype(BF16).reshape(GROUPS, PIECE, HEAD_SIZE)
                )


def sparse_grads(call, meta, valid, q, o, own, before, after, got, earlier=()):
    first = call * CALL_HEADS
    inside = first % HALF

    wide = pl.BlockSpec((BLOCK, GROUP_SIZE * HEAD_SIZE), lambda h, m, t: (0, first + h))
    pair = pl.BlockSpec((2, BLOCK, HEAD_SIZE), lambda h, m, t: (0, 0, first + h))
    pieces = pl.BlockSpec(
        (1, 2, GROUPS, SENT, PIECE, HEAD_SIZE), lambda h, m, t: (inside + h, 0, 0, 0, 0, 0)
    )
    keys = NB * BLOCK
    width = KEY_HEADS * HEAD_SIZE
    return pl.pallas_call(
        sparse_body,
        out_shape=(
            jax.ShapeDtypeStruct(q.shape, BF16),
            jax.ShapeDtypeStruct((2, BLOCK, width), F32),
            jax.ShapeDtypeStruct((2, BLOCK, width), BF16),
            jax.ShapeDtypeStruct((2, BLOCK, width), BF16),
            jax.ShapeDtypeStruct((HALF, 2, GROUPS, SENT, PIECE, HEAD_SIZE), BF16),
        ),
        grid_spec=pltpu.PrefetchScalarGridSpec(
            num_scalar_prefetch=2,
            grid=(CALL_HEADS,),
            in_specs=[wide, wide, pair, pair, pair, pl.BlockSpec(memory_space=VM)]
            + [pl.BlockSpec(memory_space=pl.ANY)] * len(earlier),
            out_specs=[wide, pair, pair, pair, pieces],
            scratch_shapes=[
                VM((keys, HEAD_SIZE), BF16),
                VM((keys, HEAD_SIZE), BF16),
                VM((HEAD_SIZE, keys), BF16),
                VM((2, keys, 2 * BLOCK), F32),
                VM((2, keys, 2 * BLOCK), F32),
                VM((2, keys, 2 * BLOCK), BF16),
                VM((2, keys, 2 * BLOCK), BF16),
                VM((keys, HEAD_SIZE), F32),
                VM((keys, HEAD_SIZE), F32),
            ],
        ),
        input_output_aliases={8 + n: n for n in range(len(earlier))},
        name="sparse_grads",
        compiler_params=pltpu.CompilerParams(vmem_limit_bytes=24 << 20),
    )(meta, valid, q, o, own, before, after, got, *earlier)


def load_held(meta_ref, held_ref, other_ref, kc, vc):
    core = meta_ref[1]
    mine = held_ref[:, core].reshape(kc.shape)
    other = other_ref[...].reshape(kc.shape)

    @pl.when(core == 0)
    def _():
        kc[...] = mine
        vc[...] = other

    @pl.when(core != 0)
    def _():
        kc[...] = other
        vc[...] = mine


def stats_body(
    meta_ref, p0, p1, p2, p3, held_ref, other_ref, out_ref, q_ref, kc, vc, sem
):
    parts = (p0, p1, p2, p3)
    for n, part in enumerate(parts):

        @pl.when(meta_ref[3] == n)
        def _():
            copy = pltpu.make_async_copy(part, q_ref, sem)
            copy.start()
            copy.wait()

    load_held(meta_ref, held_ref, other_ref, kc, vc)
    for p in range(GROUP_SIZE // 2):
        scores = dot(kc[...], two_heads(q_ref.at[0], p), 1, 1)
        grads = dot(vc[...], two_heads(q_ref.at[1], p), 1, 1)
        top = jnp.max(scores, axis=0, keepdims=True) * EXP_SCALE
        raised = jnp.exp2(scores * EXP_SCALE - top)
        for n, row in enumerate((top, col_sum(raised), col_sum(raised * grads))):
            for j in range(2):
                at = n * GROUP_SIZE + 2 * p + j
                out_ref[at : at + 1] = row[:, j * BLOCK : (j + 1) * BLOCK]


def dense_stats(meta, parts, held, other):
    keys = held.shape[0] * PIECE
    return pl.pallas_call(
        stats_body,
        out_shape=(
            jax.ShapeDtypeStruct((3 * GROUP_SIZE, BLOCK), F32),
            jax.ShapeDtypeStruct(parts[0].shape, BF16),
        ),
        in_specs=[pl.BlockSpec(memory_space=pltpu.SMEM)]
        + [pl.BlockSpec(memory_space=pl.ANY)] * 4
        + [pl.BlockSpec(memory_space=VM)] * 2,
        out_specs=[pl.BlockSpec(memory_space=VM)] * 2,
        scratch_shapes=[
            VM((keys, HEAD_SIZE), BF16),
            VM((keys, HEAD_SIZE), BF16),
            pltpu.SemaphoreType.DMA(()),
        ],
        name="dense_stats",
        compiler_params=pltpu.CompilerParams(vmem_limit_bytes=20 << 20),
    )(meta, *parts, held, other)


def merge_stats(parts):
    n = GROUP_SIZE
    top = functools.reduce(jnp.maximum, [x[:n] for x in parts])
    factors = [jnp.exp2(x[:n] - top) for x in parts]
    total = sum(x[n : 2 * n] * f for x, f in zip(parts, factors))
    cross = sum(x[2 * n :] * f for x, f in zip(parts, factors))
    return jnp.concatenate([top, total, cross], axis=0)


def dense_body(
    meta_ref, q_ref, held_ref, other_ref, s0, s1, s2, s3, keep_ref, give_ref, dq_ref,
    kc, vc, kt, stats, dkv_ref,
):
    load_held(meta_ref, held_ref, other_ref, kc, vc)
    kt[...] = kc[...].T
    stats[...] = merge_stats([s0[...], s1[...], s2[...], s3[...]])
    core = meta_ref[1]

    def row(n, p):
        at = n * GROUP_SIZE + 2 * p
        return jnp.concatenate([stats[at : at + 1], stats[at + 1 : at + 2]], axis=1)

    for p in range(GROUP_SIZE // 2):
        top = row(0, p)
        inverse = 1.0 / row(1, p)
        delta = row(2, p) * inverse
        qp = two_heads(q_ref.at[0], p)
        op = two_heads(q_ref.at[1], p)
        scores = dot(kc[...], qp, 1, 1)
        grads = dot(vc[...], op, 1, 1)
        weights = jnp.exp2(scores * EXP_SCALE - top) * inverse
        rounded = weights.astype(BF16)
        score_grad = (weights * (grads - delta)).astype(BF16)
        new_dk = dot(score_grad, qp, 1, 0) * SCALING
        new_dv = dot(rounded, op, 1, 0)
        dkv_ref[core] = new_dk if p == 0 else dkv_ref[core] + new_dk
        dkv_ref[1 - core] = new_dv if p == 0 else dkv_ref[1 - core] + new_dv
        dqt = dot(kt[...], score_grad, 1, 0) * SCALING
        for j in range(2):
            dq_ref[:, pl.ds((2 * p + j) * HEAD_SIZE, HEAD_SIZE)] = (
                dqt[:, j * BLOCK : (j + 1) * BLOCK].T.astype(BF16)
            )
    keep_ref[...] = dkv_ref[0]
    give_ref[...] = dkv_ref[1].astype(BF16)


def dense_grads(meta, qo, held, other, stats):
    keys = held.shape[0] * PIECE
    return pl.pallas_call(
        dense_body,
        out_shape=(
            jax.ShapeDtypeStruct((keys, HEAD_SIZE), F32),
            jax.ShapeDtypeStruct((keys, HEAD_SIZE), BF16),
            jax.ShapeDtypeStruct((BLOCK, GROUP_SIZE * HEAD_SIZE), BF16),
        ),
        in_specs=[pl.BlockSpec(memory_space=pltpu.SMEM)] + [pl.BlockSpec(memory_space=VM)] * 7,
        out_specs=[pl.BlockSpec(memory_space=VM)] * 3,
        scratch_shapes=[
            VM((keys, HEAD_SIZE), BF16),
            VM((keys, HEAD_SIZE), BF16),
            VM((HEAD_SIZE, keys), BF16),
            VM((3 * GROUP_SIZE, BLOCK), F32),
            VM((2, keys, HEAD_SIZE), F32),
        ],
        name="dense_grads",
        compiler_params=pltpu.CompilerParams(vmem_limit_bytes=24 << 20),
    )(meta, qo, held, other, *stats)


def combine_body(own_ref, prev_ref, next_ref, got_ref, dk_ref, dv_ref):
    for kv, out in ((0, dk_ref), (1, dv_ref)):
        for h in range(KEY_HEADS):
            cols = pl.ds(h * HEAD_SIZE, HEAD_SIZE)
            total = own_ref[kv, :, cols] + prev_ref[kv, :, cols].astype(F32)
            total = total + next_ref[kv, :, cols].astype(F32)
            pieces = got_ref[h % HALF, kv, :, h // HALF].reshape(BLOCK, HEAD_SIZE)
            out[:, cols] = (total + pieces.astype(F32)).astype(BF16)


def combine(own, from_prev, from_next, got):
    width = KEY_HEADS * HEAD_SIZE
    return pl.pallas_call(
        combine_body,
        out_shape=(jax.ShapeDtypeStruct((BLOCK, width), BF16),) * 2,
        in_specs=[pl.BlockSpec(memory_space=VM)] * 4,
        out_specs=[pl.BlockSpec(memory_space=VM)] * 2,
        name="combine",
        compiler_params=pltpu.CompilerParams(vmem_limit_bytes=12 << 20),
    )(own, from_prev, from_next, got)


def spread_body(meta_ref, q_ref, o_ref, *rest):
    outs, stage, sems = rest[:-2], rest[-2], rest[-1]

    @pl.when(meta_ref[0] == 0)
    def _():
        loads, stores = [], []
        for h, out in enumerate(outs):
            cols = pl.ds(h * GROUP_SIZE * HEAD_SIZE, GROUP_SIZE * HEAD_SIZE)
            for j, ref in enumerate((q_ref, o_ref)):
                loads.append(
                    pltpu.make_async_copy(ref.at[:, cols], stage.at[h, j], sems.at[0, h, j])
                )
                stores.append(pltpu.make_async_copy(stage.at[h, j], out.at[j], sems.at[1, h, j]))
        for copy in loads:
            copy.start()
        for load, store in zip(loads, stores):
            load.wait()
            store.start()
        for copy in stores:
            copy.wait()


def spread_heads(meta, q, o):
    hbm = pl.BlockSpec(memory_space=pl.ANY)
    shape = (2, BLOCK, GROUP_SIZE * HEAD_SIZE)
    return pl.pallas_call(
        spread_body,
        out_shape=(jax.ShapeDtypeStruct(shape, BF16),) * KEY_HEADS,
        in_specs=[pl.BlockSpec(memory_space=pltpu.SMEM), hbm, hbm],
        out_specs=[hbm] * KEY_HEADS,
        scratch_shapes=[
            VM((KEY_HEADS,) + shape, BF16),
            pltpu.SemaphoreType.DMA((2, KEY_HEADS, 2)),
        ],
        name="spread_heads",
        compiler_params=pltpu.CompilerParams(vmem_limit_bytes=12 << 20),
    )(meta, q, o)


def first_body(meta_ref, dq_ref, *rest):
    parts, out, stage, sems = rest[:KEY_HEADS], rest[KEY_HEADS], rest[-2], rest[-1]

    @pl.when(meta_ref[0] == 0)
    def _():
        loads, stores = [], []
        for h, part in enumerate(parts):
            cols = pl.ds(h * GROUP_SIZE * HEAD_SIZE, GROUP_SIZE * HEAD_SIZE)
            loads.append(pltpu.make_async_copy(part, stage.at[h], sems.at[0, h]))
            stores.append(pltpu.make_async_copy(stage.at[h], out.at[:, cols], sems.at[1, h]))
        for copy in loads:
            copy.start()
        for load, store in zip(loads, stores):
            load.wait()
            store.start()
        for copy in stores:
            copy.wait()


def put_first(meta, dq, parts):
    hbm = pl.BlockSpec(memory_space=pl.ANY)
    return pl.pallas_call(
        first_body,
        out_shape=jax.ShapeDtypeStruct(dq.shape, dq.dtype),
        in_specs=[pl.BlockSpec(memory_space=pltpu.SMEM)] + [hbm] * (KEY_HEADS + 1),
        out_specs=hbm,
        input_output_aliases={1: 0},
        scratch_shapes=[
            VM((KEY_HEADS, BLOCK, GROUP_SIZE * HEAD_SIZE), BF16),
            pltpu.SemaphoreType.DMA((2, KEY_HEADS)),
        ],
        name="put_first",
        compiler_params=pltpu.CompilerParams(vmem_limit_bytes=12 << 20),
    )(meta, dq, *parts)


def pick_body(meta_ref, *rest, at):
    parts, out_ref, sem = rest[:-2], rest[-2], rest[-1]
    for n, part in enumerate(parts):

        @pl.when(meta_ref[at] == n)
        def _():
            copy = pltpu.make_async_copy(part, out_ref, sem)
            copy.start()
            copy.wait()


def pick(meta, at, parts):
    return pl.pallas_call(
        functools.partial(pick_body, at=at),
        out_shape=jax.ShapeDtypeStruct(parts[0].shape, parts[0].dtype),
        in_specs=[pl.BlockSpec(memory_space=pltpu.SMEM)]
        + [pl.BlockSpec(memory_space=pl.ANY)] * len(parts),
        out_specs=pl.BlockSpec(memory_space=VM),
        scratch_shapes=[pltpu.SemaphoreType.DMA(())],
        name="pick",
        compiler_params=pltpu.CompilerParams(vmem_limit_bytes=12 << 20),
    )(meta, *parts)


def tp_pairs(pairs, ctx_size, tp_size):
    return [(c * tp_size + a, c * tp_size + b) for c in range(ctx_size) for a, b in pairs]


def add(*xs):
    return sum(x.astype(F32) for x in xs).astype(BF16)


def per_device(queries, key_tensor, value_tensor, output_gradient, key_blocks, slot_valid):
    tp_size, ctx_size = lax.axis_size("tp"), lax.axis_size("ctx")
    blocks = ctx_size * tp_size
    b_index = lax.axis_index("ctx") * tp_size + lax.axis_index("tp")
    core = lax.axis_index("ctx") % 2
    t_index = lax.axis_index("tp")
    meta = jnp.stack([b_index, core, t_index % 4, t_index // 4, lax.axis_index("ctx")])
    meta = meta.astype(jnp.int32)
    table = key_blocks.reshape(-1)
    valid = slot_valid.reshape(-1)
    up = [(i, i + 1) for i in range(1, blocks - 1)]
    down = [(i + 1, i) for i in range(1, blocks - 1)]
    partner = [(i, (i // tp_size ^ 1) * tp_size + i % tp_size) for i in range(blocks)]
    four = range(4)

    def swap(x):
        return lax.all_to_all(x, BOTH, split_axis=0, concat_axis=0, tiled=True)

    def send(x, pairs):
        return lax.ppermute(x, BOTH, pairs)

    def send_tp(x, pairs):
        return send(x, tp_pairs(pairs, ctx_size, tp_size))

    def along_x(n):
        return [(4 * z + x, 4 * z + (x + n) % 4) for z in four for x in four]

    def along_z(n):
        return [(4 * z + x, 4 * ((z + n) % 4) + x) for z in four for x in four]

    pieces, both = pack_pieces(key_tensor, value_tensor)
    held = swap(pieces.reshape(blocks, CHUNKS, PIECE, HEAD_SIZE))
    before, after = send(both, up), send(both, down)
    slices = spread_heads(meta, queries, output_gradient)
    moved = [slices[0]] * ctx_size
    for c in (4, 2, 6, 3, 5, 7, 1):
        moved[c] = send(slices[c // 2 + HALF * (c % 2)], [(0, c * tp_size)])

    listed = list(gather_pieces(table, meta, held, blocks, 0, False))
    more, given = gather_pieces(table, meta, held, blocks, 1, True)
    listed.append(more)
    given = send(given, partner)
    shape = (HALF, 2, GROUPS, SENT, PIECE, HEAD_SIZE)
    got = []
    for j in range(CHUNKS):
        got.append(swap(listed[j]).reshape(shape))

    qo = pick(meta, 4, moved)
    moved = [qo] + [send_tp(qo, [(0, n)]) for n in range(1, 4)]
    qo = pick(meta, 2, moved)
    moved = [qo] + [send_tp(qo, [(x, 4 * n + x) for x in four]) for n in range(1, 4)]

    grads, back = (), []
    calls = HALF // CALL_HEADS
    for j in range(CHUNKS):
        for n in range(calls):
            call = calls * j + n
            grads = sparse_grads(
                call, meta, valid, queries, output_gradient, both, before, after, got[j],
                grads if n > 0 else grads[:4],
            )
        back.append(swap(grads[4].reshape(blocks, SENT, PIECE, HEAD_SIZE)))
    dq, own, to_prev, to_next = grads[:4]
    from_next, from_prev = send(to_prev, down), send(to_next, up)

    stats, qo = dense_stats(meta, moved, held, given)
    others = [send_tp(stats, along_x(n)) for n in range(1, 4)]
    stats = merge_stats([stats] + others)
    others = [send_tp(stats, along_z(n)) for n in range(1, 4)]
    dense, to_partner, part = dense_grads(meta, qo, held, given, [stats] + others)
    dense_other = send(to_partner, partner)
    others = [send_tp(part, [(4 * n + x, x) for x in four]) for n in range(1, 4)]
    total = add(part, *others)
    others = [send_tp(total, [(n, 0)]) for n in range(1, 4)]
    total = add(total, *others)
    parts = [total] * KEY_HEADS
    for c in range(1, ctx_size):
        parts[c // 2 + HALF * (c % 2)] = send(total, [(c * tp_size, 0)])
    d_q = put_first(meta, dq, parts)

    first = scatter_pieces(table, back[0], blocks)
    summed = scatter_last(table, meta, back[1], first, dense, dense_other, blocks)
    home = swap(summed).reshape(HALF, 2, GROUPS, CHUNKS, PIECE, HEAD_SIZE)
    d_k, d_v = combine(own, from_prev, from_next, home)
    return d_q, d_k, d_v


def solution(mesh):
    spec = P(BOTH, None)

    return jax.shard_map(
        per_device,
        mesh=mesh,
        in_specs=(spec, spec, spec, spec, P(), P()),
        out_specs=(spec, spec, spec),
        check_vma=False,
    )
```

```python
import functools
import math

import jax
import jax.numpy as jnp
from jax import lax
from jax.experimental import pallas as pl
from jax.experimental.pallas import tpu as pltpu
from jax.sharding import PartitionSpec as P


KEY_HEADS = 8
GROUP_SIZE = 8
HEAD_SIZE = 128
BLOCK = 128
NB = 8
GROUPS = 16
PIECE = 8
SENT = 5
FIRST_SENT = NB - SENT
CHUNKS = 2
HALF = KEY_HEADS // CHUNKS
CALL_HEADS = 4
BOTH = ("ctx", "tp")
SCALING = 1.0 / math.sqrt(HEAD_SIZE)
EXP_SCALE = SCALING * math.log2(math.e)
FAR = 1e30
F32 = jnp.float32
BF16 = jnp.bfloat16
VM = pltpu.VMEM


def dot(a, b, ca, cb):
    return lax.dot_general(a, b, (((ca,), (cb,)), ((), ())), preferred_element_type=F32)


def pack_body(k_ref, v_ref, out_ref, both_ref):
    for kv, ref in enumerate((k_ref, v_ref)):
        both_ref[kv] = ref[...]
        for j in range(CHUNKS):
            for y in range(HALF):
                cols = pl.ds((j * HALF + y) * HEAD_SIZE, HEAD_SIZE)
                out_ref[y, kv, :, j] = ref[:, cols].reshape(GROUPS, PIECE, HEAD_SIZE)


def pack_pieces(k, v):
    return pl.pallas_call(
        pack_body,
        out_shape=(
            jax.ShapeDtypeStruct((HALF, 2, GROUPS, CHUNKS, PIECE, HEAD_SIZE), BF16),
            jax.ShapeDtypeStruct((2,) + k.shape, BF16),
        ),
        in_specs=[pl.BlockSpec(memory_space=VM)] * 2,
        out_specs=[pl.BlockSpec(memory_space=VM)] * 2,
        name="pack_pieces",
    )(k, v)


def gather_body(table_ref, meta_ref, held_ref, out_ref, *give_ref, rows, chunk):
    base = pl.program_id(0) * rows

    def one(d, carry):
        for s in range(SENT):
            block = table_ref[(base + d) * NB + FIRST_SENT + s]
            out_ref[d, s] = held_ref[block, chunk]
        return carry

    lax.fori_loop(0, rows, one, 0, unroll=8)
    if give_ref:

        @pl.when(pl.program_id(0) == 0)
        def _():
            give_ref[0][...] = held_ref[:, 1 - meta_ref[1]]


def gather_pieces(table, meta, held, blocks, chunk, give):
    steps = 2
    rows = blocks // steps
    shapes = [jax.ShapeDtypeStruct((blocks, SENT, PIECE, HEAD_SIZE), BF16)]
    specs = [pl.BlockSpec((rows, SENT, PIECE, HEAD_SIZE), lambda i, t, m: (i, 0, 0, 0))]
    if give:
        shapes.append(jax.ShapeDtypeStruct((blocks, PIECE, HEAD_SIZE), BF16))
        specs.append(pl.BlockSpec((blocks, PIECE, HEAD_SIZE), lambda i, t, m: (0, 0, 0)))
    return pl.pallas_call(
        functools.partial(gather_body, rows=rows, chunk=chunk),
        out_shape=shapes,
        grid_spec=pltpu.PrefetchScalarGridSpec(
            num_scalar_prefetch=2,
            grid=(steps,),
            in_specs=[pl.BlockSpec(memory_space=VM)],
            out_specs=specs,
        ),
        name="gather_pieces",
        compiler_params=pltpu.CompilerParams(vmem_limit_bytes=12 << 20),
    )(table, meta, held)


def add_listed(table_ref, got_ref, accs, blocks):
    for acc in accs:
        acc[...] = jnp.zeros_like(acc)

    def one(d, total):
        for s in range(1, SENT):
            block = table_ref[d * NB + FIRST_SENT + s]
            accs[s - 1][block] += got_ref[d, s].astype(F32)
        return total + got_ref[d, 0].astype(F32)

    zero = jnp.zeros((PIECE, HEAD_SIZE), F32)
    accs[0][0] += lax.fori_loop(0, blocks, one, zero, unroll=8)
    return (accs[0][...] + accs[1][...]) + (accs[2][...] + accs[3][...])


def scatter_body(table_ref, got_ref, out_ref, *accs, blocks):
    out_ref[...] = add_listed(table_ref, got_ref, accs, blocks)


def scatter_last_body(
    table_ref, meta_ref, got_ref, first_ref, dense_ref, other_ref, out_ref, *accs, blocks
):
    core = meta_ref[1]
    second = add_listed(table_ref, got_ref, accs, blocks)
    mine = dense_ref[...].reshape(second.shape)
    other = other_ref[...].astype(F32).reshape(second.shape)
    out_ref[:, core] = (jnp.where(core == 0, first_ref[...], second) + mine).astype(BF16)
    out_ref[:, 1 - core] = (jnp.where(core == 0, second, first_ref[...]) + other).astype(BF16)


def slot_sums(blocks):
    return [VM((blocks, PIECE, HEAD_SIZE), F32)] * (SENT - 1)


def scatter_pieces(table, got, blocks):
    return pl.pallas_call(
        functools.partial(scatter_body, blocks=blocks),
        out_shape=jax.ShapeDtypeStruct((blocks, PIECE, HEAD_SIZE), F32),
        in_specs=[pl.BlockSpec(memory_space=pltpu.SMEM), pl.BlockSpec(memory_space=VM)],
        out_specs=pl.BlockSpec(memory_space=VM),
        scratch_shapes=slot_sums(blocks),
        name="scatter_pieces",
        compiler_params=pltpu.CompilerParams(vmem_limit_bytes=12 << 20),
    )(table, got)


def scatter_last(table, meta, got, first, dense, other, blocks):
    return pl.pallas_call(
        functools.partial(scatter_last_body, blocks=blocks),
        out_shape=jax.ShapeDtypeStruct((blocks, CHUNKS, PIECE, HEAD_SIZE), BF16),
        in_specs=[pl.BlockSpec(memory_space=pltpu.SMEM)] * 2 + [pl.BlockSpec(memory_space=VM)] * 4,
        out_specs=pl.BlockSpec(memory_space=VM),
        scratch_shapes=slot_sums(blocks),
        name="scatter_last",
        compiler_params=pltpu.CompilerParams(vmem_limit_bytes=12 << 20),
    )(table, meta, got, first, dense, other)


def two_heads(ref, p):
    first = ref[:, pl.ds(2 * p * HEAD_SIZE, HEAD_SIZE)]
    second = ref[:, pl.ds((2 * p + 1) * HEAD_SIZE, HEAD_SIZE)]
    return jnp.concatenate([first, second], axis=0)


def col_sum(x):
    return jnp.sum(x, axis=0, keepdims=True)


def sparse_body(
    meta_ref, valid_ref, q_ref, o_ref, self_ref, before_ref, after_ref, g_ref, *rest
):
    dq_ref, own_ref, prev_ref, next_ref, sent_ref = rest[-14:-9]
    kc, vc, kt, st, dp, pb, ds, dk, dv = rest[-9:]
    b = meta_ref[0]

    @pl.when(b == 0)
    def _():
        dq_ref[...] = jnp.zeros_like(dq_ref)
        own_ref[...] = jnp.zeros_like(own_ref)
        prev_ref[...] = jnp.zeros_like(prev_ref)
        next_ref[...] = jnp.zeros_like(next_ref)
        sent_ref[...] = jnp.zeros_like(sent_ref)

    @pl.when(b != 0)
    def _():
        for kv, dst in ((0, kc), (1, vc)):
            for s, part in enumerate((before_ref, self_ref, after_ref)):
                dst[s * BLOCK : (s + 1) * BLOCK] = part[kv]
            for s in range(SENT):
                at = (FIRST_SENT + s) * BLOCK
                dst[at : at + BLOCK] = g_ref[0, kv, :, s].reshape(BLOCK, HEAD_SIZE)
        kt[...] = kc[...].T
        live = [valid_ref[b * NB + s] > 0 for s in range(NB)]

        def heads(ref, p):
            return two_heads(ref, p)

        def pair(p, w):
            qp = heads(q_ref, p)
            op = heads(o_ref, p)
            st[w] = dot(kc[...], qp, 1, 1)
            dp[w] = dot(vc[...], op, 1, 1)
            top = jnp.full((1, 2 * BLOCK), -FAR, F32)
            for s in range(NB):
                here = jnp.max(st[w, s * BLOCK : (s + 1) * BLOCK], axis=0, keepdims=True)
                top = jnp.maximum(top, jnp.where(live[s], here, -FAR))
            top = top * EXP_SCALE
            total = jnp.zeros((1, 2 * BLOCK), F32)
            cross = jnp.zeros((1, 2 * BLOCK), F32)
            for s in range(NB):
                rows = slice(s * BLOCK, (s + 1) * BLOCK)
                shift = jnp.where(live[s], top, FAR)
                raised = jnp.exp2(st[w, rows] * EXP_SCALE - shift)
                st[w, rows] = raised
                total = total + col_sum(raised)
                cross = cross + col_sum(raised * dp[w, rows])
            inverse = 1.0 / total
            delta = cross * inverse
            for s in range(NB):
                rows = slice(s * BLOCK, (s + 1) * BLOCK)
                weights = st[w, rows] * inverse
                pb[w, rows] = weights.astype(BF16)
                ds[w, rows] = (weights * (dp[w, rows] - delta)).astype(BF16)
            new_dv = dot(pb[w], op, 1, 0)
            new_dk = dot(ds[w], qp, 1, 0)
            dv[...] = new_dv if p == 0 else dv[...] + new_dv
            dk[...] = new_dk if p == 0 else dk[...] + new_dk
            dqt = dot(kt[...], ds[w], 1, 0) * SCALING
            out = jnp.concatenate([dqt[:, :BLOCK].T, dqt[:, BLOCK:].T], axis=1).astype(BF16)
            dq_ref[:, pl.ds(2 * p * HEAD_SIZE, 2 * HEAD_SIZE)] = out

        def two_pairs(i, carry):
            for w in range(2):
                pair(2 * i + w, w)
            return carry

        for i in range(GROUP_SIZE // 4):
            two_pairs(i, 0)
        for kv, acc, factor in ((0, dk, SCALING), (1, dv, 1.0)):
            prev_ref[kv] = (acc[0:BLOCK] * factor).astype(BF16)
            own_ref[kv] = acc[BLOCK : 2 * BLOCK] * factor
            next_ref[kv] = (acc[2 * BLOCK : 3 * BLOCK] * factor).astype(BF16)
            for s in range(SENT):
                at = (FIRST_SENT + s) * BLOCK
                sent_ref[0, kv, :, s] = (
                    (acc[at : at + BLOCK] * factor).astype(BF16).reshape(GROUPS, PIECE, HEAD_SIZE)
                )


def sparse_grads(call, meta, valid, q, o, own, before, after, got, earlier=()):
    first = call * CALL_HEADS
    inside = first % HALF

    wide = pl.BlockSpec((BLOCK, GROUP_SIZE * HEAD_SIZE), lambda h, m, t: (0, first + h))
    pair = pl.BlockSpec((2, BLOCK, HEAD_SIZE), lambda h, m, t: (0, 0, first + h))
    pieces = pl.BlockSpec(
        (1, 2, GROUPS, SENT, PIECE, HEAD_SIZE), lambda h, m, t: (inside + h, 0, 0, 0, 0, 0)
    )
    keys = NB * BLOCK
    width = KEY_HEADS * HEAD_SIZE
    return pl.pallas_call(
        sparse_body,
        out_shape=(
            jax.ShapeDtypeStruct(q.shape, BF16),
            jax.ShapeDtypeStruct((2, BLOCK, width), F32),
            jax.ShapeDtypeStruct((2, BLOCK, width), BF16),
            jax.ShapeDtypeStruct((2, BLOCK, width), BF16),
            jax.ShapeDtypeStruct((HALF, 2, GROUPS, SENT, PIECE, HEAD_SIZE), BF16),
        ),
        grid_spec=pltpu.PrefetchScalarGridSpec(
            num_scalar_prefetch=2,
            grid=(CALL_HEADS,),
            in_specs=[wide, wide, pair, pair, pair, pieces]
            + [pl.BlockSpec(memory_space=pl.ANY)] * len(earlier),
            out_specs=[wide, pair, pair, pair, pieces],
            scratch_shapes=[
                VM((keys, HEAD_SIZE), BF16),
                VM((keys, HEAD_SIZE), BF16),
                VM((HEAD_SIZE, keys), BF16),
                VM((2, keys, 2 * BLOCK), F32),
                VM((2, keys, 2 * BLOCK), F32),
                VM((2, keys, 2 * BLOCK), BF16),
                VM((2, keys, 2 * BLOCK), BF16),
                VM((keys, HEAD_SIZE), F32),
                VM((keys, HEAD_SIZE), F32),
            ],
        ),
        input_output_aliases={8 + n: n for n in range(len(earlier))},
        name="sparse_grads",
    )(meta, valid, q, o, own, before, after, got, *earlier)


def load_held(meta_ref, held_ref, other_ref, kc, vc):
    core = meta_ref[1]
    mine = held_ref[:, core].reshape(kc.shape)
    other = other_ref[...].reshape(kc.shape)

    @pl.when(core == 0)
    def _():
        kc[...] = mine
        vc[...] = other

    @pl.when(core != 0)
    def _():
        kc[...] = other
        vc[...] = mine


def stats_body(
    meta_ref, p0, p1, p2, p3, held_ref, other_ref, out_ref, q_ref, kc, vc, sem
):
    parts = (p0, p1, p2, p3)
    for n, part in enumerate(parts):

        @pl.when(meta_ref[3] == n)
        def _():
            copy = pltpu.make_async_copy(part, q_ref, sem)
            copy.start()
            copy.wait()

    load_held(meta_ref, held_ref, other_ref, kc, vc)
    for p in range(GROUP_SIZE // 2):
        scores = dot(kc[...], two_heads(q_ref.at[0], p), 1, 1)
        grads = dot(vc[...], two_heads(q_ref.at[1], p), 1, 1)
        top = jnp.max(scores, axis=0, keepdims=True) * EXP_SCALE
        raised = jnp.exp2(scores * EXP_SCALE - top)
        for n, row in enumerate((top, col_sum(raised), col_sum(raised * grads))):
            for j in range(2):
                at = n * GROUP_SIZE + 2 * p + j
                out_ref[at : at + 1] = row[:, j * BLOCK : (j + 1) * BLOCK]


def dense_stats(meta, parts, held, other):
    keys = held.shape[0] * PIECE
    return pl.pallas_call(
        stats_body,
        out_shape=(
            jax.ShapeDtypeStruct((3 * GROUP_SIZE, BLOCK), F32),
            jax.ShapeDtypeStruct(parts[0].shape, BF16),
        ),
        in_specs=[pl.BlockSpec(memory_space=pltpu.SMEM)]
        + [pl.BlockSpec(memory_space=pl.ANY)] * 4
        + [pl.BlockSpec(memory_space=VM)] * 2,
        out_specs=[pl.BlockSpec(memory_space=VM)] * 2,
        scratch_shapes=[
            VM((keys, HEAD_SIZE), BF16),
            VM((keys, HEAD_SIZE), BF16),
            pltpu.SemaphoreType.DMA(()),
        ],
        name="dense_stats",
        compiler_params=pltpu.CompilerParams(vmem_limit_bytes=20 << 20),
    )(meta, *parts, held, other)


def merge_stats(parts):
    n = GROUP_SIZE
    top = functools.reduce(jnp.maximum, [x[:n] for x in parts])
    factors = [jnp.exp2(x[:n] - top) for x in parts]
    total = sum(x[n : 2 * n] * f for x, f in zip(parts, factors))
    cross = sum(x[2 * n :] * f for x, f in zip(parts, factors))
    return jnp.concatenate([top, total, cross], axis=0)


def dense_body(
    meta_ref, q_ref, held_ref, other_ref, s0, s1, s2, s3, keep_ref, give_ref, dq_ref,
    kc, vc, kt, stats, dkv_ref,
):
    load_held(meta_ref, held_ref, other_ref, kc, vc)
    kt[...] = kc[...].T
    stats[...] = merge_stats([s0[...], s1[...], s2[...], s3[...]])
    core = meta_ref[1]

    def row(n, p):
        at = n * GROUP_SIZE + 2 * p
        return jnp.concatenate([stats[at : at + 1], stats[at + 1 : at + 2]], axis=1)

    for p in range(GROUP_SIZE // 2):
        top = row(0, p)
        inverse = 1.0 / row(1, p)
        delta = row(2, p) * inverse
        qp = two_heads(q_ref.at[0], p)
        op = two_heads(q_ref.at[1], p)
        scores = dot(kc[...], qp, 1, 1)
        grads = dot(vc[...], op, 1, 1)
        weights = jnp.exp2(scores * EXP_SCALE - top) * inverse
        rounded = weights.astype(BF16)
        score_grad = (weights * (grads - delta)).astype(BF16)
        new_dk = dot(score_grad, qp, 1, 0) * SCALING
        new_dv = dot(rounded, op, 1, 0)
        dkv_ref[core] = new_dk if p == 0 else dkv_ref[core] + new_dk
        dkv_ref[1 - core] = new_dv if p == 0 else dkv_ref[1 - core] + new_dv
        dqt = dot(kt[...], score_grad, 1, 0) * SCALING
        for j in range(2):
            dq_ref[:, pl.ds((2 * p + j) * HEAD_SIZE, HEAD_SIZE)] = (
                dqt[:, j * BLOCK : (j + 1) * BLOCK].T.astype(BF16)
            )
    keep_ref[...] = dkv_ref[0]
    give_ref[...] = dkv_ref[1].astype(BF16)


def dense_grads(meta, qo, held, other, stats):
    keys = held.shape[0] * PIECE
    return pl.pallas_call(
        dense_body,
        out_shape=(
            jax.ShapeDtypeStruct((keys, HEAD_SIZE), F32),
            jax.ShapeDtypeStruct((keys, HEAD_SIZE), BF16),
            jax.ShapeDtypeStruct((BLOCK, GROUP_SIZE * HEAD_SIZE), BF16),
        ),
        in_specs=[pl.BlockSpec(memory_space=pltpu.SMEM)] + [pl.BlockSpec(memory_space=VM)] * 7,
        out_specs=[pl.BlockSpec(memory_space=VM)] * 3,
        scratch_shapes=[
            VM((keys, HEAD_SIZE), BF16),
            VM((keys, HEAD_SIZE), BF16),
            VM((HEAD_SIZE, keys), BF16),
            VM((3 * GROUP_SIZE, BLOCK), F32),
            VM((2, keys, HEAD_SIZE), F32),
        ],
        name="dense_grads",
        compiler_params=pltpu.CompilerParams(vmem_limit_bytes=24 << 20),
    )(meta, qo, held, other, *stats)


def combine_body(own_ref, prev_ref, next_ref, got_ref, dk_ref, dv_ref):
    for kv, out in ((0, dk_ref), (1, dv_ref)):
        for h in range(KEY_HEADS):
            cols = pl.ds(h * HEAD_SIZE, HEAD_SIZE)
            total = own_ref[kv, :, cols] + prev_ref[kv, :, cols].astype(F32)
            total = total + next_ref[kv, :, cols].astype(F32)
            pieces = got_ref[h % HALF, kv, :, h // HALF].reshape(BLOCK, HEAD_SIZE)
            out[:, cols] = (total + pieces.astype(F32)).astype(BF16)


def combine(own, from_prev, from_next, got):
    width = KEY_HEADS * HEAD_SIZE
    return pl.pallas_call(
        combine_body,
        out_shape=(jax.ShapeDtypeStruct((BLOCK, width), BF16),) * 2,
        in_specs=[pl.BlockSpec(memory_space=VM)] * 4,
        out_specs=[pl.BlockSpec(memory_space=VM)] * 2,
        name="combine",
        compiler_params=pltpu.CompilerParams(vmem_limit_bytes=12 << 20),
    )(own, from_prev, from_next, got)


def spread_body(meta_ref, q_ref, o_ref, *rest):
    outs, stage, sems = rest[:-2], rest[-2], rest[-1]

    @pl.when(meta_ref[0] == 0)
    def _():
        loads, stores = [], []
        for h, out in enumerate(outs):
            cols = pl.ds(h * GROUP_SIZE * HEAD_SIZE, GROUP_SIZE * HEAD_SIZE)
            for j, ref in enumerate((q_ref, o_ref)):
                loads.append(
                    pltpu.make_async_copy(ref.at[:, cols], stage.at[h, j], sems.at[0, h, j])
                )
                stores.append(pltpu.make_async_copy(stage.at[h, j], out.at[j], sems.at[1, h, j]))
        for copy in loads:
            copy.start()
        for load, store in zip(loads, stores):
            load.wait()
            store.start()
        for copy in stores:
            copy.wait()


def spread_heads(meta, q, o):
    hbm = pl.BlockSpec(memory_space=pl.ANY)
    shape = (2, BLOCK, GROUP_SIZE * HEAD_SIZE)
    return pl.pallas_call(
        spread_body,
        out_shape=(jax.ShapeDtypeStruct(shape, BF16),) * KEY_HEADS,
        in_specs=[pl.BlockSpec(memory_space=pltpu.SMEM), hbm, hbm],
        out_specs=[hbm] * KEY_HEADS,
        scratch_shapes=[
            VM((KEY_HEADS,) + shape, BF16),
            pltpu.SemaphoreType.DMA((2, KEY_HEADS, 2)),
        ],
        name="spread_heads",
    )(meta, q, o)


def first_body(meta_ref, dq_ref, *rest):
    parts, out, stage, sems = rest[:KEY_HEADS], rest[KEY_HEADS], rest[-2], rest[-1]

    @pl.when(meta_ref[0] == 0)
    def _():
        loads, stores = [], []
        for h, part in enumerate(parts):
            cols = pl.ds(h * GROUP_SIZE * HEAD_SIZE, GROUP_SIZE * HEAD_SIZE)
            loads.append(pltpu.make_async_copy(part, stage.at[h], sems.at[0, h]))
            stores.append(pltpu.make_async_copy(stage.at[h], out.at[:, cols], sems.at[1, h]))
        for copy in loads:
            copy.start()
        for load, store in zip(loads, stores):
            load.wait()
            store.start()
        for copy in stores:
            copy.wait()


def put_first(meta, dq, parts):
    hbm = pl.BlockSpec(memory_space=pl.ANY)
    return pl.pallas_call(
        first_body,
        out_shape=jax.ShapeDtypeStruct(dq.shape, dq.dtype),
        in_specs=[pl.BlockSpec(memory_space=pltpu.SMEM)] + [hbm] * (KEY_HEADS + 1),
        out_specs=hbm,
        input_output_aliases={1: 0},
        scratch_shapes=[
            VM((KEY_HEADS, BLOCK, GROUP_SIZE * HEAD_SIZE), BF16),
            pltpu.SemaphoreType.DMA((2, KEY_HEADS)),
        ],
        name="put_first",
    )(meta, dq, *parts)


def pick_body(meta_ref, *rest, at):
    parts, out_ref, sem = rest[:-2], rest[-2], rest[-1]
    for n, part in enumerate(parts):

        @pl.when(meta_ref[at] == n)
        def _():
            copy = pltpu.make_async_copy(part, out_ref, sem)
            copy.start()
            copy.wait()


def pick(meta, at, parts):
    return pl.pallas_call(
        functools.partial(pick_body, at=at),
        out_shape=jax.ShapeDtypeStruct(parts[0].shape, parts[0].dtype),
        in_specs=[pl.BlockSpec(memory_space=pltpu.SMEM)]
        + [pl.BlockSpec(memory_space=pl.ANY)] * len(parts),
        out_specs=pl.BlockSpec(memory_space=VM),
        scratch_shapes=[pltpu.SemaphoreType.DMA(())],
        name="pick",
    )(meta, *parts)


def tp_pairs(pairs, ctx_size, tp_size):
    return [(c * tp_size + a, c * tp_size + b) for c in range(ctx_size) for a, b in pairs]


def add(*xs):
    return sum(x.astype(F32) for x in xs).astype(BF16)


def per_device(queries, key_tensor, value_tensor, output_gradient, key_blocks, slot_valid):
    tp_size, ctx_size = lax.axis_size("tp"), lax.axis_size("ctx")
    blocks = ctx_size * tp_size
    b_index = lax.axis_index("ctx") * tp_size + lax.axis_index("tp")
    core = lax.axis_index("ctx") % 2
    t_index = lax.axis_index("tp")
    meta = jnp.stack([b_index, core, t_index % 4, t_index // 4, lax.axis_index("ctx")])
    meta = meta.astype(jnp.int32)
    table = key_blocks.reshape(-1)
    valid = slot_valid.reshape(-1)
    up = [(i, i + 1) for i in range(1, blocks - 1)]
    down = [(i + 1, i) for i in range(1, blocks - 1)]
    partner = [(i, (i // tp_size ^ 1) * tp_size + i % tp_size) for i in range(blocks)]
    four = range(4)

    def swap(x):
        return lax.all_to_all(x, BOTH, split_axis=0, concat_axis=0, tiled=True)

    def send(x, pairs):
        return lax.ppermute(x, BOTH, pairs)

    def send_tp(x, pairs):
        return send(x, tp_pairs(pairs, ctx_size, tp_size))

    def along_x(n):
        return [(4 * z + x, 4 * z + (x + n) % 4) for z in four for x in four]

    def along_z(n):
        return [(4 * z + x, 4 * ((z + n) % 4) + x) for z in four for x in four]

    pieces, both = pack_pieces(key_tensor, value_tensor)
    held = swap(pieces.reshape(blocks, CHUNKS, PIECE, HEAD_SIZE))
    before, after = send(both, up), send(both, down)
    slices = spread_heads(meta, queries, output_gradient)
    moved = [slices[0]] * ctx_size
    for c in (4, 2, 6, 3, 5, 7, 1):
        moved[c] = send(slices[c // 2 + HALF * (c % 2)], [(0, c * tp_size)])

    listed = list(gather_pieces(table, meta, held, blocks, 0, False))
    more, given = gather_pieces(table, meta, held, blocks, 1, True)
    listed.append(more)
    given = send(given, partner)
    shape = (HALF, 2, GROUPS, SENT, PIECE, HEAD_SIZE)
    got = []
    for j in range(CHUNKS):
        got.append(swap(listed[j]).reshape(shape))

    qo = pick(meta, 4, moved)
    moved = [qo] + [send_tp(qo, [(0, n)]) for n in range(1, 4)]
    qo = pick(meta, 2, moved)
    moved = [qo] + [send_tp(qo, [(x, 4 * n + x) for x in four]) for n in range(1, 4)]

    grads, back = (), []
    calls = HALF // CALL_HEADS
    for j in range(CHUNKS):
        for n in range(calls):
            call = calls * j + n
            grads = sparse_grads(
                call, meta, valid, queries, output_gradient, both, before, after, got[j],
                grads if n > 0 else grads[:4],
            )
        back.append(swap(grads[4].reshape(blocks, SENT, PIECE, HEAD_SIZE)))
    dq, own, to_prev, to_next = grads[:4]
    from_next, from_prev = send(to_prev, down), send(to_next, up)

    stats, qo = dense_stats(meta, moved, held, given)
    others = [send_tp(stats, along_x(n)) for n in range(1, 4)]
    stats = merge_stats([stats] + others)
    others = [send_tp(stats, along_z(n)) for n in range(1, 4)]
    dense, to_partner, part = dense_grads(meta, qo, held, given, [stats] + others)
    dense_other = send(to_partner, partner)
    others = [send_tp(part, [(4 * n + x, x) for x in four]) for n in range(1, 4)]
    total = add(part, *others)
    others = [send_tp(total, [(n, 0)]) for n in range(1, 4)]
    total = add(total, *others)
    parts = [total] * KEY_HEADS
    for c in (4, 5, 2, 3, 6, 7, 1):
        parts[c // 2 + HALF * (c % 2)] = send(total, [(c * tp_size, 0)])
    d_q = put_first(meta, dq, parts)

    first = scatter_pieces(table, back[0], blocks)
    summed = scatter_last(table, meta, back[1], first, dense, dense_other, blocks)
    home = swap(summed).reshape(HALF, 2, GROUPS, CHUNKS, PIECE, HEAD_SIZE)
    d_k, d_v = combine(own, from_prev, from_next, home)
    return d_q, d_k, d_v


def solution(mesh):
    spec = P(BOTH, None)

    return jax.shard_map(
        per_device,
        mesh=mesh,
        in_specs=(spec, spec, spec, spec, P(), P()),
        out_specs=(spec, spec, spec),
        check_vma=False,
    )
```
